32 devices in a mesh: query: 8 (over z, y), cand: 4 (over x, core).
Axes of the slice: x: 2, y: 2, z: 4, core: 2. Of those that a mesh axis runs over, the one named last changes fastest.
Arguments:
- tokens: bfloat16 [2, 8, 4, 512, 768], P(None, 'query', 'cand'), may hold values from -6 to 6
- cotangent: bfloat16 [2, 8, 4, 512, 768], P(None, 'query', 'cand'), may hold values from -6 to 6
- lengths: int32 [2, 8, 4, 2], P(None, 'query'), may hold values from 0 to 512, as said below
- relevance: float32 [2, 8, 4, 2], P(None, 'query'), may hold values from -8 to 8
- rel_table: int32 [1023], replicated, may hold values from 0 to 255
- w_query: bfloat16 [768, 768], P('query'), may hold values from -0.21875 to 0.21875
- w_key: bfloat16 [768, 768], P('query'), may hold values from -0.21875 to 0.21875
- w_value: bfloat16 [768, 768], P('query'), may hold values from -0.21875 to 0.21875
- w_output: bfloat16 [768, 768], P('query'), may hold values from -3.5 to 3.5
- w_inner: bfloat16 [768, 3072], P('query'), may hold values from -0.21875 to 0.21875
- w_outer: bfloat16 [3072, 768], P('query'), may hold values from -0.109375 to 0.109375
- bias_query: bfloat16 [768], P('query'), may hold values from -3 to 3
- bias_value: bfloat16 [768], P('query'), may hold values from -3 to 3
- bias_attn: bfloat16 [768], P('query'), may hold values from -3 to 3
- bias_inner: bfloat16 [3072], P('query'), may hold values from -3 to 3
- bias_outer: bfloat16 [768], P('query'), may hold values from -3 to 3
- gain_attn: bfloat16 [768], P('query'), may hold values from 0.099609375 to 1.8984375
- shift_attn: bfloat16 [768], P('query'), may hold values from -3 to 3
- gain_ffn: bfloat16 [768], P('query'), may hold values from 0.099609375 to 1.8984375
- shift_ffn: bfloat16 [768], P('query'), may hold values from -3 to 3
- rel_bias: bfloat16 [256, 12], P('query'), may hold values from -5 to 5
- w_score: bfloat16 [768], P('query'), may hold values from -0.3125 to 0.3125
Outputs:
- hidden: bfloat16 [2, 8, 4, 512, 768], P(None, 'query', 'cand')
- query_loss: float32 [2, 8], P(None, 'query')
- grad_tokens: float32 [2, 8, 4, 512, 768], P(None, 'query', 'cand')
- grad_w_query: float32 [768, 768], P(('query', 'cand'))
- grad_w_key: float32 [768, 768], P(('query', 'cand'))
- grad_w_value: float32 [768, 768], P(('query', 'cand'))
- grad_w_output: float32 [768, 768], P(('query', 'cand'))
- grad_w_inner: float32 [768, 3072], P(('query', 'cand'))
- grad_w_outer: float32 [3072, 768], P(('query', 'cand'))
- grad_bias_query: float32 [768], P(('query', 'cand'))
- grad_bias_value: float32 [768], P(('query', 'cand'))
- grad_bias_attn: float32 [768], P(('query', 'cand'))
- grad_bias_inner: float32 [3072], P(('query', 'cand'))
- grad_bias_outer: float32 [768], P(('query', 'cand'))
- grad_gain_attn: float32 [768], P(('query', 'cand'))
- grad_shift_attn: float32 [768], P(('query', 'cand'))
- grad_gain_ffn: float32 [768], P(('query', 'cand'))
- grad_shift_ffn: float32 [768], P(('query', 'cand'))
- grad_rel_bias: float32 [256, 12], P(('query', 'cand'))
- grad_w_score: float32 [768], P(('query', 'cand'))
The draws below stay inside these ranges and needn't reach their ends.
Inputs may be any that keep to these rules, and one draw needn't show every extreme that they name: `lengths`: A slot holds one sequence of 256 to 512 tokens (second length 0) or two of 128 to 256 tokens each; some slot holds one of exactly 512 tokens and some two of exactly 256.
All inputs are finite; a program needn't handle non-finite values.
Results may differ from the reference program's by a relative error of at most 0.017.
Values may be sent and summed in bfloat16 or wider, within the bound.
No kernel may reach another device: no remote copies, remote signals or barrier semaphores. Data moves between devices by JAX's collectives and lax.ppermute only.
A program may use at most 192 MiB of HBM per device.

```python
import jax
import jax.numpy as jnp
from jax import lax

D = 768
H = 12
HD = 64
FF = 3072
NB = 256
SHORT = 256
LONG = 512
MB = 2
QUERIES = 8
SLOTS = 4


def length_pair(key):
    k_pair, k_long, k_short = jax.random.split(key, 3)
    dims_all = (MB, QUERIES, SLOTS)
    pair_slot = jax.random.randint(k_pair, dims_all, 0, 2)
    long_len = jax.random.randint(k_long, dims_all, LONG // 2, LONG + 1)
    short_len = jax.random.randint(k_short, dims_all + (2,), SHORT // 2, SHORT + 1)
    pair_slot = pair_slot.at[0, 0, 0].set(0).at[0, 0, 1].set(1)
    long_len = long_len.at[0, 0, 0].set(LONG)
    short_len = short_len.at[0, 0, 1].set(SHORT)
    first_len = jnp.where(pair_slot == 1, short_len[..., 0], long_len)
    second = jnp.where(pair_slot == 1, short_len[..., 1], 0)
    return jnp.stack([first_len, second], axis=-1).astype(jnp.int32)


def draw_lengths(key, part):
    return length_pair(jax.random.fold_in(key, 11))


def plant(array, stream_key, least, largest):
    longest = array.shape.index(max(array.shape))
    spots = []
    for shift in (0, 1):
        where = [jax.random.randint(jax.random.fold_in(stream_key, axis), (), 0, length) for axis, length in enumerate(array.shape)]
        where[longest] = (where[longest] + shift) % array.shape[longest]
        spots.append(tuple(where))
    return array.at[spots[0]].set(least).at[spots[1]].set(largest)


def block_scale(stream_key, shape, cuts, smallest, largest):
    gain, own = 1.0, jax.random.fold_in(stream_key, 6)
    for axis_at, blocks in cuts:
        steps = jnp.exp(jax.random.uniform(jax.random.fold_in(own, axis_at), (blocks,), jnp.float32, smallest / len(cuts), largest / len(cuts)))
        gain = gain * jnp.repeat(steps, shape[axis_at] // blocks).reshape([-1 if axis == axis_at else 1 for axis in range(len(shape))])
    return gain


def scatter_about(own_key, dims, deviation, most, cuts=(), kind=jnp.bfloat16):
    loudness = block_scale(own_key, dims, cuts, -0.22, 0.18) if cuts else 1.0
    drawn = jax.random.normal(own_key, dims, jnp.float32) * deviation * loudness
    return jnp.minimum(jnp.maximum(drawn, -most), most).astype(kind)


def setup_inputs(seed: int = 0) -> dict:
    streams_of = jax.random.split(jax.random.key(seed), 23)
    tokens = scatter_about(streams_of[0], (MB, QUERIES, SLOTS, LONG, D), 1.0, 6.0, ((1, 8), (2, 4)))
    cotangent = scatter_about(streams_of[1], (MB, QUERIES, SLOTS, LONG, D), 1.0, 6.0, ((1, 8), (2, 4)))
    lengths = draw_lengths(jax.random.fold_in(streams_of[22], 71), 0)
    relevance = scatter_about(streams_of[3], (MB, QUERIES, SLOTS, 2), 2.0, 8.0, ((1, 8),), jnp.float32)
    rel_table = plant(jax.random.randint(streams_of[4], (2 * LONG - 1,), 0, NB), jax.random.fold_in(streams_of[4], 1), 0, NB - 1).astype(jnp.int32)
    w_query = scatter_about(streams_of[5], (D, D), D ** -0.5, 0.21875, ((0, 8),))
    w_key = scatter_about(streams_of[6], (D, D), D ** -0.5, 0.21875, ((0, 8),))
    w_value = scatter_about(streams_of[7], (D, D), D ** -0.5, 0.21875, ((0, 8),))
    w_output = scatter_about(streams_of[8], (D, D), (2 * D // LONG) ** -0.5, 3.5, ((0, 8),))
    w_inner = scatter_about(streams_of[9], (D, FF), D ** -0.5, 0.21875, ((0, 8),))
    w_outer = scatter_about(streams_of[10], (FF, D), FF ** -0.5, 0.109375, ((0, 8),))
    bias_query = scatter_about(streams_of[11], (D,), 0.5, 3.0, ((0, 8),))
    bias_value = scatter_about(streams_of[12], (D,), 0.5, 3.0, ((0, 8),))
    bias_attn = scatter_about(streams_of[13], (D,), 0.5, 3.0, ((0, 8),))
    bias_inner = scatter_about(streams_of[14], (FF,), 0.5, 3.0, ((0, 8),))
    bias_outer = scatter_about(streams_of[15], (D,), 0.5, 3.0, ((0, 8),))
    gain_attn = jnp.clip(1.0 + 0.18 * jax.random.normal(streams_of[16], (D,), jnp.float32), 0.099609375, 1.8984375).astype(jnp.bfloat16)
    shift_attn = scatter_about(streams_of[17], (D,), 0.5, 3.0, ((0, 8),))
    gain_ffn = jnp.clip(1.0 + 0.18 * jax.random.normal(streams_of[18], (D,), jnp.float32), 0.099609375, 1.8984375).astype(jnp.bfloat16)
    shift_ffn = scatter_about(streams_of[19], (D,), 0.5, 3.0, ((0, 8),))
    rel_bias = scatter_about(streams_of[20], (NB, H), 1.0, 5.0, ((0, 8),))
    w_score = scatter_about(streams_of[21], (D,), (D // 2) ** -0.5, 0.3125, ((0, 8),))
    return {"tokens": tokens, "cotangent": cotangent, "lengths": lengths, "relevance": relevance, "rel_table": rel_table, "w_query": w_query, "w_key": w_key, "w_value": w_value, "w_output": w_output, "w_inner": w_inner, "w_outer": w_outer, "bias_query": bias_query, "bias_value": bias_value, "bias_attn": bias_attn, "bias_inner": bias_inner, "bias_outer": bias_outer, "gain_attn": gain_attn, "shift_attn": shift_attn, "gain_ffn": gain_ffn, "shift_ffn": shift_ffn, "rel_bias": rel_bias, "w_score": w_score}


HIGHEST = lax.Precision.HIGHEST

@jax.custom_vjp
def low(v):
    return lax.optimization_barrier(v.astype(jnp.bfloat16)).astype(jnp.float32)

@jax.custom_vjp
def low_back(v):
    return v

def low_keep(v):
    return (low(v), None)

def low_pass(kept, grad):
    return (grad,)

def back_keep(v):
    return (v, None)

def back_low(kept, grad):
    return (low(grad),)
low.defvjp(low_keep, low_pass)
low_back.defvjp(back_keep, back_low)

def matmul_hi(left_mat, right_mat):
    return jnp.dot(left_mat, right_mat, precision=HIGHEST)

def layer_norm(values, gain_vec, shift_vec):
    row_mean = lax.optimization_barrier(jnp.mean(values, axis=-1, keepdims=True))
    centred = values - row_mean
    row_var = lax.optimization_barrier(jnp.mean(centred * centred, axis=-1, keepdims=True))
    return centred * lax.rsqrt(row_var + 1e-05) * gain_vec + shift_vec

def slot_forward(params, inputs, seq_lens, rel_table):
    w_query, w_key, w_value, w_output, w_inner, w_outer, bias_query, bias_value, bias_attn, bias_inner, bias_outer, gain_attn, shift_attn, gain_ffn, shift_ffn, rel_bias, w_score = params
    length = inputs.shape[0]
    middle = length // 2
    queries = low(low_back(matmul_hi(inputs, w_query) + bias_query)).reshape(length, H, HD)
    keys_r = low(low_back(matmul_hi(inputs, w_key))).reshape(length, H, HD)
    values_r = low(low_back(matmul_hi(inputs, w_value) + bias_value)).reshape(length, H, HD)
    places = jnp.arange(length, dtype=jnp.int32)
    second = seq_lens[1] > 0
    segment = jnp.where(second & (places >= middle), 1, 0).astype(jnp.int32)
    seg_len = jnp.where(segment == 1, seq_lens[1], seq_lens[0])
    key_live = places - segment * middle < seg_len
    allowed = (segment[:, None] == segment[None, :]) & key_live[None, :]
    distance_bias = rel_bias[rel_table]
    rel_index = places[None, :] - places[:, None] + (length - 1)
    bias_full = jnp.transpose(distance_bias[rel_index], (2, 0, 1))
    raw_scores = low_back(jnp.einsum('ihd,jhd->hij', queries, keys_r, precision=HIGHEST))
    logits = jnp.where(allowed[None], raw_scores * HD ** (-0.5) + bias_full, -1000000000.0)
    row_peak = lax.optimization_barrier(jnp.max(logits, axis=-1, keepdims=True))
    row_exp = jnp.exp(logits - row_peak)
    weights_attn = low(row_exp / lax.optimization_barrier(jnp.sum(row_exp, axis=-1, keepdims=True)))
    context = jnp.einsum('hij,jhd->ihd', weights_attn, values_r, precision=HIGHEST).reshape(length, H * HD)
    context = low(low_back(context))
    attn_out = low_back(matmul_hi(context, w_output) + bias_attn)
    hidden_one = layer_norm(inputs + attn_out, gain_attn, shift_attn)
    inner_pre = low_back(matmul_hi(low(hidden_one), w_inner) + bias_inner)
    activated = low(jax.nn.gelu(inner_pre, approximate=False))
    outer_out = low_back(matmul_hi(activated, w_outer) + bias_outer)
    hidden = low(layer_norm(hidden_one + outer_out, gain_ffn, shift_ffn))
    cls_rows = jnp.stack([hidden[0], hidden[middle]])
    return (hidden, matmul_hi(cls_rows, w_score))

def group_fn(params, group_in, lens_group, rel_group, rel_table):
    slot_ck = jax.checkpoint(slot_forward)
    hidden, scores = lax.map(lambda packed: slot_ck(params, packed[0], packed[1], rel_table), (group_in, lens_group))
    present = jnp.stack([lens_group[:, 0] > 0, lens_group[:, 1] > 0], axis=-1)
    masked = jnp.where(present, scores, -1000000000.0)
    score_peak = jnp.max(masked)
    log_total = score_peak + jnp.log(jnp.sum(jnp.exp(masked - score_peak)))
    log_prob = masked - log_total
    rel_masked = jnp.where(present, rel_group, -1000000000.0)
    rel_peak = jnp.max(rel_masked)
    rel_exp = jnp.exp(rel_masked - rel_peak)
    target = rel_exp / jnp.sum(rel_exp)
    query_loss = -jnp.sum(jnp.where(present, target * log_prob, 0.0))
    return (hidden, query_loss)

def reference(tokens, cotangent, lengths, relevance, rel_table, w_query, w_key, w_value, w_output, w_inner, w_outer, bias_query, bias_value, bias_attn, bias_inner, bias_outer, gain_attn, shift_attn, gain_ffn, shift_ffn, rel_bias, w_score):
    params = tuple((item.astype(jnp.float32) for item in (w_query, w_key, w_value, w_output, w_inner, w_outer, bias_query, bias_value, bias_attn, bias_inner, bias_outer, gain_attn, shift_attn, gain_ffn, shift_ffn, rel_bias, w_score)))
    groups = MB * QUERIES
    groups_in = tokens.astype(jnp.float32).reshape(groups, SLOTS, LONG, D)
    lens_r = lengths.reshape(groups, SLOTS, 2)
    rel_r = relevance.reshape(groups, SLOTS, 2)
    group_ck = jax.checkpoint(group_fn)

    def forward(group_data, param_set):
        return lax.map(lambda packed: group_ck(param_set, packed[0], packed[1], packed[2], rel_table), (group_data, lens_r, rel_r))
    (hidden, losses), pullback = jax.vjp(forward, groups_in, params)
    cot_r = cotangent.astype(jnp.float32).reshape(groups, SLOTS, LONG, D)
    grad_tokens, grad_params = pullback((cot_r, jnp.ones_like(losses)))
    return (hidden.reshape(tokens.shape).astype(jnp.bfloat16), losses.reshape(MB, QUERIES), grad_tokens.reshape(tokens.shape), grad_params[0], grad_params[1], grad_params[2], grad_params[3], grad_params[4], grad_params[5], grad_params[6], grad_params[7], grad_params[8], grad_params[9], grad_params[10], grad_params[11], grad_params[12], grad_params[13], grad_params[14], grad_params[15], grad_params[16])
```

```python
from functools import partial

import jax
import jax.numpy as jnp
import numpy as np
from jax import lax
from jax.experimental import pallas as pl
from jax.experimental.pallas import tpu as pltpu
from jax.sharding import PartitionSpec as P

HD = 64
PAIR = 2 * HD
TRIO = 3 * PAIR
TILE = 128
BF = jnp.bfloat16
F32 = jnp.float32
NEG = -1000000000.0
EPS = 1e-05

ERFC_P = 0.3
ERFC_C = (
    0.16919777981386785,
    0.17054619772689322,
    0.14956727662616615,
    0.21002273459109255,
    -0.08286335340540726,
    0.5302129644860679,
    -0.49655482906135956,
    0.4777385344298923,
    -0.12786727948795917,
)

VECTORS = (
    "bias_query",
    "bias_value",
    "bias_attn",
    "bias_outer",
    "gain_attn",
    "shift_attn",
    "gain_ffn",
    "shift_ffn",
    "w_score",
)
TABLE_ROWS = 16
ROW = {name: index for index, name in enumerate(VECTORS)}


def cost(micros=0.001):
    return pl.CostEstimate(flops=int(micros * 1.15e9), bytes_accessed=0, transcendentals=0)


def contract(left_mat, right_mat, left_dim, right_dim):
    return lax.dot_general(
        left_mat,
        right_mat,
        (((left_dim,), (right_dim,)), ((), ())),
        preferred_element_type=F32,
    )


def gelu_pair(u):
    size = jnp.abs(u)
    t = 1.0 / (1.0 + (ERFC_P * 0.5**0.5) * size)
    poly = jnp.full_like(u, 0.5 * ERFC_C[-1])
    for coef in ERFC_C[-2::-1]:
        poly = poly * t + 0.5 * coef
    bell = jnp.exp(-0.5 * (u * u))
    tail = poly * t * bell
    cdf = jnp.where(u < 0, tail, 1.0 - tail)
    return u * cdf, cdf + u * ((2.0 * np.pi) ** -0.5 * bell)


def normalise(values):
    centred = values - jnp.mean(values, axis=-1, keepdims=True)
    inv_std = lax.rsqrt(jnp.mean(centred * centred, axis=-1, keepdims=True) + EPS)
    return centred * inv_std, inv_std


def norm_backward(grad_out, normed, inv_std, gain_vec):
    grad_normed = grad_out * gain_vec
    return inv_std * (
        grad_normed
        - jnp.mean(grad_normed, axis=-1, keepdims=True)
        - normed * jnp.mean(grad_normed * normed, axis=-1, keepdims=True)
    )


def row_chunks(rows, size, step):
    size = min(size, rows)

    @pl.loop(0, rows // size)
    def _(index):
        step(pl.ds(pl.multiple_of(index * size, size), size))


def split_rows(core, tile, rows, keep, send):
    for block in range(tile.shape[0] // (2 * rows)):
        place = slice(block * rows, (block + 1) * rows)
        if rows % 8 == 0:
            own = pl.multiple_of((2 * block + core) * rows, 8)
            other = pl.multiple_of((2 * block + 1 - core) * rows, 8)
            keep[place, :] = tile[pl.ds(own, rows), :]
            send[place, :] = tile[pl.ds(other, rows), :]
        else:
            even = tile[2 * block * rows : (2 * block + 1) * rows, :]
            odd = tile[(2 * block + 1) * rows : (2 * block + 2) * rows, :]
            keep[place, :] = jnp.where(core == 0, even, odd)
            send[place, :] = jnp.where(core == 0, odd, even)


def attn_fwd_kernel(x_ref, w_ref, b_ref, dist_ref, mask_ref, *refs):
    qkv_ref, ctx_ref, p_ref, table = refs[-4:]
    length = x_ref.shape[0]
    width = 2 * length

    @pl.when(pl.program_id(1) == 0)
    def _():
        for head in range(2):
            row = jnp.broadcast_to(dist_ref[0, head : head + 1, :], (TILE, width))
            table[head] = pltpu.roll(row, 0, 1, stride=1, stride_axis=0)

    qkv = (contract(x_ref[...], w_ref[...], 1, 0) + b_ref[...]).astype(BF)
    qkv_ref[...] = qkv
    q = qkv[:, :PAIR] * jnp.asarray(HD**-0.5, BF)
    k = qkv[:, PAIR : 2 * PAIR]
    v = qkv[:, 2 * PAIR :]
    lane = lax.broadcasted_iota(jnp.int32, (length, PAIR), 1)
    outs = []
    for head in range(2):
        own = (lane < HD) == (head == 0)
        raw = contract(jnp.where(own, q, jnp.zeros_like(q)), k, 1, 1)
        for start in range(0, length, TILE):
            half = start // (length // 2)
            logits = (
                raw[start : start + TILE]
                + table[head, :, length - start : width - start]
                + mask_ref[0, half : half + 1, :]
            )
            peak = jnp.max(logits, axis=1, keepdims=True)
            grown = jnp.exp(logits - peak)
            total = jnp.sum(grown, axis=1, keepdims=True)
            p_ref[0, head, start : start + TILE, :] = (grown * (1.0 / total)).astype(BF)
        outs.append(contract(p_ref[0, head], v, 1, 0))
    ctx_ref[...] = jnp.where(lane < HD, outs[0], outs[1]).astype(BF)


def attn_fwd(inputs, weight, bias, dist, mask, first, held):
    rows, width = inputs.shape
    micros = mask.shape[0]
    length = rows // micros
    pairs = weight.shape[1] // TRIO
    every = bias.shape[1] // TRIO
    return pl.pallas_call(
        attn_fwd_kernel,
        grid=(pairs, micros),
        in_specs=[
            pl.BlockSpec((length, width), lambda h, m: (m, 0)),
            pl.BlockSpec((width, TRIO), lambda h, m: (0, h)),
            pl.BlockSpec((1, TRIO), lambda h, m: (0, h + first)),
            pl.BlockSpec((1, 8, 2 * length), lambda h, m: (h + first, 0, 0)),
            pl.BlockSpec((1, 8, length), lambda h, m: (m, 0, 0)),
        ]
        + [pl.BlockSpec(memory_space=pl.ANY)] * len(held),
        out_specs=[
            pl.BlockSpec((length, TRIO), lambda h, m: (m, h + first)),
            pl.BlockSpec((length, PAIR), lambda h, m: (m, h + first)),
            pl.BlockSpec((1, 2, length, length), lambda h, m: (m, h + first, 0, 0)),
        ],
        out_shape=[
            jax.ShapeDtypeStruct((rows, every * TRIO), BF),
            jax.ShapeDtypeStruct((rows, every * PAIR), BF),
            jax.ShapeDtypeStruct((micros, 2 * every, length, length), BF),
        ],
        input_output_aliases={5 + index: index for index in range(len(held))},
        scratch_shapes=[pltpu.VMEM((2, TILE, 2 * length), F32)],
        compiler_params=pltpu.CompilerParams(vmem_limit_bytes=40 << 20),
        cost_estimate=cost(),
        name="attn_fwd",
    )(inputs, weight, bias, dist, mask, *held)


def attn_bwd_kernel(
    block_rows, place_ref, qkv_ref, o_ref, dr_ref, p_ref, wo_ref, x_ref, *refs
):
    dqkv_ref, gd_ref, db_ref, keep_ref, send_ref, acc, dsb, dw, kept, sent = refs[-10:]
    length = qkv_ref.shape[0]
    width = 2 * length
    first = pl.program_id(1) == 0
    last = pl.program_id(1) == pl.num_programs(1) - 1

    @pl.when(first)
    def _():
        acc[...] = jnp.zeros_like(acc)
        dw[...] = jnp.zeros_like(dw)
        db_ref[...] = jnp.zeros_like(db_ref)

    q = qkv_ref[:, :PAIR]
    k = qkv_ref[:, PAIR : 2 * PAIR]
    v = qkv_ref[:, 2 * PAIR :]
    do = contract(dr_ref[...], wo_ref[...], 1, 1).astype(BF)
    lane = lax.broadcasted_iota(jnp.int32, (length, PAIR), 1)
    prod = do.astype(F32) * o_ref[...].astype(F32)
    dq, dk, dv = [], [], []
    for head in range(2):
        own = (lane < HD) == (head == 0)
        inner = jnp.sum(jnp.where(own, prod, 0.0), axis=1, keepdims=True)
        dp = contract(jnp.where(own, do, jnp.zeros_like(do)), v, 1, 1)
        for start in range(0, length, TILE):
            rows = slice(start, start + TILE)
            ds = p_ref[0, head, rows, :].astype(F32) * (dp[rows] - inner[rows])
            acc[head, :, length - start : width - start] += ds
            dsb[head, rows, :] = (ds * HD**-0.5).astype(BF)
        dq.append(contract(dsb[head], k, 1, 0))
        dk.append(contract(dsb[head], q, 0, 0))
        dv.append(contract(p_ref[0, head], do, 0, 0))
    for index, (low, high) in enumerate((dq, dk, dv)):
        cols = slice(index * PAIR, (index + 1) * PAIR)
        grad = jnp.where(lane < HD, low, high).astype(BF)
        dqkv_ref[:, cols] = grad
        db_ref[0, 0:1, cols] += jnp.sum(grad.astype(F32), axis=0, keepdims=True)
    dw[...] += contract(x_ref[...], dqkv_ref[...], 0, 0)

    @pl.when(last)
    def _():
        split_rows(place_ref[0], dw, block_rows, kept, sent)
        keep_ref[...] = kept[...].astype(BF)
        send_ref[...] = sent[...].astype(BF)
        for head in range(2):
            total = acc[head, 0:8, :]
            for start in range(8, TILE, 8):
                total = total + pltpu.roll(acc[head, start : start + 8, :], width - start, 1)
            row = total[0:1, :]
            for step in range(1, 8):
                row = row + pltpu.roll(total[step : step + 1, :], width - step, 1)
            gd_ref[0, head : head + 1, :] = row


def attn_bwd(
    place, block_rows, qkv, ctx, d_r, probs, w_output, inputs, first, pairs, held=(), start=0, every=None
):
    rows, width = inputs.shape
    micros, _, length, _ = probs.shape
    at = lambda shape, place: pl.BlockSpec(shape, lambda h, m, c: place(h, m))
    half = width // 2
    every = every or pairs
    return pl.pallas_call(
        partial(attn_bwd_kernel, block_rows),
        grid_spec=pltpu.PrefetchScalarGridSpec(
            num_scalar_prefetch=1,
            grid=(pairs, micros),
            in_specs=[
                at((length, TRIO), lambda h, m: (m, h + first)),
                at((length, PAIR), lambda h, m: (m, h + first)),
                at((length, width), lambda h, m: (m, 0)),
                at((1, 2, length, length), lambda h, m: (m, h + first, 0, 0)),
                at((PAIR, width), lambda h, m: (h + first, 0)),
                at((length, width), lambda h, m: (m, 0)),
            ]
            + [pl.BlockSpec(memory_space=pl.ANY)] * len(held),
            out_specs=[
                at((length, TRIO), lambda h, m: (m, h + start)),
                at((1, 8, 2 * length), lambda h, m: (h + start, 0, 0)),
                at((1, 8, TRIO), lambda h, m: (h + start, 0, 0)),
                at((half, TRIO), lambda h, m: (0, h + start)),
                at((half, TRIO), lambda h, m: (0, h + start)),
            ],
            scratch_shapes=[
                pltpu.VMEM((2, TILE, 2 * length), F32),
                pltpu.VMEM((2, length, length), BF),
                pltpu.VMEM((width, TRIO), F32),
                pltpu.VMEM((half, TRIO), F32),
                pltpu.VMEM((half, TRIO), F32),
            ],
        ),
        out_shape=[
            jax.ShapeDtypeStruct((rows, every * TRIO), BF),
            jax.ShapeDtypeStruct((every, 8, 2 * length), F32),
            jax.ShapeDtypeStruct((every, 8, TRIO), F32),
            jax.ShapeDtypeStruct((half, every * TRIO), BF),
            jax.ShapeDtypeStruct((half, every * TRIO), BF),
        ],
        input_output_aliases={7 + index: index for index in range(len(held))},
        compiler_params=pltpu.CompilerParams(vmem_limit_bytes=44 << 20),
        cost_estimate=cost(),
        name="attn_bwd",
    )(place, qkv, ctx, d_r, probs, w_output, inputs, *held)


def vec(ref, name):
    return ref[ROW[name] : ROW[name] + 1, :]


def ffn_in_kernel(
    x_ref, ctx_ref, wo_ref, vec_ref, w_ref, b_ref, n1_ref, i1_ref, low_ref, act_ref, slope_ref
):
    rows = x_ref.shape[0]

    @pl.when(pl.program_id(0) == 0)
    def _():
        size = min(256, rows)
        for start in range(0, rows, size):
            at = slice(start, start + size)
            attn = contract(ctx_ref[at, :], wo_ref[...], 1, 0) + vec(vec_ref, "bias_attn")
            normed, inv_std = normalise(x_ref[at, :].astype(F32) + attn)
            n1_ref[at, :] = normed
            i1_ref[at, :] = inv_std
            first = normed * vec(vec_ref, "gain_attn") + vec(vec_ref, "shift_attn")
            low_ref[at, :] = first.astype(BF)

    low = low_ref[...]
    wide = w_ref.shape[1]
    size = min(256, wide)
    for start in range(0, wide, size):
        cols = slice(start, start + size)
        u = contract(low, w_ref[:, cols], 1, 0) + b_ref[:, cols]
        act, slope = gelu_pair(u)
        act_ref[:, cols] = act.astype(BF)
        slope_ref[:, cols] = slope.astype(BF)


def ffn_in(inputs, context, w_output, vectors, w_inner, bias):
    rows, width = inputs.shape
    hidden = w_inner.shape[1]
    size = min(512, hidden)
    whole = pl.BlockSpec((rows, width), lambda n: (0, 0))
    column = pl.BlockSpec((rows, 1), lambda n: (0, 0))
    cols = pl.BlockSpec((rows, size), lambda n: (0, n))
    out = jax.ShapeDtypeStruct((rows, hidden), BF)
    return pl.pallas_call(
        ffn_in_kernel,
        grid=(hidden // size,),
        in_specs=[
            whole,
            whole,
            pl.BlockSpec((width, width), lambda n: (0, 0)),
            pl.BlockSpec((TABLE_ROWS, width), lambda n: (0, 0)),
            pl.BlockSpec((width, size), lambda n: (0, n)),
            pl.BlockSpec((1, size), lambda n: (0, n)),
        ],
        out_specs=[whole, column, whole, cols, cols],
        out_shape=[
            jax.ShapeDtypeStruct((rows, width), F32),
            jax.ShapeDtypeStruct((rows, 1), F32),
            jax.ShapeDtypeStruct((rows, width), BF),
            out,
            out,
        ],
        compiler_params=pltpu.CompilerParams(vmem_limit_bytes=44 << 20),
        cost_estimate=cost(),
        name="ffn_in",
    )(inputs, context, w_output, vectors, w_inner, bias)


def ffn_out_kernel(act_ref, w_ref, n1_ref, vec_ref, n2_ref, i2_ref, hid_ref, score_ref):
    first = n1_ref[...] * vec(vec_ref, "gain_attn") + vec(vec_ref, "shift_attn")
    outer = contract(act_ref[...], w_ref[...], 1, 0) + vec(vec_ref, "bias_outer")
    normed, inv_std = normalise(first + outer)
    n2_ref[...] = normed
    i2_ref[...] = inv_std
    low = (normed * vec(vec_ref, "gain_ffn") + vec(vec_ref, "shift_ffn")).astype(BF)
    hid_ref[...] = low
    row = low[0:8, :].astype(F32)[0:1, :] * vec(vec_ref, "w_score")
    score_ref[0] = jnp.broadcast_to(jnp.sum(row, axis=1, keepdims=True), score_ref.shape[1:])


def ffn_out(act, w_outer, normed, vectors, count):
    rows, hidden = act.shape
    width = w_outer.shape[1]
    size = rows // count
    block = pl.BlockSpec((size, width), lambda r: (r, 0))
    return pl.pallas_call(
        ffn_out_kernel,
        grid=(count,),
        in_specs=[
            pl.BlockSpec((size, hidden), lambda r: (r, 0)),
            pl.BlockSpec((hidden, width), lambda r: (0, 0)),
            block,
            pl.BlockSpec((TABLE_ROWS, width), lambda r: (0, 0)),
        ],
        out_specs=[
            block,
            pl.BlockSpec((size, 1), lambda r: (r, 0)),
            block,
            pl.BlockSpec((1, 8, 128), lambda r: (r, 0, 0)),
        ],
        out_shape=[
            jax.ShapeDtypeStruct((rows, width), F32),
            jax.ShapeDtypeStruct((rows, 1), F32),
            jax.ShapeDtypeStruct((rows, width), BF),
            jax.ShapeDtypeStruct((count, 8, 128), F32),
        ],
        compiler_params=pltpu.CompilerParams(vmem_limit_bytes=40 << 20),
        cost_estimate=cost(),
        name="ffn_out",
    )(act, w_outer, normed, vectors)


def list_loss(scores, lens, relevance):
    present = lens > 0
    masked = jnp.where(present, scores, NEG)
    peak = jnp.max(masked, axis=1, keepdims=True)
    log_total = peak + jnp.log(jnp.sum(jnp.exp(masked - peak), axis=1, keepdims=True))
    log_prob = masked - log_total
    rel = jnp.where(present, relevance, NEG)
    rel_exp = jnp.exp(rel - jnp.max(rel, axis=1, keepdims=True))
    target = rel_exp / jnp.sum(rel_exp, axis=1, keepdims=True)
    loss = -jnp.sum(jnp.where(present, target * log_prob, 0.0), axis=1, keepdims=True)
    return loss, jnp.where(present, jnp.exp(log_prob) - target, 0.0)


def outer_bwd_kernel(
    block_rows, place_ref, score_ref, len_ref, rel_ref, cot_ref, n2_ref, i2_ref, hid_ref, vec_ref,
    act_ref, dr_ref, low, sum_ref, loss_ref, keep_ref, send_ref, tile, kept, sent,
):
    rows, width = cot_ref.shape

    @pl.when(pl.program_id(0) == 0)
    def _():
        loss, grad = list_loss(score_ref[...], len_ref[...], rel_ref[...])
        loss_ref[...] = jnp.broadcast_to(loss, loss_ref.shape)
        lane = lax.broadcasted_iota(jnp.int32, grad.shape, 1)
        micros = grad.shape[0]
        sum_ref[...] = jnp.zeros_like(sum_ref)
        firsts = {}
        for half in range(2):
            own = jnp.where(lane == 2 * place_ref[1] + half, grad, 0.0)
            own = jnp.sum(own, axis=1, keepdims=True)
            for micro in range(micros):
                firsts[(2 * micro + half) * (rows // (2 * micros))] = own[micro : micro + 1, :]
        score_row = vec(vec_ref, "w_score")
        gain = vec(vec_ref, "gain_ffn")

        def step(at):
            grad_out = cot_ref[at, :].astype(F32)
            place = lax.broadcasted_iota(jnp.int32, (grad_out.shape[0], 1), 0) + at.start
            shift = jnp.zeros_like(place, F32)
            for first, value in firsts.items():
                shift = jnp.where(place == first, value, shift)
            grad_out = grad_out + shift * score_row
            normed = n2_ref[at, :]
            grad_in = norm_backward(grad_out, normed, i2_ref[at, :], gain)
            dr_ref[at, :] = grad_in
            grad_low = grad_in.astype(BF)
            low[at, :] = grad_low
            sum_ref[0:1, :] += jnp.sum(grad_out * normed, axis=0, keepdims=True)
            sum_ref[1:2, :] += jnp.sum(grad_out, axis=0, keepdims=True)
            sum_ref[2:3, :] += jnp.sum(grad_low.astype(F32), axis=0, keepdims=True)

        row_chunks(rows, 128, step)
        total = jnp.zeros((1, width), F32)
        for first, value in firsts.items():
            total = total + value * hid_ref[first : first + 8, :].astype(F32)[0:1, :]
        sum_ref[3:4, :] = total

    tile[...] = contract(act_ref[...], low[...], 0, 0)
    split_rows(place_ref[0], tile, block_rows, kept, sent)
    keep_ref[...] = kept[...].astype(BF)
    send_ref[...] = sent[...].astype(BF)


def outer_bwd(
    place, block_rows, scores, lens, relevance, cot, normed, inv_std, hid, vectors, act
):
    rows, width = cot.shape
    hidden = act.shape[1]
    size = width
    at = lambda shape, index: pl.BlockSpec(shape, lambda n, c: index(n))
    whole = at((rows, width), lambda n: (0, 0))
    tiny = at(scores.shape, lambda n: (0, 0))
    half = at((size // 2, width), lambda n: (n, 0))
    return pl.pallas_call(
        partial(outer_bwd_kernel, block_rows),
        grid_spec=pltpu.PrefetchScalarGridSpec(
            num_scalar_prefetch=1,
            grid=(hidden // size,),
            in_specs=[
                tiny, tiny, tiny, whole, whole, at((rows, 1), lambda n: (0, 0)), whole,
                at((TABLE_ROWS, width), lambda n: (0, 0)), at((rows, size), lambda n: (0, n)),
            ],
            out_specs=[
                whole, whole, at((8, width), lambda n: (0, 0)),
                at((scores.shape[0], 128), lambda n: (0, 0)), half, half,
            ],
            scratch_shapes=[
                pltpu.VMEM((size, width), F32),
                pltpu.VMEM((size // 2, width), F32),
                pltpu.VMEM((size // 2, width), F32),
            ],
        ),
        out_shape=[
            jax.ShapeDtypeStruct((rows, width), F32),
            jax.ShapeDtypeStruct((rows, width), BF),
            jax.ShapeDtypeStruct((8, width), F32),
            jax.ShapeDtypeStruct((scores.shape[0], 128), F32),
            jax.ShapeDtypeStruct((hidden // 2, width), BF),
            jax.ShapeDtypeStruct((hidden // 2, width), BF),
        ],
        compiler_params=pltpu.CompilerParams(vmem_limit_bytes=56 << 20),
        cost_estimate=cost(),
        name="outer_bwd",
    )(place, scores, lens, relevance, cot, normed, inv_std, hid, vectors, act)


def act_bwd_kernel(dr_ref, slope_ref, w2_ref, din_ref, db_ref):
    grad = dr_ref[...]
    wide = w2_ref.shape[0]
    size = min(256, wide)
    for start in range(0, wide, size):
        cols = slice(start, start + size)
        d_act = contract(grad, w2_ref[cols, :], 1, 1)
        d_in = (d_act * slope_ref[:, cols].astype(F32)).astype(BF)
        din_ref[:, cols] = d_in
        db_ref[:, cols] = jnp.sum(d_in.astype(F32), axis=0, keepdims=True)


def act_bwd(grad, slope, w_outer):
    rows, hidden = slope.shape
    width = grad.shape[1]
    size = min(512, hidden)
    cols = pl.BlockSpec((rows, size), lambda n: (0, n))
    return pl.pallas_call(
        act_bwd_kernel,
        grid=(hidden // size,),
        in_specs=[
            pl.BlockSpec((rows, width), lambda n: (0, 0)),
            cols,
            pl.BlockSpec((size, width), lambda n: (n, 0)),
        ],
        out_specs=[cols, pl.BlockSpec((1, size), lambda n: (0, n))],
        out_shape=[
            jax.ShapeDtypeStruct((rows, hidden), BF),
            jax.ShapeDtypeStruct((1, hidden), F32),
        ],
        compiler_params=pltpu.CompilerParams(vmem_limit_bytes=44 << 20),
        cost_estimate=cost(),
        name="act_bwd",
    )(grad, slope, w_outer)


def inner_bwd_kernel(
    block_rows, place_ref, din_ref, w1_ref, low_ref, dr_ref, n1_ref, i1_ref, vec_ref, ctx_ref,
    one_ref, grad_ref, sum_ref, keep_ref, send_ref, acc, tile, kept, sent,
):
    step_id = pl.program_id(0)
    last = pl.num_programs(0) - 1
    rows = low_ref.shape[0]

    @pl.when(step_id < last)
    def _():
        d_in = din_ref[...]
        tile[...] = contract(low_ref[...], d_in, 0, 0)
        part = contract(d_in, w1_ref[...], 1, 1)

        @pl.when(step_id == 0)
        def _():
            acc[...] = dr_ref[...] + part

        @pl.when(step_id > 0)
        def _():
            acc[...] += part

    @pl.when(step_id == last)
    def _():
        sum_ref[...] = jnp.zeros_like(sum_ref)
        gain = vec(vec_ref, "gain_attn")

        def step(at):
            grad_out = acc[at, :]
            normed = n1_ref[at, :]
            grad_in = norm_backward(grad_out, normed, i1_ref[at, :], gain)
            one_ref[at, :] = grad_in
            grad_low = grad_in.astype(BF)
            grad_ref[at, :] = grad_low
            sum_ref[0:1, :] += jnp.sum(grad_out * normed, axis=0, keepdims=True)
            sum_ref[1:2, :] += jnp.sum(grad_out, axis=0, keepdims=True)
            sum_ref[2:3, :] += jnp.sum(grad_low.astype(F32), axis=0, keepdims=True)

        row_chunks(rows, 128, step)
        tile[...] = contract(ctx_ref[...], grad_ref[...], 0, 0)

    split_rows(place_ref[0], tile, block_rows, kept, sent)
    keep_ref[...] = kept[...].astype(BF)
    send_ref[...] = sent[...].astype(BF)


def inner_bwd(place, block_rows, d_in, w_inner, low, d_r, normed, inv_std, vectors, context):
    rows, width = low.shape
    hidden = d_in.shape[1]
    size = width
    tiles = hidden // size
    at = lambda shape, index: pl.BlockSpec(shape, lambda n, c: index(n))
    whole = at((rows, width), lambda n: (0, 0))
    near = lambda n: (0, jnp.minimum(n, tiles - 1))
    half = at((width // 2, size), lambda n: (0, n))
    return pl.pallas_call(
        partial(inner_bwd_kernel, block_rows),
        grid_spec=pltpu.PrefetchScalarGridSpec(
            num_scalar_prefetch=1,
            grid=(tiles + 1,),
            in_specs=[
                at((rows, size), near), at((width, size), near), whole, whole, whole,
                at((rows, 1), lambda n: (0, 0)), at((TABLE_ROWS, width), lambda n: (0, 0)), whole,
            ],
            out_specs=[whole, whole, at((8, width), lambda n: (0, 0)), half, half],
            scratch_shapes=[
                pltpu.VMEM((rows, width), F32),
                pltpu.VMEM((width, size), F32),
                pltpu.VMEM((width // 2, size), F32),
                pltpu.VMEM((width // 2, size), F32),
            ],
        ),
        out_shape=[
            jax.ShapeDtypeStruct((rows, width), F32),
            jax.ShapeDtypeStruct((rows, width), BF),
            jax.ShapeDtypeStruct((8, width), F32),
            jax.ShapeDtypeStruct((width // 2, hidden + width), BF),
            jax.ShapeDtypeStruct((width // 2, hidden + width), BF),
        ],
        compiler_params=pltpu.CompilerParams(vmem_limit_bytes=56 << 20),
        cost_estimate=cost(),
        name="inner_bwd",
    )(place, d_in, w_inner, low, d_r, normed, inv_std, vectors, context)


def shifted(axis_size, group, stride, step):
    pairs = []
    for source in range(axis_size):
        place = source // stride % group
        pairs.append((source, source + ((place + step) % group - place) * stride))
    return pairs


class Grid:
    def __init__(self, query_size, cand_size):
        query, cand = lax.axis_index("query"), lax.axis_index("cand")
        self.sizes = {"outer": query_size // 2, "inner": 2, "far": cand_size // 2, "core": 2}
        self.lengths = {"query": query_size, "cand": cand_size}
        self.axes = {
            "outer": ("query", 2),
            "inner": ("query", 1),
            "far": ("cand", 2),
            "core": ("cand", 1),
        }
        self.at = {
            "outer": query // 2,
            "inner": query % 2,
            "far": cand // 2,
            "core": cand % 2,
        }

    def move(self, value, dim, step):
        axis, stride = self.axes[dim]
        return lax.ppermute(
            value, axis, shifted(self.lengths[axis], self.sizes[dim], stride, step)
        )


def pack_kernel(pairs, place_ref, wq, wk, wv, wo, w2, table, first, middle, outer):
    core, far = place_ref[0], place_ref[1]
    half = wq.shape[0] // 2
    rows = pl.ds(pl.multiple_of(core * half, 16), half)
    for pair in range(pairs):
        for index, weight in enumerate((wq, wk, wv)):
            to = (pair * 3 + index) * PAIR
            first[:half, to : to + PAIR] = weight[rows, pair * PAIR : (pair + 1) * PAIR]
    first[half:, :] = table[...]
    count = wq.shape[1] // PAIR // pairs - 1
    for run in range(count):
        cols = pl.ds(pl.multiple_of(((run + 1) * pairs + far) * PAIR, PAIR), PAIR)
        for index, weight in enumerate((wq, wk, wv)):
            middle[run * half : (run + 1) * half, index * PAIR : (index + 1) * PAIR] = weight[rows, cols]
    wide = wo.shape[1] // 2
    cols = pl.ds(pl.multiple_of(far * wide, PAIR), wide)
    middle[count * half :, :] = wo[rows, cols]
    tall = w2.shape[0] // 2
    outer[...] = w2[pl.ds(pl.multiple_of(core * tall, 16), tall), cols]


def pack(place, pairs, wq, wk, wv, wo, w2, table):
    shard, width = wq.shape
    half = shard // 2
    count = width // PAIR // pairs
    shapes = [
        (half + TABLE_ROWS, pairs * TRIO),
        (count * half, width // 2),
        (w2.shape[0] // 2, width // 2),
    ]
    return pl.pallas_call(
        partial(pack_kernel, pairs),
        grid_spec=pltpu.PrefetchScalarGridSpec(
            num_scalar_prefetch=1,
            grid=(1,),
            in_specs=[
                pl.BlockSpec(value.shape, lambda i, c: (0, 0)) for value in (wq, wk, wv, wo, w2, table)
            ],
            out_specs=[pl.BlockSpec(shape, lambda i, c: (0, 0)) for shape in shapes],
        ),
        out_shape=[jax.ShapeDtypeStruct(shape, BF) for shape in shapes],
        compiler_params=pltpu.CompilerParams(vmem_limit_bytes=60 << 20),
        cost_estimate=cost(),
        name="pack",
    )(place, wq, wk, wv, wo, w2, table)


class Gather:
    def __init__(self, grid, blocks, places=None):
        self.grid = grid
        self.pieces = [blocks]
        self.places = [places or [dict(grid.at)]]
        self.received = []

    def start(self, dim, joined=True):
        grid, size = self.grid, self.grid.sizes[dim]
        if joined and len(self.pieces) > 1:
            self.pieces = [jnp.concatenate(self.pieces)]
            self.places = [sum(self.places, [])]
        self.coming = []
        for piece, places in zip(self.pieces, self.places):
            for step in range(1, size):
                self.received.append(grid.move(piece, dim, step))
                self.coming.append(
                    [{**place, dim: (place[dim] - step) % size} for place in places]
                )

    def fold(self):
        self.pieces = self.pieces + self.received
        self.places = self.places + self.coming
        self.received = []

    def part(self, first, rows):
        gather = Gather(self.grid, None)
        gather.pieces = [
            jnp.concatenate([piece[:, first : first + rows] for piece in self.pieces])
        ]
        gather.places = [sum(self.places, [])]
        return gather


def place_kernel(splits, order_ref, *refs):
    count = 1 + max(run[0] for split in splits for run in split)
    sources, targets, sems = refs[: -1 - count], refs[-1 - count : -1], refs[-1]
    copies = []
    at = 0
    for source, split in zip(sources, splits):
        wide = source.shape[-1]
        for index in range(source.shape[0]):
            first = 0
            for target, rows, stride, offset in split:
                row = pl.multiple_of(order_ref[0, at] * rows, 16)
                cols = slice(None)
                if stride:
                    col = order_ref[1, at] * (stride * wide) + offset * wide
                    cols = pl.ds(pl.multiple_of(col, 128), wide)
                copies.append(
                    pltpu.make_async_copy(
                        source.at[index, pl.ds(first, rows), :],
                        targets[target].at[pl.ds(row, rows), cols],
                        sems.at[len(copies)],
                    )
                )
                first += rows
            at += 1
    for copy in copies:
        copy.start()
    for copy in copies:
        copy.wait()


def place_blocks(shapes, *gathers):
    places, pieces, splits, copies = [], [], [], 0
    for gather, split in gathers:
        for piece, found in zip(gather.pieces, gather.places):
            pieces.append(piece)
            splits.append(split)
            places += found
            copies += len(found) * len(split)
    row = [(place["outer"] * 2 + place["inner"]) * 2 + place["core"] for place in places]
    col = [place["far"] for place in places]
    order = jnp.stack([jnp.stack(row), jnp.stack(col)]).astype(jnp.int32)
    return pl.pallas_call(
        partial(place_kernel, splits),
        grid_spec=pltpu.PrefetchScalarGridSpec(
            num_scalar_prefetch=1,
            grid=(1,),
            in_specs=[pl.BlockSpec(memory_space=pl.ANY)] * len(pieces),
            out_specs=[pl.BlockSpec(memory_space=pltpu.VMEM)] * len(shapes),
            scratch_shapes=[pltpu.SemaphoreType.DMA((copies,))],
        ),
        out_shape=[jax.ShapeDtypeStruct(shape, BF) for shape in shapes],
        compiler_params=pltpu.CompilerParams(vmem_limit_bytes=24 << 20),
        cost_estimate=cost(),
        name="place_blocks",
    )(order, *pieces)


class Scatter:
    def __init__(self, grid, keep, send, order, rider=None):
        self.grid = grid
        self.dims = ["outer", "inner", "far"]
        self.order = list(order)
        self.sizes = [grid.sizes[dim] for dim in self.dims]
        self.rider = rider
        self.parts = [self.blocks(keep)]
        self.shapes = [self.blocks(send).shape]
        self.received = [grid.move(self.load(send), "core", 1)]

    def blocks(self, value):
        return value.reshape(*self.sizes, -1, value.shape[-1])

    def load(self, value):
        if self.rider is None:
            return value
        value = value.reshape(-1, value.shape[-1])
        return jnp.concatenate([value, self.rider.astype(BF)])

    def start(self):
        dim = self.order.pop(0)
        axis = self.dims.index(dim)
        size, here = self.grid.sizes[dim], self.grid.at[dim]
        sent = []
        for step in range(1, size):
            total = 0.0
            for part in self.parts:
                piece = lax.dynamic_index_in_dim(part, (here + step) % size, axis, keepdims=False)
                total += piece.astype(F32)
            sent.append(total.astype(BF))
        self.shapes = [value.shape for value in sent]
        self.received = [
            self.grid.move(self.load(value), dim, step) for step, value in enumerate(sent, 1)
        ]
        self.parts = [
            lax.dynamic_index_in_dim(part, here, axis, keepdims=False) for part in self.parts
        ]
        self.dims.remove(dim)

    def fold(self):
        for value, shape in zip(self.received, self.shapes):
            if self.rider is not None:
                count = value.shape[0] - self.rider.shape[0]
                self.rider = self.rider + value[count:].astype(F32)
                value = value[:count]
            self.parts.append(value.reshape(shape))
        self.received = []

    def result(self):
        while self.order:
            self.start()
            self.fold()
        return sum(part.astype(F32) for part in self.parts)


def after(values, *steps):
    moved = [piece for step in steps for piece in step.received]
    count = len(values)
    held = lax.optimization_barrier((*values, *moved))
    values, moved = held[:count], list(held[count:])
    for step in steps:
        count = len(step.received)
        step.received, moved = moved[:count], moved[count:]
        step.fold()
    return values


def key_masks(lens, length):
    middle = length // 2
    places = jnp.arange(length, dtype=jnp.int32)
    first, second = lens[:, :1], lens[:, 1:]
    single = places < first
    low = jnp.where(second > 0, single & (places < middle), single)
    high = jnp.where(second > 0, (places >= middle) & (places - middle < second), single)
    mask = jnp.where(jnp.stack([low, high], axis=1), 0.0, NEG)
    return jnp.pad(mask, ((0, 0), (0, 6), (0, 0)))


def body(
    sizes,
    tokens,
    cotangent,
    lengths,
    relevance,
    rel_table,
    w_query,
    w_key,
    w_value,
    w_output,
    w_inner,
    w_outer,
    bias_query,
    bias_value,
    bias_attn,
    bias_inner,
    bias_outer,
    gain_attn,
    shift_attn,
    gain_ffn,
    shift_ffn,
    rel_bias,
    w_score,
):
    query_size, cand_size = sizes
    devices = query_size * cand_size
    grid = Grid(query_size, cand_size)
    both = ("query", "cand")
    own_slot = lax.axis_index("cand")
    micros, length, width = tokens.shape[0], tokens.shape[3], tokens.shape[4]
    heads = rel_bias.shape[1]
    buckets = rel_bias.shape[0] * query_size
    pairs = heads // 2
    group_pairs = pairs // 3
    shard = w_query.shape[0]
    hidden = w_inner.shape[1]
    inner_shard = bias_inner.shape[0]
    place = jnp.stack([grid.at["core"], grid.at["far"]]).astype(jnp.int32)

    def own_part(value):
        rows = value.shape[0] // cand_size
        return lax.dynamic_slice_in_dim(value, own_slot * rows, rows, 0)

    def padded(row):
        row = row.reshape(1, -1)
        return jnp.pad(row, ((0, 0), (0, width - row.shape[1])))

    vectors = (
        bias_query, bias_value, bias_attn, bias_outer, gain_attn, shift_attn, gain_ffn, shift_ffn,
        w_score,
    )
    table = jnp.stack(vectors)
    table = jnp.concatenate(
        [
            jnp.pad(table, ((0, 0), (0, width - shard))),
            padded(bias_inner),
            padded(rel_bias),
            jnp.zeros((TABLE_ROWS - len(VECTORS) - 2, width), BF),
        ]
    )
    groups = (group_pairs, pairs - group_pairs)
    w_inner = lax.all_gather(own_part(w_inner), both, axis=0, tiled=True)
    stepped = shard % 32 == 0 and width // grid.sizes["far"] == TRIO == PAIR * (pairs // 2)
    if stepped:
        half = shard // 2
        blocks = pack(place, group_pairs, w_query, w_key, w_value, w_output, w_outer, table)
        head = Gather(grid, blocks[0][None])
        head.start("outer")
        block, outer_block = after(tuple(blocks[1:]), head)
        both_parts = Gather(grid, block[None])
        head.start("inner")
        both_parts.start("outer")
        (outer_block,) = after((outer_block,), head, both_parts)
        near_part = both_parts.part(0, half)
        far_part = both_parts.part(half, block.shape[0] - half)
        head.start("core", joined=False)
        near_part.start("inner")
        far_part.start("far")
        (outer_block,) = after((outer_block,), head, near_part, far_part)
        outer_part = Gather(grid, outer_block[None])
        near_part.start("far")
        far_part.start("inner")
        outer_part.start("outer")
        shapes = ((width, group_pairs * TRIO), (2 * query_size * TABLE_ROWS, width))
        first_weight, table = place_blocks(shapes, (head, ((0, half, 0, 0), (1, TABLE_ROWS, 0, 0))))
        table = table.reshape(query_size, 2, TABLE_ROWS, width)[:, 0]
    else:
        packed = jnp.stack(
            [value.reshape(shard, pairs, PAIR) for value in (w_query, w_key, w_value)], axis=2
        ).reshape(shard, pairs * TRIO)
        gather = partial(lax.all_gather, axis_name="query", axis=0, tiled=True)
        first_weight = gather(packed[:, : group_pairs * TRIO])
        second_weight = gather(packed[:, group_pairs * TRIO :])
        w_output = gather(w_output)
        w_outer = lax.all_gather(own_part(w_outer), both, axis=0, tiled=True)
        table = gather(table).reshape(query_size, TABLE_ROWS, width)

    count = len(VECTORS)
    bias_inner = table[:, count, :inner_shard].reshape(1, hidden).astype(F32)
    rel_bias = table[:, count + 1, : rel_bias.size].reshape(buckets, heads)
    table = table[:, :count, :shard].transpose(1, 0, 2).reshape(count, width).astype(F32)
    bias_qkv = jnp.stack(
        [
            table[0].reshape(pairs, PAIR),
            jnp.zeros((pairs, PAIR), F32),
            table[1].reshape(pairs, PAIR),
        ],
        axis=1,
    ).reshape(1, pairs * TRIO)
    table = jnp.pad(table, ((0, TABLE_ROWS - count), (0, 0)))

    one_hot = (rel_table[:, None] == jnp.arange(buckets, dtype=jnp.int32)[None, :]).astype(BF)
    one_hot = jnp.pad(one_hot, ((1, 0), (0, 0)))
    dist = contract(rel_bias, one_hot, 0, 1).reshape(pairs, 2, 2 * length)
    dist = jnp.pad(dist, ((0, 0), (0, 6), (0, 0)))
    own_lens = lax.dynamic_index_in_dim(lengths[:, 0], own_slot, 1, keepdims=False)
    mask = key_masks(own_lens, length)

    inputs = tokens.reshape(micros * length, width)
    held = attn_fwd(inputs, first_weight, bias_qkv, dist, mask, 0, ())
    if stepped:
        held = after(held, near_part, far_part, outer_part)
        near_part.start("core")
        far_part.start("core")
        held = after(held, near_part, far_part)
        outer_part.start("inner")
        second_weight, w_output = place_blocks(
            ((width, groups[1] * TRIO), (width, width)),
            (near_part, ((0, half, 1, 0),)),
            (far_part, ((0, half, 1, 2), (1, half, 1, 0))),
        )
    qkv, context, probs = attn_fwd(
        inputs, second_weight, bias_qkv, dist, mask, group_pairs, held
    )
    if stepped:
        qkv, context, probs = after((qkv, context, probs), outer_part)
        outer_part.start("far")
    normed_one, inv_one, low, act, slope = ffn_in(
        inputs, context, w_output, table, w_inner, bias_inner
    )
    if stepped:
        normed_one, inv_one, low, act, slope = after(
            (normed_one, inv_one, low, act, slope), outer_part
        )
        outer_part.start("core")
        (act,) = after((act,), outer_part)
        (w_outer,) = place_blocks(
            ((hidden, width),), (outer_part, ((0, w_outer.shape[0] // 2, 1, 0),))
        )
    normed_two, inv_two, hidden_out, scores = ffn_out(act, w_outer, normed_one, table, 2 * micros)

    all_scores = lax.all_gather(
        scores[:, 0, 0].reshape(micros, 1, 2), "cand", axis=1, tiled=True
    ).reshape(micros, 2 * cand_size)
    spot = jnp.stack([grid.at["core"], own_slot]).astype(jnp.int32)
    block_rows = width // devices
    grad_two, grad_outer, sums_two, loss, keep, send = outer_bwd(
        spot,
        hidden // devices,
        all_scores,
        lengths.reshape(micros, 2 * cand_size),
        relevance.reshape(micros, 2 * cand_size),
        cotangent.reshape(micros * length, width),
        normed_two,
        inv_two,
        hidden_out,
        table,
        act,
    )
    sum_outer = Scatter(grid, keep, send, ("far", "inner", "outer"))
    grad_in, grad_bias_inner = after(act_bwd(grad_outer, slope, w_outer), sum_outer)
    sum_outer.start()
    grad_one, grad_attn, sums_one, keep, send = after(
        inner_bwd(
            spot, block_rows, grad_in, w_inner, low, grad_two, normed_one, inv_one, table, context
        ),
        sum_outer,
    )
    sum_inner = Scatter(grid, keep, send, ("inner", "far", "outer"))
    sum_outer.start()
    attend = partial(attn_bwd, spot, block_rows, qkv, context)
    *early, grad_attn = after(
        (*attend(grad_attn, probs, w_output, inputs, 0, group_pairs), grad_attn),
        sum_outer,
        sum_inner,
    )
    grad_qkv, dist_grad, bias_grad, keep, send = early
    sum_early = Scatter(grid, keep, send, ("inner", "far", "outer"))
    sum_inner.start()
    sum_outer.start()
    late_qkv, late_dist, late_bias, keep, send, grad_qkv, dist_grad, bias_grad = after(
        (
            *attend(grad_attn, probs, w_output, inputs, group_pairs, pairs - group_pairs),
            grad_qkv,
            dist_grad,
            bias_grad,
        ),
        sum_early,
        sum_outer,
        sum_inner,
    )
    sum_inner.start()
    sum_early.start()

    dist_grad = jnp.concatenate([dist_grad, late_dist])[:, :2].reshape(heads, 2 * length)
    grad_rel = lax.dot_general(
        dist_grad,
        one_hot.astype(F32),
        (((1,), (0,)), ((), ())),
        precision=lax.Precision.HIGHEST,
    )
    bias_grad = jnp.concatenate([bias_grad, late_bias])[:, 0].reshape(pairs, 3, PAIR)
    small = [
        sums_one[:3],
        sums_two[:4],
        bias_grad.transpose(1, 0, 2).reshape(3, width),
        grad_bias_inner.reshape(-1, width),
        jnp.pad(grad_rel, ((0, 0), (0, width - buckets))),
    ]
    rows = sum(value.shape[0] for value in small)
    fold = keep.shape[1] // width
    small.append(jnp.zeros((-rows % (8 * fold), width), F32))
    small = jnp.concatenate(small)
    rows = small.shape[0] // fold
    rider = jnp.concatenate([small[i * rows : (i + 1) * rows] for i in range(fold)], axis=1)
    sum_late = Scatter(grid, keep, send, ("inner", "far", "outer"), rider)
    wide = group_pairs * TRIO
    grad_inputs = grad_one + contract(grad_qkv, first_weight, 1, 1)
    grad_inputs = grad_inputs + contract(late_qkv, second_weight, 1, 1)

    sum_late.fold()
    for scatter in (sum_inner, sum_early):
        scatter.fold()
    own_late = sum_late.result()
    own_early = sum_early.result()
    own_outer = sum_outer.result()
    own_inner = sum_inner.result()
    own = jnp.concatenate([own_early, own_late], axis=1).reshape(block_rows, pairs, 3, PAIR)
    own_query, own_key, own_value = [own[:, :, i].reshape(-1, width) for i in range(3)]

    small = jnp.concatenate(
        [sum_late.rider[:, i * width : (i + 1) * width] for i in range(fold)], axis=0
    )
    index = lax.axis_index("query") * cand_size + own_slot
    small_own = lax.dynamic_slice_in_dim(small, index * block_rows, block_rows, 1)
    at = 10 + hidden // width
    flat = small[10:at].reshape(-1)
    own_bias_inner = lax.dynamic_slice_in_dim(flat, index * (hidden // devices), hidden // devices)
    rel_rows = buckets // devices
    own_rel = lax.dynamic_slice_in_dim(small[at : at + heads], index * rel_rows, rel_rows, 1)
    shape = (micros, 1, 1, length, width)
    return (
        hidden_out.reshape(shape),
        loss[:, :1],
        grad_inputs.reshape(shape),
        own_query,
        own_key,
        own_value,
        own_inner[:, hidden:],
        own_inner[:, :hidden],
        own_outer,
        small_own[7],
        small_own[9],
        small_own[2],
        own_bias_inner,
        small_own[5],
        small_own[0],
        small_own[1],
        small_own[3],
        small_own[4],
        own_rel.T,
        small_own[6],
    )


def solution(mesh):
    both = ("query", "cand")
    slots = P(None, "query", "cand", None, None)
    lists = P(None, "query", None, None)
    rows = P("query", None)
    vec_spec = P("query")
    return jax.shard_map(
        partial(body, (mesh.shape["query"], mesh.shape["cand"])),
        mesh=mesh,
        in_specs=(slots, slots, lists, lists, P()) + (rows,) * 6 + (vec_spec,) * 9 + (rows, vec_spec),
        out_specs=(slots, P(None, "query"), slots)
        + (P(both, None),) * 6
        + (P(both),) * 9
        + (P(both, None), P(both)),
        check_vma=False,
    )
```

```python
from functools import partial

import jax
import jax.numpy as jnp
import numpy as np
from jax import lax
from jax.experimental import pallas as pl
from jax.experimental.pallas import tpu as pltpu
from jax.sharding import PartitionSpec as P

HD = 64
PAIR = 2 * HD
TRIO = 3 * PAIR
TILE = 128
BF = jnp.bfloat16
F32 = jnp.float32
NEG = -1000000000.0
EPS = 1e-05

ERFC_P = 0.3
ERFC_C = (
    0.16919777981386785,
    0.17054619772689322,
    0.14956727662616615,
    0.21002273459109255,
    -0.08286335340540726,
    0.5302129644860679,
    -0.49655482906135956,
    0.4777385344298923,
    -0.12786727948795917,
)

VECTORS = (
    "bias_query",
    "bias_value",
    "bias_attn",
    "bias_outer",
    "gain_attn",
    "shift_attn",
    "gain_ffn",
    "shift_ffn",
    "w_score",
)
TABLE_ROWS = 16
ROW = {name: index for index, name in enumerate(VECTORS)}


def cost(micros=0.001):
    return pl.CostEstimate(flops=int(micros * 1.15e9), bytes_accessed=0, transcendentals=0)


def contract(left_mat, right_mat, left_dim, right_dim):
    return lax.dot_general(
        left_mat,
        right_mat,
        (((left_dim,), (right_dim,)), ((), ())),
        preferred_element_type=F32,
    )


def gelu_pair(u):
    size = jnp.abs(u)
    t = 1.0 / (1.0 + (ERFC_P * 0.5**0.5) * size)
    poly = jnp.full_like(u, 0.5 * ERFC_C[-1])
    for coef in ERFC_C[-2::-1]:
        poly = poly * t + 0.5 * coef
    bell = jnp.exp(-0.5 * (u * u))
    tail = poly * t * bell
    cdf = jnp.where(u < 0, tail, 1.0 - tail)
    return u * cdf, cdf + u * ((2.0 * np.pi) ** -0.5 * bell)


def normalise(values):
    centred = values - jnp.mean(values, axis=-1, keepdims=True)
    inv_std = lax.rsqrt(jnp.mean(centred * centred, axis=-1, keepdims=True) + EPS)
    return centred * inv_std, inv_std


def norm_backward(grad_out, normed, inv_std, gain_vec):
    grad_normed = grad_out * gain_vec
    return inv_std * (
        grad_normed
        - jnp.mean(grad_normed, axis=-1, keepdims=True)
        - normed * jnp.mean(grad_normed * normed, axis=-1, keepdims=True)
    )


def row_chunks(rows, size, step):
    size = min(size, rows)

    @pl.loop(0, rows // size)
    def _(index):
        step(pl.ds(pl.multiple_of(index * size, size), size))


def split_rows(core, tile, rows, spots, keep, send):
    for block, spot in enumerate(spots):
        place = slice(spot * rows, (spot + 1) * rows)
        if rows % 8 == 0:
            own = pl.multiple_of((2 * block + core) * rows, 8)
            other = pl.multiple_of((2 * block + 1 - core) * rows, 8)
            keep[place, :] = tile[pl.ds(own, rows), :]
            send[place, :] = tile[pl.ds(other, rows), :]
        else:
            even = tile[2 * block * rows : (2 * block + 1) * rows, :]
            odd = tile[(2 * block + 1) * rows : (2 * block + 2) * rows, :]
            keep[place, :] = jnp.where(core == 0, even, odd)
            send[place, :] = jnp.where(core == 0, odd, even)


def attn_fwd_kernel(x_ref, w_ref, b_ref, dist_ref, mask_ref, *refs):
    qkv_ref, ctx_ref, p_ref, table = refs[-4:]
    length = x_ref.shape[0]
    width = 2 * length

    @pl.when(pl.program_id(1) == 0)
    def _():
        for head in range(2):
            row = jnp.broadcast_to(dist_ref[0, head : head + 1, :], (TILE, width))
            table[head] = pltpu.roll(row, 0, 1, stride=1, stride_axis=0)

    qkv = (contract(x_ref[...], w_ref[...], 1, 0) + b_ref[...]).astype(BF)
    qkv_ref[...] = qkv
    q = qkv[:, :PAIR] * jnp.asarray(HD**-0.5, BF)
    k = qkv[:, PAIR : 2 * PAIR]
    v = qkv[:, 2 * PAIR :]
    lane = lax.broadcasted_iota(jnp.int32, (length, PAIR), 1)
    outs = []
    for head in range(2):
        own = (lane < HD) == (head == 0)
        raw = contract(jnp.where(own, q, jnp.zeros_like(q)), k, 1, 1)
        for start in range(0, length, TILE):
            half = start // (length // 2)
            logits = (
                raw[start : start + TILE]
                + table[head, :, length - start : width - start]
                + mask_ref[0, half : half + 1, :]
            )
            peak = jnp.max(logits, axis=1, keepdims=True)
            grown = jnp.exp(logits - peak)
            total = jnp.sum(grown, axis=1, keepdims=True)
            p_ref[0, head, start : start + TILE, :] = (grown * (1.0 / total)).astype(BF)
        outs.append(contract(p_ref[0, head], v, 1, 0))
    ctx_ref[...] = jnp.where(lane < HD, outs[0], outs[1]).astype(BF)


def attn_fwd(inputs, weight, bias, dist, mask, first, held):
    rows, width = inputs.shape
    micros = mask.shape[0]
    length = rows // micros
    pairs = weight.shape[1] // TRIO
    every = bias.shape[1] // TRIO
    return pl.pallas_call(
        attn_fwd_kernel,
        grid=(pairs, micros),
        in_specs=[
            pl.BlockSpec((length, width), lambda h, m: (m, 0)),
            pl.BlockSpec((width, TRIO), lambda h, m: (0, h)),
            pl.BlockSpec((1, TRIO), lambda h, m: (0, h + first)),
            pl.BlockSpec((1, 8, 2 * length), lambda h, m: (h + first, 0, 0)),
            pl.BlockSpec((1, 8, length), lambda h, m: (m, 0, 0)),
        ]
        + [pl.BlockSpec(memory_space=pl.ANY)] * len(held),
        out_specs=[
            pl.BlockSpec((length, TRIO), lambda h, m: (m, h + first)),
            pl.BlockSpec((length, PAIR), lambda h, m: (m, h + first)),
            pl.BlockSpec((1, 2, length, length), lambda h, m: (m, h + first, 0, 0)),
        ],
        out_shape=[
            jax.ShapeDtypeStruct((rows, every * TRIO), BF),
            jax.ShapeDtypeStruct((rows, every * PAIR), BF),
            jax.ShapeDtypeStruct((micros, 2 * every, length, length), BF),
        ],
        input_output_aliases={5 + index: index for index in range(len(held))},
        scratch_shapes=[pltpu.VMEM((2, TILE, 2 * length), F32)],
        compiler_params=pltpu.CompilerParams(vmem_limit_bytes=62 << 20),
        cost_estimate=cost(),
        name="attn_fwd",
    )(inputs, weight, bias, dist, mask, *held)


def attn_bwd_kernel(
    blocks, place_ref, qkv_ref, o_ref, dr_ref, p_ref, wo_ref, x_ref, *refs
):
    dqkv_ref, gd_ref, db_ref, keep_ref, send_ref, acc, dsb, dw, kept, sent = refs[-10:]
    length = qkv_ref.shape[0]
    width = 2 * length
    first = pl.program_id(1) == 0
    last = pl.program_id(1) == pl.num_programs(1) - 1

    @pl.when(first)
    def _():
        acc[...] = jnp.zeros_like(acc)
        dw[...] = jnp.zeros_like(dw)
        db_ref[...] = jnp.zeros_like(db_ref)

    q = qkv_ref[:, :PAIR]
    k = qkv_ref[:, PAIR : 2 * PAIR]
    v = qkv_ref[:, 2 * PAIR :]
    do = contract(dr_ref[...], wo_ref[...], 1, 1).astype(BF)
    lane = lax.broadcasted_iota(jnp.int32, (length, PAIR), 1)
    prod = do.astype(F32) * o_ref[...].astype(F32)
    dq, dk, dv = [], [], []
    for head in range(2):
        own = (lane < HD) == (head == 0)
        inner = jnp.sum(jnp.where(own, prod, 0.0), axis=1, keepdims=True)
        dp = contract(jnp.where(own, do, jnp.zeros_like(do)), v, 1, 1)
        for start in range(0, length, TILE):
            rows = slice(start, start + TILE)
            ds = p_ref[0, head, rows, :].astype(F32) * (dp[rows] - inner[rows])
            acc[head, :, length - start : width - start] += ds
            dsb[head, rows, :] = (ds * HD**-0.5).astype(BF)
        dq.append(contract(dsb[head], k, 1, 0))
        dk.append(contract(dsb[head], q, 0, 0))
        dv.append(contract(p_ref[0, head], do, 0, 0))
    for index, (low, high) in enumerate((dq, dk, dv)):
        cols = slice(index * PAIR, (index + 1) * PAIR)
        grad = jnp.where(lane < HD, low, high).astype(BF)
        dqkv_ref[:, cols] = grad
        db_ref[0, 0:1, cols] += jnp.sum(grad.astype(F32), axis=0, keepdims=True)
    dw[...] += contract(x_ref[...], dqkv_ref[...], 0, 0)

    @pl.when(last)
    def _():
        split_rows(place_ref[3], dw, *blocks, kept, sent)
        keep_ref[...] = kept[...].astype(BF)
        send_ref[...] = sent[...].astype(BF)
        for head in range(2):
            total = acc[head, 0:8, :]
            for start in range(8, TILE, 8):
                total = total + pltpu.roll(acc[head, start : start + 8, :], width - start, 1)
            row = total[0:1, :]
            for step in range(1, 8):
                row = row + pltpu.roll(total[step : step + 1, :], width - step, 1)
            gd_ref[0, head : head + 1, :] = row


def attn_bwd(
    place, blocks, qkv, ctx, d_r, probs, w_output, inputs, first, pairs, held=(), start=0, every=None
):
    rows, width = inputs.shape
    micros, _, length, _ = probs.shape
    at = lambda shape, place: pl.BlockSpec(shape, lambda h, m, c: place(h, m))
    half = width // 2
    every = every or pairs
    return pl.pallas_call(
        partial(attn_bwd_kernel, blocks),
        grid_spec=pltpu.PrefetchScalarGridSpec(
            num_scalar_prefetch=1,
            grid=(pairs, micros),
            in_specs=[
                at((length, TRIO), lambda h, m: (m, h + first)),
                at((length, PAIR), lambda h, m: (m, h + first)),
                at((length, width), lambda h, m: (m, 0)),
                at((1, 2, length, length), lambda h, m: (m, h + first, 0, 0)),
                at((PAIR, width), lambda h, m: (h + first, 0)),
                at((length, width), lambda h, m: (m, 0)),
            ]
            + [pl.BlockSpec(memory_space=pl.ANY)] * len(held),
            out_specs=[
                at((length, TRIO), lambda h, m: (m, h + start)),
                at((1, 8, 2 * length), lambda h, m: (h + start, 0, 0)),
                at((1, 8, TRIO), lambda h, m: (h + start, 0, 0)),
                at((half, TRIO), lambda h, m: (0, h + start)),
                at((half, TRIO), lambda h, m: (0, h + start)),
            ],
            scratch_shapes=[
                pltpu.VMEM((2, TILE, 2 * length), F32),
                pltpu.VMEM((2, length, length), BF),
                pltpu.VMEM((width, TRIO), F32),
                pltpu.VMEM((half, TRIO), F32),
                pltpu.VMEM((half, TRIO), F32),
            ],
        ),
        out_shape=[
            jax.ShapeDtypeStruct((rows, every * TRIO), BF),
            jax.ShapeDtypeStruct((every, 8, 2 * length), F32),
            jax.ShapeDtypeStruct((every, 8, TRIO), F32),
            jax.ShapeDtypeStruct((half, every * TRIO), BF),
            jax.ShapeDtypeStruct((half, every * TRIO), BF),
        ],
        input_output_aliases={7 + index: index for index in range(len(held))},
        compiler_params=pltpu.CompilerParams(vmem_limit_bytes=62 << 20),
        cost_estimate=cost(),
        name="attn_bwd",
    )(place, qkv, ctx, d_r, probs, w_output, inputs, *held)


def vec(ref, name):
    return ref[ROW[name] : ROW[name] + 1, :]


def ffn_in_kernel(
    x_ref, ctx_ref, wo_ref, vec_ref, w_ref, b_ref, n1_ref, i1_ref, low_ref, act_ref, slope_ref
):
    rows = x_ref.shape[0]

    @pl.when(pl.program_id(0) == 0)
    def _():
        size = min(256, rows)
        for start in range(0, rows, size):
            at = slice(start, start + size)
            attn = contract(ctx_ref[at, :], wo_ref[...], 1, 0) + vec(vec_ref, "bias_attn")
            normed, inv_std = normalise(x_ref[at, :].astype(F32) + attn)
            n1_ref[at, :] = normed
            i1_ref[at, :] = inv_std
            first = normed * vec(vec_ref, "gain_attn") + vec(vec_ref, "shift_attn")
            low_ref[at, :] = first.astype(BF)

    low = low_ref[...]
    wide = w_ref.shape[1]
    size = min(256, wide)
    for start in range(0, wide, size):
        cols = slice(start, start + size)
        u = contract(low, w_ref[:, cols], 1, 0) + b_ref[:, cols]
        act, slope = gelu_pair(u)
        act_ref[:, cols] = act.astype(BF)
        slope_ref[:, cols] = slope.astype(BF)


def ffn_in(inputs, context, w_output, vectors, w_inner, bias):
    rows, width = inputs.shape
    hidden = w_inner.shape[1]
    size = min(512, hidden)
    whole = pl.BlockSpec((rows, width), lambda n: (0, 0))
    column = pl.BlockSpec((rows, 1), lambda n: (0, 0))
    cols = pl.BlockSpec((rows, size), lambda n: (0, n))
    out = jax.ShapeDtypeStruct((rows, hidden), BF)
    return pl.pallas_call(
        ffn_in_kernel,
        grid=(hidden // size,),
        in_specs=[
            whole,
            whole,
            pl.BlockSpec((width, width), lambda n: (0, 0)),
            pl.BlockSpec((TABLE_ROWS, width), lambda n: (0, 0)),
            pl.BlockSpec((width, size), lambda n: (0, n)),
            pl.BlockSpec((1, size), lambda n: (0, n)),
        ],
        out_specs=[whole, column, whole, cols, cols],
        out_shape=[
            jax.ShapeDtypeStruct((rows, width), F32),
            jax.ShapeDtypeStruct((rows, 1), F32),
            jax.ShapeDtypeStruct((rows, width), BF),
            out,
            out,
        ],
        compiler_params=pltpu.CompilerParams(vmem_limit_bytes=62 << 20),
        cost_estimate=cost(),
        name="ffn_in",
    )(inputs, context, w_output, vectors, w_inner, bias)


def ffn_out_kernel(act_ref, w_ref, n1_ref, vec_ref, n2_ref, i2_ref, hid_ref, score_ref):
    first = n1_ref[...] * vec(vec_ref, "gain_attn") + vec(vec_ref, "shift_attn")
    outer = contract(act_ref[...], w_ref[...], 1, 0) + vec(vec_ref, "bias_outer")
    normed, inv_std = normalise(first + outer)
    n2_ref[...] = normed
    i2_ref[...] = inv_std
    low = (normed * vec(vec_ref, "gain_ffn") + vec(vec_ref, "shift_ffn")).astype(BF)
    hid_ref[...] = low
    row = low[0:8, :].astype(F32)[0:1, :] * vec(vec_ref, "w_score")
    score_ref[0] = jnp.broadcast_to(jnp.sum(row, axis=1, keepdims=True), score_ref.shape[1:])


def ffn_out(act, w_outer, normed, vectors, count):
    rows, hidden = act.shape
    width = w_outer.shape[1]
    size = rows // count
    block = pl.BlockSpec((size, width), lambda r: (r, 0))
    return pl.pallas_call(
        ffn_out_kernel,
        grid=(count,),
        in_specs=[
            pl.BlockSpec((size, hidden), lambda r: (r, 0)),
            pl.BlockSpec((hidden, width), lambda r: (0, 0)),
            block,
            pl.BlockSpec((TABLE_ROWS, width), lambda r: (0, 0)),
        ],
        out_specs=[
            block,
            pl.BlockSpec((size, 1), lambda r: (r, 0)),
            block,
            pl.BlockSpec((1, 8, 128), lambda r: (r, 0, 0)),
        ],
        out_shape=[
            jax.ShapeDtypeStruct((rows, width), F32),
            jax.ShapeDtypeStruct((rows, 1), F32),
            jax.ShapeDtypeStruct((rows, width), BF),
            jax.ShapeDtypeStruct((count, 8, 128), F32),
        ],
        compiler_params=pltpu.CompilerParams(vmem_limit_bytes=62 << 20),
        cost_estimate=cost(),
        name="ffn_out",
    )(act, w_outer, normed, vectors)


def list_loss(scores, lens, relevance):
    present = lens > 0
    masked = jnp.where(present, scores, NEG)
    peak = jnp.max(masked, axis=1, keepdims=True)
    log_total = peak + jnp.log(jnp.sum(jnp.exp(masked - peak), axis=1, keepdims=True))
    log_prob = masked - log_total
    rel = jnp.where(present, relevance, NEG)
    rel_exp = jnp.exp(rel - jnp.max(rel, axis=1, keepdims=True))
    target = rel_exp / jnp.sum(rel_exp, axis=1, keepdims=True)
    loss = -jnp.sum(jnp.where(present, target * log_prob, 0.0), axis=1, keepdims=True)
    return loss, jnp.where(present, jnp.exp(log_prob) - target, 0.0)


def outer_bwd_kernel(
    blocks, place_ref, score_ref, len_ref, rel_ref, cot_ref, n2_ref, i2_ref, hid_ref, vec_ref,
    act_ref, dr_ref, low, sum_ref, loss_ref, keep_ref, send_ref, tile, kept, sent,
):
    rows, width = cot_ref.shape

    @pl.when(pl.program_id(0) == 0)
    def _():
        loss, grad = list_loss(score_ref[...], len_ref[...], rel_ref[...])
        loss_ref[...] = jnp.broadcast_to(loss, loss_ref.shape)
        lane = lax.broadcasted_iota(jnp.int32, grad.shape, 1)
        micros = grad.shape[0]
        sum_ref[...] = jnp.zeros_like(sum_ref)
        firsts = {}
        for half in range(2):
            own = jnp.where(lane == 2 * place_ref[4] + half, grad, 0.0)
            own = jnp.sum(own, axis=1, keepdims=True)
            for micro in range(micros):
                firsts[(2 * micro + half) * (rows // (2 * micros))] = own[micro : micro + 1, :]
        score_row = vec(vec_ref, "w_score")
        gain = vec(vec_ref, "gain_ffn")

        def step(at):
            grad_out = cot_ref[at, :].astype(F32)
            place = lax.broadcasted_iota(jnp.int32, (grad_out.shape[0], 1), 0) + at.start
            shift = jnp.zeros_like(place, F32)
            for first, value in firsts.items():
                shift = jnp.where(place == first, value, shift)
            grad_out = grad_out + shift * score_row
            normed = n2_ref[at, :]
            grad_in = norm_backward(grad_out, normed, i2_ref[at, :], gain)
            dr_ref[at, :] = grad_in
            grad_low = grad_in.astype(BF)
            low[at, :] = grad_low
            sum_ref[0:1, :] += jnp.sum(grad_out * normed, axis=0, keepdims=True)
            sum_ref[1:2, :] += jnp.sum(grad_out, axis=0, keepdims=True)
            sum_ref[2:3, :] += jnp.sum(grad_low.astype(F32), axis=0, keepdims=True)

        row_chunks(rows, 128, step)
        total = jnp.zeros((1, width), F32)
        for first, value in firsts.items():
            total = total + value * hid_ref[first : first + 8, :].astype(F32)[0:1, :]
        sum_ref[3:4, :] = total

    tile[...] = contract(act_ref[...], low[...], 0, 0)
    split_rows(place_ref[3], tile, *blocks, kept, sent)
    keep_ref[...] = kept[...].astype(BF).reshape(keep_ref.shape)
    send_ref[...] = sent[...].astype(BF).reshape(send_ref.shape)


def outer_bwd(
    place, blocks, scores, lens, relevance, cot, normed, inv_std, hid, vectors, act
):
    rows, width = cot.shape
    hidden = act.shape[1]
    size = width
    at = lambda shape, index: pl.BlockSpec(shape, lambda n, c: index(n))
    whole = at((rows, width), lambda n: (0, 0))
    tiny = at(scores.shape, lambda n: (0, 0))
    rows_of, spots = blocks
    tiles = hidden // size
    half = at((len(spots), 1, rows_of, width), lambda n: (0, n, 0, 0))
    return pl.pallas_call(
        partial(outer_bwd_kernel, blocks),
        grid_spec=pltpu.PrefetchScalarGridSpec(
            num_scalar_prefetch=1,
            grid=(hidden // size,),
            in_specs=[
                tiny, tiny, tiny, whole, whole, at((rows, 1), lambda n: (0, 0)), whole,
                at((TABLE_ROWS, width), lambda n: (0, 0)), at((rows, size), lambda n: (0, n)),
            ],
            out_specs=[
                whole, whole, at((8, width), lambda n: (0, 0)),
                at((scores.shape[0], 128), lambda n: (0, 0)), half, half,
            ],
            scratch_shapes=[
                pltpu.VMEM((size, width), F32),
                pltpu.VMEM((size // 2, width), F32),
                pltpu.VMEM((size // 2, width), F32),
            ],
        ),
        out_shape=[
            jax.ShapeDtypeStruct((rows, width), F32),
            jax.ShapeDtypeStruct((rows, width), BF),
            jax.ShapeDtypeStruct((8, width), F32),
            jax.ShapeDtypeStruct((scores.shape[0], 128), F32),
            jax.ShapeDtypeStruct((len(spots), tiles, rows_of, width), BF),
            jax.ShapeDtypeStruct((len(spots), tiles, rows_of, width), BF),
        ],
        compiler_params=pltpu.CompilerParams(vmem_limit_bytes=62 << 20),
        cost_estimate=cost(),
        name="outer_bwd",
    )(place, scores, lens, relevance, cot, normed, inv_std, hid, vectors, act)


def act_bwd_kernel(dr_ref, slope_ref, w2_ref, din_ref, db_ref):
    grad = dr_ref[...]
    wide = w2_ref.shape[0]
    size = min(256, wide)
    for start in range(0, wide, size):
        cols = slice(start, start + size)
        d_act = contract(grad, w2_ref[cols, :], 1, 1)
        d_in = (d_act * slope_ref[:, cols].astype(F32)).astype(BF)
        din_ref[:, cols] = d_in
        db_ref[:, cols] = jnp.sum(d_in.astype(F32), axis=0, keepdims=True)


def act_bwd(grad, slope, w_outer):
    rows, hidden = slope.shape
    width = grad.shape[1]
    size = min(512, hidden)
    cols = pl.BlockSpec((rows, size), lambda n: (0, n))
    return pl.pallas_call(
        act_bwd_kernel,
        grid=(hidden // size,),
        in_specs=[
            pl.BlockSpec((rows, width), lambda n: (0, 0)),
            cols,
            pl.BlockSpec((size, width), lambda n: (n, 0)),
        ],
        out_specs=[cols, pl.BlockSpec((1, size), lambda n: (0, n))],
        out_shape=[
            jax.ShapeDtypeStruct((rows, hidden), BF),
            jax.ShapeDtypeStruct((1, hidden), F32),
        ],
        compiler_params=pltpu.CompilerParams(vmem_limit_bytes=62 << 20),
        cost_estimate=cost(),
        name="act_bwd",
    )(grad, slope, w_outer)


def inner_bwd_kernel(
    blocks, place_ref, din_ref, w1_ref, low_ref, dr_ref, n1_ref, i1_ref, vec_ref, ctx_ref,
    one_ref, grad_ref, sum_ref, keep_ref, send_ref, acc, tile, kept, sent,
):
    step_id = pl.program_id(0)
    last = pl.num_programs(0) - 1
    rows = low_ref.shape[0]

    @pl.when(step_id < last)
    def _():
        d_in = din_ref[...]
        tile[...] = contract(low_ref[...], d_in, 0, 0)
        part = contract(d_in, w1_ref[...], 1, 1)

        @pl.when(step_id == 0)
        def _():
            acc[...] = dr_ref[...] + part

        @pl.when(step_id > 0)
        def _():
            acc[...] += part

    @pl.when(step_id == last)
    def _():
        sum_ref[...] = jnp.zeros_like(sum_ref)
        gain = vec(vec_ref, "gain_attn")

        def step(at):
            grad_out = acc[at, :]
            normed = n1_ref[at, :]
            grad_in = norm_backward(grad_out, normed, i1_ref[at, :], gain)
            one_ref[at, :] = grad_in
            grad_low = grad_in.astype(BF)
            grad_ref[at, :] = grad_low
            sum_ref[0:1, :] += jnp.sum(grad_out * normed, axis=0, keepdims=True)
            sum_ref[1:2, :] += jnp.sum(grad_out, axis=0, keepdims=True)
            sum_ref[2:3, :] += jnp.sum(grad_low.astype(F32), axis=0, keepdims=True)

        row_chunks(rows, 128, step)
        tile[...] = contract(ctx_ref[...], grad_ref[...], 0, 0)

    split_rows(place_ref[3], tile, *blocks, kept, sent)
    keep_ref[...] = kept[...].astype(BF)
    send_ref[...] = sent[...].astype(BF)


def inner_bwd(place, blocks, d_in, w_inner, low, d_r, normed, inv_std, vectors, context):
    rows, width = low.shape
    hidden = d_in.shape[1]
    size = width
    tiles = hidden // size
    at = lambda shape, index: pl.BlockSpec(shape, lambda n, c: index(n))
    whole = at((rows, width), lambda n: (0, 0))
    near = lambda n: (0, jnp.minimum(n, tiles - 1))
    half = at((width // 2, size), lambda n: (0, n))
    return pl.pallas_call(
        partial(inner_bwd_kernel, blocks),
        grid_spec=pltpu.PrefetchScalarGridSpec(
            num_scalar_prefetch=1,
            grid=(tiles + 1,),
            in_specs=[
                at((rows, size), near), at((width, size), near), whole, whole, whole,
                at((rows, 1), lambda n: (0, 0)), at((TABLE_ROWS, width), lambda n: (0, 0)), whole,
            ],
            out_specs=[whole, whole, at((8, width), lambda n: (0, 0)), half, half],
            scratch_shapes=[
                pltpu.VMEM((rows, width), F32),
                pltpu.VMEM((width, size), F32),
                pltpu.VMEM((width // 2, size), F32),
                pltpu.VMEM((width // 2, size), F32),
            ],
        ),
        out_shape=[
            jax.ShapeDtypeStruct((rows, width), F32),
            jax.ShapeDtypeStruct((rows, width), BF),
            jax.ShapeDtypeStruct((8, width), F32),
            jax.ShapeDtypeStruct((width // 2, hidden + width), BF),
            jax.ShapeDtypeStruct((width // 2, hidden + width), BF),
        ],
        compiler_params=pltpu.CompilerParams(vmem_limit_bytes=62 << 20),
        cost_estimate=cost(),
        name="inner_bwd",
    )(place, d_in, w_inner, low, d_r, normed, inv_std, vectors, context)


def shifted(axis_size, group, stride, step):
    pairs = []
    for source in range(axis_size):
        place = source // stride % group
        pairs.append((source, source + ((place + step) % group - place) * stride))
    return pairs


class Grid:
    def __init__(self, query_size, cand_size):
        query, cand = lax.axis_index("query"), lax.axis_index("cand")
        self.sizes = {"outer": query_size // 2, "inner": 2, "far": cand_size // 2, "core": 2}
        self.lengths = {"query": query_size, "cand": cand_size}
        self.axes = {
            "outer": ("query", 2),
            "inner": ("query", 1),
            "far": ("cand", 2),
            "core": ("cand", 1),
        }
        self.at = {
            "outer": query // 2,
            "inner": query % 2,
            "far": cand // 2,
            "core": cand % 2,
        }

    def move(self, value, dim, step):
        axis, stride = self.axes[dim]
        return lax.ppermute(
            value, axis, shifted(self.lengths[axis], self.sizes[dim], stride, step)
        )


def pack_kernel(pairs, place_ref, wq, wk, wv, wo, table, first, middle):
    far, core = place_ref[2], place_ref[3]
    half = wq.shape[0] // 2
    rows = pl.ds(pl.multiple_of(core * half, 16), half)
    for pair in range(pairs):
        for index, weight in enumerate((wq, wk, wv)):
            to = (pair * 3 + index) * PAIR
            first[:half, to : to + PAIR] = weight[rows, pair * PAIR : (pair + 1) * PAIR]
    first[half:, :] = table[...]
    count = wq.shape[1] // PAIR // pairs - 1
    for run in range(count):
        cols = pl.ds(pl.multiple_of(((run + 1) * pairs + far) * PAIR, PAIR), PAIR)
        for index, weight in enumerate((wq, wk, wv)):
            middle[run * half : (run + 1) * half, index * PAIR : (index + 1) * PAIR] = weight[rows, cols]
    wide = wo.shape[1] // 2
    cols = pl.ds(pl.multiple_of(far * wide, PAIR), wide)
    middle[count * half :, :] = wo[rows, cols]


def pack(place, pairs, wq, wk, wv, wo, table):
    shard, width = wq.shape
    half = shard // 2
    count = width // PAIR // pairs
    shapes = [
        (half + TABLE_ROWS, pairs * TRIO),
        (count * half, width // 2),
    ]
    return pl.pallas_call(
        partial(pack_kernel, pairs),
        grid_spec=pltpu.PrefetchScalarGridSpec(
            num_scalar_prefetch=1,
            grid=(1,),
            in_specs=[
                pl.BlockSpec(value.shape, lambda i, c: (0, 0)) for value in (wq, wk, wv, wo, table)
            ],
            out_specs=[pl.BlockSpec(shape, lambda i, c: (0, 0)) for shape in shapes],
        ),
        out_shape=[jax.ShapeDtypeStruct(shape, BF) for shape in shapes],
        compiler_params=pltpu.CompilerParams(vmem_limit_bytes=60 << 20),
        cost_estimate=cost(),
        name="pack",
    )(place, wq, wk, wv, wo, table)


def join_kernel(runs, count, *refs):
    sources, targets = refs[:count], refs[count:]
    at = 0
    for source in sources:
        size = source.shape[0]
        for target, (first, rows) in zip(targets, runs):
            target[at : at + size] = source[:, first : first + rows, :]
        at += size


def join(pieces, runs):
    total = sum(piece.shape[0] for piece in pieces)
    wide = pieces[0].shape[2]
    whole = lambda shape: pl.BlockSpec(shape, lambda i: (0, 0, 0))
    shapes = [(total, rows, wide) for _, rows in runs]
    return pl.pallas_call(
        partial(join_kernel, runs, len(pieces)),
        grid=(1,),
        in_specs=[whole(piece.shape) for piece in pieces],
        out_specs=[whole(shape) for shape in shapes],
        out_shape=[jax.ShapeDtypeStruct(shape, BF) for shape in shapes],
        compiler_params=pltpu.CompilerParams(vmem_limit_bytes=62 << 20),
        cost_estimate=cost(),
        name="join",
    )(*pieces)


class Gather:
    def __init__(self, grid, blocks, places=None):
        self.grid = grid
        self.pieces = [blocks]
        self.places = [places or [{"outer": 0, "inner": 0, "far": 0, "core": 0}]]
        self.received = []

    def joined(self, *runs):
        places = sum(self.places, [])
        runs = runs or ((0, self.pieces[0].shape[1]),)
        return [Gather(self.grid, piece, places) for piece in join(self.pieces, runs)]

    def start(self, dim):
        size = self.grid.sizes[dim]
        self.coming = []
        for piece, places in zip(self.pieces, self.places):
            for step in range(1, size):
                self.received.append(self.grid.move(piece, dim, step))
                self.coming.append(
                    [{**place, dim: (place[dim] + step) % size} for place in places]
                )

    def fold(self):
        self.pieces = self.pieces + self.received
        self.places = self.places + self.coming
        self.received = []


def place_kernel(splits, places, outer, spot_ref, *refs):
    count = 1 + max(run[0] for split in splits for run in split)
    sources, targets, sems = refs[: -1 - count], refs[-1 - count : -1], refs[-1]
    copies = []
    at = 0
    for source, split in zip(sources, splits):
        wide = source.shape[-1]
        for index in range(source.shape[0]):
            place = places[at]
            zed = lax.rem(spot_ref[0] + (outer - place["outer"]), outer)
            other = {
                dim: lax.rem(spot_ref[i] + place[dim], 2)
                for i, dim in enumerate(("inner", "far", "core"), 1)
            }
            block = (zed * 2 + other["inner"]) * 2 + other["core"]
            first = 0
            for target, rows, stride, offset in split:
                cols = slice(None)
                if stride:
                    col = other["far"] * (stride * wide) + offset * wide
                    cols = pl.ds(pl.multiple_of(col, 128), wide)
                copies.append(
                    pltpu.make_async_copy(
                        source.at[index, pl.ds(first, rows), :],
                        targets[target].at[pl.ds(pl.multiple_of(block * rows, 16), rows), cols],
                        sems.at[len(copies)],
                    )
                )
                first += rows
            at += 1
    for copy in copies:
        copy.start()
    for copy in copies:
        copy.wait()


def place_blocks(spot, shapes, *gathers):
    places, pieces, splits, copies = [], [], [], 0
    for gather, split in gathers:
        for piece, found in zip(gather.pieces, gather.places):
            pieces.append(piece)
            splits.append(split)
            places += found
            copies += len(found) * len(split)
    return pl.pallas_call(
        partial(place_kernel, splits, places, gather.grid.sizes["outer"]),
        grid_spec=pltpu.PrefetchScalarGridSpec(
            num_scalar_prefetch=1,
            grid=(1,),
            in_specs=[pl.BlockSpec(memory_space=pl.ANY)] * len(pieces),
            out_specs=[pl.BlockSpec(memory_space=pltpu.VMEM)] * len(shapes),
            scratch_shapes=[pltpu.SemaphoreType.DMA((copies,))],
        ),
        out_shape=[jax.ShapeDtypeStruct(shape, BF) for shape in shapes],
        compiler_params=pltpu.CompilerParams(vmem_limit_bytes=24 << 20),
        cost_estimate=cost(),
        name="place_blocks",
    )(spot, *pieces)


class Scatter:
    def __init__(self, grid, keep, send, order):
        self.grid = grid
        self.dims = list(order)
        self.order = list(order)
        self.sizes = [grid.sizes[dim] for dim in self.dims]
        self.rider, self.others = None, ()
        self.parts = [self.blocks(keep)]
        self.shape = self.blocks(send).shape
        self.received = [grid.move(send, "core", 1)]

    def blocks(self, value):
        return value.reshape(*self.sizes, -1, value.shape[-1])

    @staticmethod
    def spots(grid, order, tiles=1):
        sizes = {dim: grid.sizes[dim] for dim in order}
        if tiles > 1:
            sizes["outer"] //= tiles
        spots = []
        for block in range(int(np.prod(list(sizes.values())))):
            at = {
                "outer": block // (2 * sizes["far"]),
                "inner": block // sizes["far"] % 2,
                "far": block % sizes["far"],
            }
            spot = 0
            for dim in order:
                spot = spot * sizes[dim] + at[dim]
            spots.append(spot)
        return tuple(spots)

    def step(self, dim):
        axis = self.dims.index(dim)
        size, here = self.grid.sizes[dim], self.grid.at[dim]
        sent = []
        for step in range(1, size):
            total = 0.0
            for part in self.parts:
                piece = lax.dynamic_index_in_dim(part, (here + step) % size, axis, keepdims=False)
                total += piece.astype(F32)
            sent.append(total.astype(BF))
        self.parts = [
            lax.dynamic_index_in_dim(part, here, axis, keepdims=False) for part in self.parts
        ]
        self.dims.remove(dim)
        return sent

    def start(self, *others):
        dim = self.order.pop(0)
        sent = self.step(dim)
        self.others = others
        self.shape = sent[0].shape
        for other in others:
            other.order.remove(dim)
            more = other.step(dim)
            other.shape = more[0].shape
            sent = [jnp.concatenate(pair, axis=-1) for pair in zip(sent, more)]
        if self.rider is not None:
            wide = sent[0].shape[-1]
            rider = jnp.pad(self.rider, ((0, 0), (0, wide - self.rider.shape[1]))).astype(BF)
            sent = [jnp.concatenate([value.reshape(-1, wide), rider]) for value in sent]
        self.received = [self.grid.move(value, dim, step) for step, value in enumerate(sent, 1)]

    def fold(self):
        for value in self.received:
            if self.rider is not None:
                count = value.shape[0] - self.rider.shape[0]
                self.rider = self.rider + value[count:, : self.rider.shape[1]].astype(F32)
                value = value[:count]
            value = value.reshape(*self.shape[:-1], value.shape[-1])
            at = 0
            for scatter in (self, *self.others):
                wide = scatter.shape[-1]
                scatter.parts.append(value[..., at : at + wide])
                at += wide
        self.received, self.others = [], ()

    def result(self):
        while self.order:
            self.start()
            self.fold()
        return sum(part.astype(F32) for part in self.parts)


def after(values, *steps):
    moved = [piece for step in steps for piece in step.received]
    count = len(values)
    held = lax.optimization_barrier((*values, *moved))
    values, moved = held[:count], list(held[count:])
    for step in steps:
        count = len(step.received)
        step.received, moved = moved[:count], moved[count:]
        step.fold()
    return values


def key_masks(lens, length):
    middle = length // 2
    places = jnp.arange(length, dtype=jnp.int32)
    first, second = lens[:, :1], lens[:, 1:]
    single = places < first
    low = jnp.where(second > 0, single & (places < middle), single)
    high = jnp.where(second > 0, (places >= middle) & (places - middle < second), single)
    mask = jnp.where(jnp.stack([low, high], axis=1), 0.0, NEG)
    return jnp.pad(mask, ((0, 0), (0, 6), (0, 0)))


def body(
    sizes,
    tokens,
    cotangent,
    lengths,
    relevance,
    rel_table,
    w_query,
    w_key,
    w_value,
    w_output,
    w_inner,
    w_outer,
    bias_query,
    bias_value,
    bias_attn,
    bias_inner,
    bias_outer,
    gain_attn,
    shift_attn,
    gain_ffn,
    shift_ffn,
    rel_bias,
    w_score,
):
    query_size, cand_size = sizes
    devices = query_size * cand_size
    grid = Grid(query_size, cand_size)
    both = ("query", "cand")
    own_slot = lax.axis_index("cand")
    micros, length, width = tokens.shape[0], tokens.shape[3], tokens.shape[4]
    heads = rel_bias.shape[1]
    buckets = rel_bias.shape[0] * query_size
    pairs = heads // 2
    group_pairs = pairs // 3
    shard = w_query.shape[0]
    hidden = w_inner.shape[1]
    inner_shard = bias_inner.shape[0]
    spot = jnp.stack([*(grid.at[dim] for dim in ("outer", "inner", "far", "core")), own_slot])
    spot = spot.astype(jnp.int32)

    def own_part(value):
        rows = value.shape[0] // cand_size
        return lax.dynamic_slice_in_dim(value, own_slot * rows, rows, 0)

    def padded(row):
        row = row.reshape(1, -1)
        return jnp.pad(row, ((0, 0), (0, width - row.shape[1])))

    vectors = (
        bias_query, bias_value, bias_attn, bias_outer, gain_attn, shift_attn, gain_ffn, shift_ffn,
        w_score,
    )
    table = jnp.stack(vectors)
    table = jnp.concatenate(
        [
            jnp.pad(table, ((0, 0), (0, width - shard))),
            padded(bias_inner),
            padded(rel_bias),
            jnp.zeros((TABLE_ROWS - len(VECTORS) - 2, width), BF),
        ]
    )
    groups = (group_pairs, pairs - group_pairs)
    w_inner = lax.all_gather(own_part(w_inner), both, axis=0, tiled=True)
    w_outer = lax.all_gather(own_part(w_outer), both, axis=0, tiled=True)
    stepped = shard % 32 == 0 and width // grid.sizes["far"] == TRIO == PAIR * (pairs // 2)
    if stepped:
        half = shard // 2
        blocks = pack(spot, group_pairs, w_query, w_key, w_value, w_output, table)
        head = Gather(grid, blocks[0][None])
        head.start("outer")
        after((), head)
        (head,) = head.joined()
        block, head.pieces[0] = lax.optimization_barrier((blocks[1], head.pieces[0]))
        rest = Gather(grid, block[None])
        head.start("inner")
        rest.start("outer")
        after((), head, rest)
        head.start("core")
        near_part, far_part = rest.joined((0, half), (half, block.shape[0] - half))
        near_part.start("inner")
        far_part.start("far")
        after((), head)
        shapes = ((width, group_pairs * TRIO), (2 * query_size * TABLE_ROWS, width))
        first_weight, table = place_blocks(
            spot, shapes, (head, ((0, half, 0, 0), (1, TABLE_ROWS, 0, 0)))
        )
        table = table.reshape(query_size, 2, TABLE_ROWS, width)[:, 0]
    else:
        packed = jnp.stack(
            [value.reshape(shard, pairs, PAIR) for value in (w_query, w_key, w_value)], axis=2
        ).reshape(shard, pairs * TRIO)
        gather = partial(lax.all_gather, axis_name="query", axis=0, tiled=True)
        first_weight = gather(packed[:, : group_pairs * TRIO])
        second_weight = gather(packed[:, group_pairs * TRIO :])
        w_output = gather(w_output)
        table = gather(table).reshape(query_size, TABLE_ROWS, width)

    count = len(VECTORS)
    bias_inner = table[:, count, :inner_shard].reshape(1, hidden).astype(F32)
    rel_bias = table[:, count + 1, : rel_bias.size].reshape(buckets, heads)
    table = table[:, :count, :shard].transpose(1, 0, 2).reshape(count, width).astype(F32)
    bias_qkv = jnp.stack(
        [
            table[0].reshape(pairs, PAIR),
            jnp.zeros((pairs, PAIR), F32),
            table[1].reshape(pairs, PAIR),
        ],
        axis=1,
    ).reshape(1, pairs * TRIO)
    table = jnp.pad(table, ((0, TABLE_ROWS - count), (0, 0)))

    one_hot = (rel_table[:, None] == jnp.arange(buckets, dtype=jnp.int32)[None, :]).astype(BF)
    one_hot = jnp.pad(one_hot, ((1, 0), (0, 0)))
    dist = contract(rel_bias, one_hot, 0, 1).reshape(pairs, 2, 2 * length)
    dist = jnp.pad(dist, ((0, 0), (0, 6), (0, 0)))
    own_lens = lax.dynamic_index_in_dim(lengths[:, 0], own_slot, 1, keepdims=False)
    mask = key_masks(own_lens, length)

    inputs = tokens.reshape(micros * length, width)
    if stepped:
        first_weight, bias_qkv, dist = after((first_weight, bias_qkv, dist), near_part, far_part)
        (near_part,), (far_part,) = near_part.joined(), far_part.joined()
        near_part.start("far")
        far_part.start("inner")
    held = attn_fwd(inputs, first_weight, bias_qkv, dist, mask, 0, ())
    if stepped:
        held = after(held, near_part, far_part)
        near_part.start("core")
        far_part.start("core")
        held = after(held, near_part, far_part)
        second_weight, w_output = place_blocks(
            spot,
            ((width, groups[1] * TRIO), (width, width)),
            (near_part, ((0, half, 1, 0),)),
            (far_part, ((0, half, 1, 2), (1, half, 1, 0))),
        )
    qkv, context, probs = attn_fwd(
        inputs, second_weight, bias_qkv, dist, mask, group_pairs, held
    )
    normed_one, inv_one, low, act, slope = ffn_in(
        inputs, context, w_output, table, w_inner, bias_inner
    )
    normed_two, inv_two, hidden_out, scores = ffn_out(act, w_outer, normed_one, table, 2 * micros)

    all_scores = lax.all_gather(
        scores[:, 0, 0].reshape(micros, 1, 2), "cand", axis=1, tiled=True
    ).reshape(micros, 2 * cand_size)
    block_rows = width // devices
    by_far, by_inner = ("far", "inner", "outer"), ("inner", "far", "outer")
    tiles = hidden // width
    grad_two, grad_outer, sums_two, loss, keep, send = outer_bwd(
        spot,
        (hidden // devices, Scatter.spots(grid, by_far, tiles)),
        all_scores,
        lengths.reshape(micros, 2 * cand_size),
        relevance.reshape(micros, 2 * cand_size),
        cotangent.reshape(micros * length, width),
        normed_two,
        inv_two,
        hidden_out,
        table,
        act,
    )
    far_blocks = (block_rows, Scatter.spots(grid, by_far))
    inner_blocks = (block_rows, Scatter.spots(grid, by_inner))
    sum_outer = Scatter(grid, keep, send, by_far)
    grad_in, grad_bias_inner = after(act_bwd(grad_outer, slope, w_outer), sum_outer)
    sum_outer.start()
    grad_one, grad_attn, sums_one, keep, send = after(
        inner_bwd(
            spot, inner_blocks, grad_in, w_inner, low, grad_two, normed_one, inv_one, table, context
        ),
        sum_outer,
    )
    sum_inner = Scatter(grid, keep, send, by_inner)
    sum_outer.start()
    *early, grad_attn = after(
        (
            *attn_bwd(
                spot, far_blocks, qkv, context, grad_attn, probs, w_output, inputs, 0, group_pairs
            ),
            grad_attn,
        ),
        sum_outer,
        sum_inner,
    )
    grad_qkv, dist_grad, bias_grad, keep, send = early
    sum_early = Scatter(grid, keep, send, by_far)
    sum_inner.start()
    sum_outer.start()
    (grad_attn,) = after((grad_attn,), sum_early)
    sum_early.start()
    late = attn_bwd(
        spot, inner_blocks, qkv, context, grad_attn, probs, w_output, inputs, group_pairs,
        pairs - group_pairs,
    )
    others = (grad_qkv, dist_grad, bias_grad, grad_bias_inner, sums_one, sums_two, loss)
    late = after((*late, *others), sum_early, sum_outer, sum_inner)
    late_qkv, late_dist, late_bias, keep, send = late[:5]
    grad_qkv, dist_grad, bias_grad, grad_bias_inner, sums_one, sums_two, loss = late[5:]
    sum_late = Scatter(grid, keep, send, by_inner)
    sum_inner.start()
    sum_early.start()

    dist_grad = jnp.concatenate([dist_grad, late_dist])[:, :2].reshape(heads, 2 * length)
    grad_rel = lax.dot_general(
        dist_grad,
        one_hot.astype(F32),
        (((1,), (0,)), ((), ())),
        precision=lax.Precision.HIGHEST,
    )
    bias_grad = jnp.concatenate([bias_grad, late_bias])[:, 0].reshape(pairs, 3, PAIR)
    small = [
        sums_one[:3],
        sums_two[:4],
        bias_grad.transpose(1, 0, 2).reshape(3, width),
        grad_bias_inner.reshape(-1, width),
        jnp.pad(grad_rel, ((0, 0), (0, width - buckets))),
    ]
    rows = sum(value.shape[0] for value in small)
    fold = keep.shape[1] // width
    small.append(jnp.zeros((-rows % (8 * fold), width), F32))
    small = jnp.concatenate(small)
    rows = small.shape[0] // fold
    rider = jnp.concatenate([small[i * rows : (i + 1) * rows] for i in range(fold)], axis=1)
    grad_qkv, late_qkv, rider = after((grad_qkv, late_qkv, rider), sum_late)
    sum_late.start()
    rider = rider + grid.move(rider.astype(BF), "core", 1).astype(F32)
    other = grid.move(rider.astype(BF), "inner", 1)
    grad_inputs = grad_one + contract(grad_qkv, first_weight, 1, 1)
    grad_inputs = grad_inputs + contract(late_qkv, second_weight, 1, 1)
    grad_inputs, other = after((grad_inputs, other), sum_early, sum_inner)
    sum_inner.start()
    after((), sum_late)
    sum_late.rider = rider + other.astype(F32)
    sum_late.start()
    after((), sum_late)
    sum_late.start(sum_early)
    after((), sum_inner)
    after((), sum_late)
    own_late = sum_late.result()
    own_early = sum_early.result()
    own_outer = sum_outer.result()
    own_inner = sum_inner.result()
    own = jnp.concatenate([own_early, own_late], axis=1).reshape(block_rows, pairs, 3, PAIR)
    own_query, own_key, own_value = [own[:, :, i].reshape(-1, width) for i in range(3)]

    small = jnp.concatenate(
        [sum_late.rider[:, i * width : (i + 1) * width] for i in range(fold)], axis=0
    )
    index = lax.axis_index("query") * cand_size + own_slot
    small_own = lax.dynamic_slice_in_dim(small, index * block_rows, block_rows, 1)
    at = 10 + hidden // width
    flat = small[10:at].reshape(-1)
    own_bias_inner = lax.dynamic_slice_in_dim(flat, index * (hidden // devices), hidden // devices)
    rel_rows = buckets // devices
    own_rel = lax.dynamic_slice_in_dim(small[at : at + heads], index * rel_rows, rel_rows, 1)
    shape = (micros, 1, 1, length, width)
    return (
        hidden_out.reshape(shape),
        loss[:, :1],
        grad_inputs.reshape(shape),
        own_query,
        own_key,
        own_value,
        own_inner[:, hidden:],
        own_inner[:, :hidden],
        own_outer,
        small_own[7],
        small_own[9],
        small_own[2],
        own_bias_inner,
        small_own[5],
        small_own[0],
        small_own[1],
        small_own[3],
        small_own[4],
        own_rel.T,
        small_own[6],
    )


def solution(mesh):
    both = ("query", "cand")
    slots = P(None, "query", "cand", None, None)
    lists = P(None, "query", None, None)
    rows = P("query", None)
    vec_spec = P("query")
    return jax.shard_map(
        partial(body, (mesh.shape["query"], mesh.shape["cand"])),
        mesh=mesh,
        in_specs=(slots, slots, lists, lists, P()) + (rows,) * 6 + (vec_spec,) * 9 + (rows, vec_spec),
        out_specs=(slots, P(None, "query"), slots)
        + (P(both, None),) * 6
        + (P(both),) * 9
        + (P(both, None), P(both)),
        check_vma=False,
    )
```

```python
from functools import partial

import jax
import jax.numpy as jnp
import numpy as np
from jax import lax
from jax.experimental import pallas as pl
from jax.experimental.pallas import tpu as pltpu
from jax.sharding import PartitionSpec as P

HD = 64
PAIR = 2 * HD
TRIO = 3 * PAIR
TILE = 128
BF = jnp.bfloat16
F32 = jnp.float32
NEG = -1000000000.0
EPS = 1e-05

ERFC_P = 0.3
ERFC_C = (
    0.16919777981386785,
    0.17054619772689322,
    0.14956727662616615,
    0.21002273459109255,
    -0.08286335340540726,
    0.5302129644860679,
    -0.49655482906135956,
    0.4777385344298923,
    -0.12786727948795917,
)

VECTORS = (
    "bias_query",
    "bias_value",
    "bias_attn",
    "bias_outer",
    "gain_attn",
    "shift_attn",
    "gain_ffn",
    "shift_ffn",
    "w_score",
)
TABLE_ROWS = 16
ROW = {name: index for index, name in enumerate(VECTORS)}


def cost(micros=0.001):
    return pl.CostEstimate(flops=int(micros * 1.15e9), bytes_accessed=0, transcendentals=0)


def contract(left_mat, right_mat, left_dim, right_dim):
    return lax.dot_general(
        left_mat,
        right_mat,
        (((left_dim,), (right_dim,)), ((), ())),
        preferred_element_type=F32,
    )


def gelu_pair(u):
    size = jnp.abs(u)
    t = 1.0 / (1.0 + (ERFC_P * 0.5**0.5) * size)
    poly = jnp.full_like(u, 0.5 * ERFC_C[-1])
    for coef in ERFC_C[-2::-1]:
        poly = poly * t + 0.5 * coef
    bell = jnp.exp(-0.5 * (u * u))
    tail = poly * t * bell
    cdf = jnp.where(u < 0, tail, 1.0 - tail)
    return u * cdf, cdf + u * ((2.0 * np.pi) ** -0.5 * bell)


def normalise(values):
    centred = values - jnp.mean(values, axis=-1, keepdims=True)
    inv_std = lax.rsqrt(jnp.mean(centred * centred, axis=-1, keepdims=True) + EPS)
    return centred * inv_std, inv_std


def norm_backward(grad_out, normed, inv_std, gain_vec):
    grad_normed = grad_out * gain_vec
    return inv_std * (
        grad_normed
        - jnp.mean(grad_normed, axis=-1, keepdims=True)
        - normed * jnp.mean(grad_normed * normed, axis=-1, keepdims=True)
    )


def row_chunks(rows, size, step):
    size = min(size, rows)

    @pl.loop(0, rows // size)
    def _(index):
        step(pl.ds(pl.multiple_of(index * size, size), size))


def split_rows(core, tile, rows, spots, keep, send):
    for block, spot in enumerate(spots):
        place = slice(spot * rows, (spot + 1) * rows)
        if rows % 8 == 0:
            own = pl.multiple_of((2 * block + core) * rows, 8)
            other = pl.multiple_of((2 * block + 1 - core) * rows, 8)
            keep[place, :] = tile[pl.ds(own, rows), :].astype(keep.dtype)
            send[place, :] = tile[pl.ds(other, rows), :].astype(send.dtype)
        else:
            even = tile[2 * block * rows : (2 * block + 1) * rows, :]
            odd = tile[(2 * block + 1) * rows : (2 * block + 2) * rows, :]
            keep[place, :] = jnp.where(core == 0, even, odd).astype(keep.dtype)
            send[place, :] = jnp.where(core == 0, odd, even).astype(send.dtype)


def attn_fwd_kernel(x_ref, w_ref, b_ref, dist_ref, mask_ref, *refs):
    qkv_ref, ctx_ref, p_ref, table = refs[-4:]
    length = x_ref.shape[0]
    width = 2 * length

    @pl.when(pl.program_id(1) == 0)
    def _():
        for head in range(2):
            row = jnp.broadcast_to(dist_ref[0, head : head + 1, :], (TILE, width))
            table[head] = pltpu.roll(row, 0, 1, stride=1, stride_axis=0)

    qkv = (contract(x_ref[...], w_ref[...], 1, 0) + b_ref[...]).astype(BF)
    qkv_ref[...] = qkv
    q = qkv[:, :PAIR] * jnp.asarray(HD**-0.5, BF)
    k = qkv[:, PAIR : 2 * PAIR]
    v = qkv[:, 2 * PAIR :]
    lane = lax.broadcasted_iota(jnp.int32, (length, PAIR), 1)
    raws = []
    for head in range(2):
        own = (lane < HD) == (head == 0)
        raws.append(contract(jnp.where(own, q, jnp.zeros_like(q)), k, 1, 1))
    outs = []
    for head in range(2):
        for start in range(0, length, TILE):
            half = start // (length // 2)
            logits = (
                raws[head][start : start + TILE]
                + table[head, :, length - start : width - start]
                + mask_ref[0, half : half + 1, :]
            )
            peak = jnp.max(logits, axis=1, keepdims=True)
            grown = jnp.exp(logits - peak)
            total = jnp.sum(grown, axis=1, keepdims=True)
            p_ref[0, head, start : start + TILE, :] = (grown * (1.0 / total)).astype(BF)
        outs.append(contract(p_ref[0, head], v, 1, 0))
    ctx_ref[...] = jnp.where(lane < HD, outs[0], outs[1]).astype(BF)


def attn_fwd(inputs, weight, bias, dist, mask, first, held):
    rows, width = inputs.shape
    micros = mask.shape[0]
    length = rows // micros
    pairs = weight.shape[1] // TRIO
    every = bias.shape[1] // TRIO
    return pl.pallas_call(
        attn_fwd_kernel,
        grid=(pairs, micros),
        in_specs=[
            pl.BlockSpec((length, width), lambda h, m: (m, 0)),
            pl.BlockSpec((width, TRIO), lambda h, m: (0, h)),
            pl.BlockSpec((1, TRIO), lambda h, m: (0, h + first)),
            pl.BlockSpec((1, 8, 2 * length), lambda h, m: (h + first, 0, 0)),
            pl.BlockSpec((1, 8, length), lambda h, m: (m, 0, 0)),
        ]
        + [pl.BlockSpec(memory_space=pl.ANY)] * len(held),
        out_specs=[
            pl.BlockSpec((length, TRIO), lambda h, m: (m, h + first)),
            pl.BlockSpec((length, PAIR), lambda h, m: (m, h + first)),
            pl.BlockSpec((1, 2, length, length), lambda h, m: (m, h + first, 0, 0)),
        ],
        out_shape=[
            jax.ShapeDtypeStruct((rows, every * TRIO), BF),
            jax.ShapeDtypeStruct((rows, every * PAIR), BF),
            jax.ShapeDtypeStruct((micros, 2 * every, length, length), BF),
        ],
        input_output_aliases={5 + index: index for index in range(len(held))},
        scratch_shapes=[pltpu.VMEM((2, TILE, 2 * length), F32)],
        compiler_params=pltpu.CompilerParams(vmem_limit_bytes=62 << 20),
        cost_estimate=cost(),
        name="attn_fwd",
    )(inputs, weight, bias, dist, mask, *held)


def attn_bwd_kernel(
    blocks, place_ref, qkv_ref, o_ref, dr_ref, p_ref, wo_ref, x_ref, *refs
):
    dqkv_ref, gd_ref, db_ref, keep_ref, send_ref, acc, dsb, dw, kept, sent = refs[-10:]
    length = qkv_ref.shape[0]
    width = 2 * length
    first = pl.program_id(1) == 0
    last = pl.program_id(1) == pl.num_programs(1) - 1

    @pl.when(first)
    def _():
        acc[...] = jnp.zeros_like(acc)
        dw[...] = jnp.zeros_like(dw)
        db_ref[...] = jnp.zeros_like(db_ref)

    q = qkv_ref[:, :PAIR]
    k = qkv_ref[:, PAIR : 2 * PAIR]
    v = qkv_ref[:, 2 * PAIR :]
    do = contract(dr_ref[...], wo_ref[...], 1, 1).astype(BF)
    lane = lax.broadcasted_iota(jnp.int32, (length, PAIR), 1)
    prod = do.astype(F32) * o_ref[...].astype(F32)
    dq, dk, dv, inners, dps = [], [], [], [], []
    for head in range(2):
        own = (lane < HD) == (head == 0)
        inners.append(jnp.sum(jnp.where(own, prod, 0.0), axis=1, keepdims=True))
        dps.append(contract(jnp.where(own, do, jnp.zeros_like(do)), v, 1, 1))
        dv.append(contract(p_ref[0, head], do, 0, 0))
    for head in range(2):
        inner, dp = inners[head], dps[head]
        for start in range(0, length, TILE):
            rows = slice(start, start + TILE)
            ds = p_ref[0, head, rows, :].astype(F32) * (dp[rows] - inner[rows])
            acc[head, :, length - start : width - start] += ds
            dsb[head, rows, :] = (ds * HD**-0.5).astype(BF)
        dq.append(contract(dsb[head], k, 1, 0))
        dk.append(contract(dsb[head], q, 0, 0))
    for index, (low, high) in enumerate((dq, dk, dv)):
        cols = slice(index * PAIR, (index + 1) * PAIR)
        grad = jnp.where(lane < HD, low, high).astype(BF)
        dqkv_ref[:, cols] = grad
        db_ref[0, 0:1, cols] += jnp.sum(grad.astype(F32), axis=0, keepdims=True)
    dw[...] += contract(x_ref[...], dqkv_ref[...], 0, 0)

    @pl.when(last)
    def _():
        split_rows(place_ref[3], dw, *blocks, kept, sent)
        keep_ref[...] = kept[...].astype(BF)
        send_ref[...] = sent[...].astype(BF)
        for head in range(2):
            total = acc[head, 0:8, :]
            for start in range(8, TILE, 8):
                total = total + pltpu.roll(acc[head, start : start + 8, :], width - start, 1)
            row = total[0:1, :]
            for step in range(1, 8):
                row = row + pltpu.roll(total[step : step + 1, :], width - step, 1)
            gd_ref[0, head : head + 1, :] = row


def attn_bwd(
    place, blocks, qkv, ctx, d_r, probs, w_output, inputs, first, pairs, held=(), start=0, every=None
):
    rows, width = inputs.shape
    micros, _, length, _ = probs.shape
    at = lambda shape, place: pl.BlockSpec(shape, lambda h, m, c: place(h, m))
    half = width // 2
    every = every or pairs
    return pl.pallas_call(
        partial(attn_bwd_kernel, blocks),
        grid_spec=pltpu.PrefetchScalarGridSpec(
            num_scalar_prefetch=1,
            grid=(pairs, micros),
            in_specs=[
                at((length, TRIO), lambda h, m: (m, h + first)),
                at((length, PAIR), lambda h, m: (m, h + first)),
                at((length, width), lambda h, m: (m, 0)),
                at((1, 2, length, length), lambda h, m: (m, h + first, 0, 0)),
                at((PAIR, width), lambda h, m: (h + first, 0)),
                at((length, width), lambda h, m: (m, 0)),
            ]
            + [pl.BlockSpec(memory_space=pl.ANY)] * len(held),
            out_specs=[
                at((length, TRIO), lambda h, m: (m, h + start)),
                at((1, 8, 2 * length), lambda h, m: (h + start, 0, 0)),
                at((1, 8, TRIO), lambda h, m: (h + start, 0, 0)),
                at((half, TRIO), lambda h, m: (0, h + start)),
                at((half, TRIO), lambda h, m: (0, h + start)),
            ],
            scratch_shapes=[
                pltpu.VMEM((2, TILE, 2 * length), F32),
                pltpu.VMEM((2, length, length), BF),
                pltpu.VMEM((width, TRIO), F32),
                pltpu.VMEM((half, TRIO), F32),
                pltpu.VMEM((half, TRIO), F32),
            ],
        ),
        out_shape=[
            jax.ShapeDtypeStruct((rows, every * TRIO), BF),
            jax.ShapeDtypeStruct((every, 8, 2 * length), F32),
            jax.ShapeDtypeStruct((every, 8, TRIO), F32),
            jax.ShapeDtypeStruct((half, every * TRIO), BF),
            jax.ShapeDtypeStruct((half, every * TRIO), BF),
        ],
        input_output_aliases={7 + index: index for index in range(len(held))},
        compiler_params=pltpu.CompilerParams(vmem_limit_bytes=62 << 20),
        cost_estimate=cost(),
        name="attn_bwd",
    )(place, qkv, ctx, d_r, probs, w_output, inputs, *held)


def vec(ref, name):
    return ref[ROW[name] : ROW[name] + 1, :]


def ffn_in_kernel(
    x_ref, ctx_ref, wo_ref, vec_ref, w_ref, b_ref, n1_ref, i1_ref, low_ref, act_ref, slope_ref
):
    rows = x_ref.shape[0]

    @pl.when(pl.program_id(0) == 0)
    def _():
        size = min(256, rows)
        for start in range(0, rows, size):
            at = slice(start, start + size)
            attn = contract(ctx_ref[at, :], wo_ref[...], 1, 0) + vec(vec_ref, "bias_attn")
            normed, inv_std = normalise(x_ref[at, :].astype(F32) + attn)
            n1_ref[at, :] = normed
            i1_ref[at, :] = inv_std
            first = normed * vec(vec_ref, "gain_attn") + vec(vec_ref, "shift_attn")
            low_ref[at, :] = first.astype(BF)

    def step(at):
        u = contract(low_ref[at, :], w_ref[...], 1, 0) + b_ref[...]
        act, slope = gelu_pair(u)
        act_ref[at, :] = act.astype(BF)
        slope_ref[at, :] = slope.astype(BF)

    row_chunks(rows, 256, step)


def ffn_in(inputs, context, w_output, vectors, w_inner, bias):
    rows, width = inputs.shape
    hidden = w_inner.shape[1]
    size = min(512, hidden)
    whole = pl.BlockSpec((rows, width), lambda n: (0, 0))
    column = pl.BlockSpec((rows, 1), lambda n: (0, 0))
    cols = pl.BlockSpec((rows, size), lambda n: (0, n))
    out = jax.ShapeDtypeStruct((rows, hidden), BF)
    return pl.pallas_call(
        ffn_in_kernel,
        grid=(hidden // size,),
        in_specs=[
            whole,
            whole,
            pl.BlockSpec((width, width), lambda n: (0, 0)),
            pl.BlockSpec((TABLE_ROWS, width), lambda n: (0, 0)),
            pl.BlockSpec((width, size), lambda n: (0, n)),
            pl.BlockSpec((1, size), lambda n: (0, n)),
        ],
        out_specs=[whole, column, whole, cols, cols],
        out_shape=[
            jax.ShapeDtypeStruct((rows, width), F32),
            jax.ShapeDtypeStruct((rows, 1), F32),
            jax.ShapeDtypeStruct((rows, width), BF),
            out,
            out,
        ],
        compiler_params=pltpu.CompilerParams(vmem_limit_bytes=62 << 20),
        cost_estimate=cost(),
        name="ffn_in",
    )(inputs, context, w_output, vectors, w_inner, bias)


def ffn_out_kernel(act_ref, w_ref, n1_ref, vec_ref, n2_ref, i2_ref, hid_ref, score_ref):
    first = n1_ref[...] * vec(vec_ref, "gain_attn") + vec(vec_ref, "shift_attn")
    outer = contract(act_ref[...], w_ref[...], 1, 0) + vec(vec_ref, "bias_outer")
    normed, inv_std = normalise(first + outer)
    n2_ref[...] = normed
    i2_ref[...] = inv_std
    low = (normed * vec(vec_ref, "gain_ffn") + vec(vec_ref, "shift_ffn")).astype(BF)
    hid_ref[...] = low
    row = low[0:8, :].astype(F32)[0:1, :] * vec(vec_ref, "w_score")
    score_ref[0] = jnp.broadcast_to(jnp.sum(row, axis=1, keepdims=True), score_ref.shape[1:])


def ffn_out(act, w_outer, normed, vectors, count):
    rows, hidden = act.shape
    width = w_outer.shape[1]
    size = rows // count
    block = pl.BlockSpec((size, width), lambda r: (r, 0))
    return pl.pallas_call(
        ffn_out_kernel,
        grid=(count,),
        in_specs=[
            pl.BlockSpec((size, hidden), lambda r: (r, 0)),
            pl.BlockSpec((hidden, width), lambda r: (0, 0)),
            block,
            pl.BlockSpec((TABLE_ROWS, width), lambda r: (0, 0)),
        ],
        out_specs=[
            block,
            pl.BlockSpec((size, 1), lambda r: (r, 0)),
            block,
            pl.BlockSpec((1, 8, 128), lambda r: (r, 0, 0)),
        ],
        out_shape=[
            jax.ShapeDtypeStruct((rows, width), F32),
            jax.ShapeDtypeStruct((rows, 1), F32),
            jax.ShapeDtypeStruct((rows, width), BF),
            jax.ShapeDtypeStruct((count, 8, 128), F32),
        ],
        compiler_params=pltpu.CompilerParams(vmem_limit_bytes=62 << 20),
        cost_estimate=cost(),
        name="ffn_out",
    )(act, w_outer, normed, vectors)


def list_loss(scores, lens, relevance):
    present = lens > 0
    masked = jnp.where(present, scores, NEG)
    peak = jnp.max(masked, axis=1, keepdims=True)
    log_total = peak + jnp.log(jnp.sum(jnp.exp(masked - peak), axis=1, keepdims=True))
    log_prob = masked - log_total
    rel = jnp.where(present, relevance, NEG)
    rel_exp = jnp.exp(rel - jnp.max(rel, axis=1, keepdims=True))
    target = rel_exp / jnp.sum(rel_exp, axis=1, keepdims=True)
    loss = -jnp.sum(jnp.where(present, target * log_prob, 0.0), axis=1, keepdims=True)
    return loss, jnp.where(present, jnp.exp(log_prob) - target, 0.0)


def outer_bwd_kernel(
    blocks, place_ref, score_ref, len_ref, rel_ref, cot_ref, n2_ref, i2_ref, hid_ref, vec_ref,
    act_ref, dr_ref, low, sum_ref, loss_ref, keep_ref, send_ref, tile, kept, sent,
):
    rows, width = cot_ref.shape

    @pl.when(pl.program_id(0) == 0)
    def _():
        loss, grad = list_loss(score_ref[...], len_ref[...], rel_ref[...])
        loss_ref[...] = jnp.broadcast_to(loss, loss_ref.shape)
        lane = lax.broadcasted_iota(jnp.int32, grad.shape, 1)
        micros = grad.shape[0]
        sum_ref[...] = jnp.zeros_like(sum_ref)
        firsts = {}
        for half in range(2):
            own = jnp.where(lane == 2 * place_ref[4] + half, grad, 0.0)
            own = jnp.sum(own, axis=1, keepdims=True)
            for micro in range(micros):
                firsts[(2 * micro + half) * (rows // (2 * micros))] = own[micro : micro + 1, :]
        score_row = vec(vec_ref, "w_score")
        gain = vec(vec_ref, "gain_ffn")

        def step(at):
            grad_out = cot_ref[at, :].astype(F32)
            place = lax.broadcasted_iota(jnp.int32, (grad_out.shape[0], 1), 0) + at.start
            shift = jnp.zeros_like(place, F32)
            for first, value in firsts.items():
                shift = jnp.where(place == first, value, shift)
            grad_out = grad_out + shift * score_row
            normed = n2_ref[at, :]
            grad_in = norm_backward(grad_out, normed, i2_ref[at, :], gain)
            dr_ref[at, :] = grad_in
            grad_low = grad_in.astype(BF)
            low[at, :] = grad_low
            sum_ref[0:1, :] += jnp.sum(grad_out * normed, axis=0, keepdims=True)
            sum_ref[1:2, :] += jnp.sum(grad_out, axis=0, keepdims=True)
            sum_ref[2:3, :] += jnp.sum(grad_low.astype(F32), axis=0, keepdims=True)

        row_chunks(rows, 128, step)
        total = jnp.zeros((1, width), F32)
        for first, value in firsts.items():
            total = total + value * hid_ref[first : first + 8, :].astype(F32)[0:1, :]
        sum_ref[3:4, :] = total

    tile[...] = contract(act_ref[...], low[...], 0, 0)
    split_rows(place_ref[3], tile, *blocks, kept, sent)
    keep_ref[...] = kept[...].astype(BF).reshape(keep_ref.shape)
    send_ref[...] = sent[...].astype(BF).reshape(send_ref.shape)


def outer_bwd(
    place, blocks, scores, lens, relevance, cot, normed, inv_std, hid, vectors, act
):
    rows, width = cot.shape
    hidden = act.shape[1]
    size = width
    at = lambda shape, index: pl.BlockSpec(shape, lambda n, c: index(n))
    whole = at((rows, width), lambda n: (0, 0))
    tiny = at(scores.shape, lambda n: (0, 0))
    rows_of, spots = blocks
    tiles = hidden // size
    half = at((len(spots), 1, rows_of, width), lambda n: (0, n, 0, 0))
    return pl.pallas_call(
        partial(outer_bwd_kernel, blocks),
        grid_spec=pltpu.PrefetchScalarGridSpec(
            num_scalar_prefetch=1,
            grid=(hidden // size,),
            in_specs=[
                tiny, tiny, tiny, whole, whole, at((rows, 1), lambda n: (0, 0)), whole,
                at((TABLE_ROWS, width), lambda n: (0, 0)), at((rows, size), lambda n: (0, n)),
            ],
            out_specs=[
                whole, whole, at((8, width), lambda n: (0, 0)),
                at((scores.shape[0], 128), lambda n: (0, 0)), half, half,
            ],
            scratch_shapes=[
                pltpu.VMEM((size, width), F32),
                pltpu.VMEM((size // 2, width), F32),
                pltpu.VMEM((size // 2, width), F32),
            ],
        ),
        out_shape=[
            jax.ShapeDtypeStruct((rows, width), F32),
            jax.ShapeDtypeStruct((rows, width), BF),
            jax.ShapeDtypeStruct((8, width), F32),
            jax.ShapeDtypeStruct((scores.shape[0], 128), F32),
            jax.ShapeDtypeStruct((len(spots), tiles, rows_of, width), BF),
            jax.ShapeDtypeStruct((len(spots), tiles, rows_of, width), BF),
        ],
        compiler_params=pltpu.CompilerParams(vmem_limit_bytes=62 << 20),
        cost_estimate=cost(),
        name="outer_bwd",
    )(place, scores, lens, relevance, cot, normed, inv_std, hid, vectors, act)


def act_bwd_kernel(dr_ref, slope_ref, w2_ref, din_ref, db_ref):
    grad = dr_ref[...]
    wide = w2_ref.shape[0]
    size = min(256, wide)
    for start in range(0, wide, size):
        cols = slice(start, start + size)
        d_act = contract(grad, w2_ref[cols, :], 1, 1)
        d_in = (d_act * slope_ref[:, cols].astype(F32)).astype(BF)
        din_ref[:, cols] = d_in
        db_ref[:, cols] = jnp.sum(d_in.astype(F32), axis=0, keepdims=True)


def act_bwd(grad, slope, w_outer):
    rows, hidden = slope.shape
    width = grad.shape[1]
    size = min(512, hidden)
    cols = pl.BlockSpec((rows, size), lambda n: (0, n))
    return pl.pallas_call(
        act_bwd_kernel,
        grid=(hidden // size,),
        in_specs=[
            pl.BlockSpec((rows, width), lambda n: (0, 0)),
            cols,
            pl.BlockSpec((size, width), lambda n: (n, 0)),
        ],
        out_specs=[cols, pl.BlockSpec((1, size), lambda n: (0, n))],
        out_shape=[
            jax.ShapeDtypeStruct((rows, hidden), BF),
            jax.ShapeDtypeStruct((1, hidden), F32),
        ],
        compiler_params=pltpu.CompilerParams(vmem_limit_bytes=62 << 20),
        cost_estimate=cost(),
        name="act_bwd",
    )(grad, slope, w_outer)


def inner_bwd_kernel(
    blocks, place_ref, din_ref, w1_ref, low_ref, dr_ref, n1_ref, i1_ref, vec_ref, ctx_ref,
    one_ref, grad_ref, sum_ref, keep_ref, send_ref, acc, tile, kept, sent,
):
    step_id = pl.program_id(0)
    last = pl.num_programs(0) - 1
    rows = low_ref.shape[0]

    @pl.when(step_id < last)
    def _():
        d_in = din_ref[...]
        tile[...] = contract(low_ref[...], d_in, 0, 0)
        part = contract(d_in, w1_ref[...], 1, 1)

        @pl.when(step_id == 0)
        def _():
            acc[...] = dr_ref[...] + part

        @pl.when(step_id > 0)
        def _():
            acc[...] += part

    @pl.when(step_id == last)
    def _():
        sum_ref[...] = jnp.zeros_like(sum_ref)
        gain = vec(vec_ref, "gain_attn")

        def step(at):
            grad_out = acc[at, :]
            normed = n1_ref[at, :]
            grad_in = norm_backward(grad_out, normed, i1_ref[at, :], gain)
            one_ref[at, :] = grad_in
            grad_low = grad_in.astype(BF)
            grad_ref[at, :] = grad_low
            sum_ref[0:1, :] += jnp.sum(grad_out * normed, axis=0, keepdims=True)
            sum_ref[1:2, :] += jnp.sum(grad_out, axis=0, keepdims=True)
            sum_ref[2:3, :] += jnp.sum(grad_low.astype(F32), axis=0, keepdims=True)

        row_chunks(rows, 128, step)
        tile[...] = contract(ctx_ref[...], grad_ref[...], 0, 0)

    split_rows(place_ref[3], tile, *blocks, kept, sent)
    keep_ref[...] = kept[...].astype(BF)
    send_ref[...] = sent[...].astype(BF)


def inner_bwd(place, blocks, d_in, w_inner, low, d_r, normed, inv_std, vectors, context):
    rows, width = low.shape
    hidden = d_in.shape[1]
    size = width
    tiles = hidden // size
    at = lambda shape, index: pl.BlockSpec(shape, lambda n, c: index(n))
    whole = at((rows, width), lambda n: (0, 0))
    near = lambda n: (0, jnp.minimum(n, tiles - 1))
    half = at((width // 2, size), lambda n: (0, n))
    return pl.pallas_call(
        partial(inner_bwd_kernel, blocks),
        grid_spec=pltpu.PrefetchScalarGridSpec(
            num_scalar_prefetch=1,
            grid=(tiles + 1,),
            in_specs=[
                at((rows, size), near), at((width, size), near), whole, whole, whole,
                at((rows, 1), lambda n: (0, 0)), at((TABLE_ROWS, width), lambda n: (0, 0)), whole,
            ],
            out_specs=[whole, whole, at((8, width), lambda n: (0, 0)), half, half],
            scratch_shapes=[
                pltpu.VMEM((rows, width), F32),
                pltpu.VMEM((width, size), F32),
                pltpu.VMEM((width // 2, size), F32),
                pltpu.VMEM((width // 2, size), F32),
            ],
        ),
        out_shape=[
            jax.ShapeDtypeStruct((rows, width), F32),
            jax.ShapeDtypeStruct((rows, width), BF),
            jax.ShapeDtypeStruct((8, width), F32),
            jax.ShapeDtypeStruct((width // 2, hidden + width), BF),
            jax.ShapeDtypeStruct((width // 2, hidden + width), BF),
        ],
        compiler_params=pltpu.CompilerParams(vmem_limit_bytes=62 << 20),
        cost_estimate=cost(),
        name="inner_bwd",
    )(place, d_in, w_inner, low, d_r, normed, inv_std, vectors, context)


def shifted(axis_size, group, stride, step):
    pairs = []
    for source in range(axis_size):
        place = source // stride % group
        pairs.append((source, source + ((place + step) % group - place) * stride))
    return pairs


class Grid:
    def __init__(self, query_size, cand_size):
        query, cand = lax.axis_index("query"), lax.axis_index("cand")
        self.sizes = {"outer": query_size // 2, "inner": 2, "far": cand_size // 2, "core": 2}
        self.lengths = {"query": query_size, "cand": cand_size}
        self.axes = {
            "outer": ("query", 2),
            "inner": ("query", 1),
            "far": ("cand", 2),
            "core": ("cand", 1),
        }
        self.at = {
            "outer": query // 2,
            "inner": query % 2,
            "far": cand // 2,
            "core": cand % 2,
        }

    def move(self, value, dim, step):
        axis, stride = self.axes[dim]
        return lax.ppermute(
            value, axis, shifted(self.lengths[axis], self.sizes[dim], stride, step)
        )


def pack_kernel(pairs, place_ref, wq, wk, wv, wo, table, first, middle):
    far, core = place_ref[2], place_ref[3]
    half = wq.shape[0] // 2
    rows = pl.ds(pl.multiple_of(core * half, 16), half)
    for pair in range(pairs):
        for index, weight in enumerate((wq, wk, wv)):
            to = (pair * 3 + index) * PAIR
            first[:half, to : to + PAIR] = weight[rows, pair * PAIR : (pair + 1) * PAIR]
    first[half:, :] = table[...]
    count = wq.shape[1] // PAIR // pairs - 1
    for run in range(count):
        cols = pl.ds(pl.multiple_of(((run + 1) * pairs + far) * PAIR, PAIR), PAIR)
        for index, weight in enumerate((wq, wk, wv)):
            middle[run * half : (run + 1) * half, index * PAIR : (index + 1) * PAIR] = weight[rows, cols]
    wide = wo.shape[1] // 2
    cols = pl.ds(pl.multiple_of(far * wide, PAIR), wide)
    middle[count * half :, :] = wo[rows, cols]


def pack(place, pairs, wq, wk, wv, wo, table):
    shard, width = wq.shape
    half = shard // 2
    count = width // PAIR // pairs
    shapes = [
        (half + TABLE_ROWS, pairs * TRIO),
        (count * half, width // 2),
    ]
    return pl.pallas_call(
        partial(pack_kernel, pairs),
        grid_spec=pltpu.PrefetchScalarGridSpec(
            num_scalar_prefetch=1,
            grid=(1,),
            in_specs=[
                pl.BlockSpec(value.shape, lambda i, c: (0, 0)) for value in (wq, wk, wv, wo, table)
            ],
            out_specs=[pl.BlockSpec(shape, lambda i, c: (0, 0)) for shape in shapes],
        ),
        out_shape=[jax.ShapeDtypeStruct(shape, BF) for shape in shapes],
        compiler_params=pltpu.CompilerParams(vmem_limit_bytes=60 << 20),
        cost_estimate=cost(),
        name="pack",
    )(place, wq, wk, wv, wo, table)


def join_kernel(runs, count, *refs):
    sources, targets = refs[:count], refs[count:]
    at = 0
    for source in sources:
        size = source.shape[0]
        for target, (first, rows) in zip(targets, runs):
            target[at : at + size] = source[:, first : first + rows, :]
        at += size


def join(pieces, runs):
    total = sum(piece.shape[0] for piece in pieces)
    wide = pieces[0].shape[2]
    whole = lambda shape: pl.BlockSpec(shape, lambda i: (0, 0, 0))
    shapes = [(total, rows, wide) for _, rows in runs]
    return pl.pallas_call(
        partial(join_kernel, runs, len(pieces)),
        grid=(1,),
        in_specs=[whole(piece.shape) for piece in pieces],
        out_specs=[whole(shape) for shape in shapes],
        out_shape=[jax.ShapeDtypeStruct(shape, BF) for shape in shapes],
        compiler_params=pltpu.CompilerParams(vmem_limit_bytes=62 << 20),
        cost_estimate=cost(),
        name="join",
    )(*pieces)


class Gather:
    def __init__(self, grid, blocks, places=None):
        self.grid = grid
        self.pieces = [blocks]
        self.places = [places or [{"outer": 0, "inner": 0, "far": 0, "core": 0}]]
        self.received = []

    def joined(self, *runs):
        places = sum(self.places, [])
        runs = runs or ((0, self.pieces[0].shape[1]),)
        return [Gather(self.grid, piece, places) for piece in join(self.pieces, runs)]

    def start(self, dim):
        size = self.grid.sizes[dim]
        self.coming = []
        for piece, places in zip(self.pieces, self.places):
            for step in range(1, size):
                self.received.append(self.grid.move(piece, dim, step))
                self.coming.append(
                    [{**place, dim: (place[dim] + step) % size} for place in places]
                )

    def fold(self):
        self.pieces = self.pieces + self.received
        self.places = self.places + self.coming
        self.received = []


def place_kernel(splits, places, outer, spot_ref, *refs):
    count = 1 + max(run[0] for split in splits for run in split)
    sources, targets, sems = refs[: -1 - count], refs[-1 - count : -1], refs[-1]
    copies = []
    at = 0
    for source, split in zip(sources, splits):
        wide = source.shape[-1]
        for index in range(source.shape[0]):
            place = places[at]
            zed = lax.rem(spot_ref[0] + (outer - place["outer"]), outer)
            other = {
                dim: lax.rem(spot_ref[i] + place[dim], 2)
                for i, dim in enumerate(("inner", "far", "core"), 1)
            }
            block = (zed * 2 + other["inner"]) * 2 + other["core"]
            first = 0
            for target, rows, stride, offset in split:
                cols = slice(None)
                if stride:
                    col = other["far"] * (stride * wide) + offset * wide
                    cols = pl.ds(pl.multiple_of(col, 128), wide)
                copies.append(
                    pltpu.make_async_copy(
                        source.at[index, pl.ds(first, rows), :],
                        targets[target].at[pl.ds(pl.multiple_of(block * rows, 16), rows), cols],
                        sems.at[len(copies)],
                    )
                )
                first += rows
            at += 1
    for copy in copies:
        copy.start()
    for copy in copies:
        copy.wait()


def place_blocks(spot, shapes, *gathers):
    places, pieces, splits, copies = [], [], [], 0
    for gather, split in gathers:
        for piece, found in zip(gather.pieces, gather.places):
            pieces.append(piece)
            splits.append(split)
            places += found
            copies += len(found) * len(split)
    return pl.pallas_call(
        partial(place_kernel, splits, places, gather.grid.sizes["outer"]),
        grid_spec=pltpu.PrefetchScalarGridSpec(
            num_scalar_prefetch=1,
            grid=(1,),
            in_specs=[pl.BlockSpec(memory_space=pl.ANY)] * len(pieces),
            out_specs=[pl.BlockSpec(memory_space=pltpu.VMEM)] * len(shapes),
            scratch_shapes=[pltpu.SemaphoreType.DMA((copies,))],
        ),
        out_shape=[jax.ShapeDtypeStruct(shape, BF) for shape in shapes],
        compiler_params=pltpu.CompilerParams(vmem_limit_bytes=24 << 20),
        cost_estimate=cost(),
        name="place_blocks",
    )(spot, *pieces)


class Scatter:
    def __init__(self, grid, keep, send, order):
        self.grid = grid
        self.dims = list(order)
        self.order = list(order)
        self.sizes = [grid.sizes[dim] for dim in self.dims]
        self.rider, self.others = None, ()
        self.parts = [self.blocks(keep)]
        self.shape = self.blocks(send).shape
        self.received = [grid.move(send, "core", 1)]

    def blocks(self, value):
        return value.reshape(*self.sizes, -1, value.shape[-1])

    @staticmethod
    def spots(grid, order, tiles=1):
        sizes = {dim: grid.sizes[dim] for dim in order}
        if tiles > 1:
            sizes["outer"] //= tiles
        spots = []
        for block in range(int(np.prod(list(sizes.values())))):
            at = {
                "outer": block // (2 * sizes["far"]),
                "inner": block // sizes["far"] % 2,
                "far": block % sizes["far"],
            }
            spot = 0
            for dim in order:
                spot = spot * sizes[dim] + at[dim]
            spots.append(spot)
        return tuple(spots)

    def step(self, dim):
        axis = self.dims.index(dim)
        size, here = self.grid.sizes[dim], self.grid.at[dim]
        sent = []
        for step in range(1, size):
            total = 0.0
            for part in self.parts:
                piece = lax.dynamic_index_in_dim(part, (here + step) % size, axis, keepdims=False)
                total += piece.astype(F32)
            sent.append(total.astype(BF))
        self.parts = [
            lax.dynamic_index_in_dim(part, here, axis, keepdims=False) for part in self.parts
        ]
        self.dims.remove(dim)
        return sent

    def start(self, *others):
        dim = self.order.pop(0)
        sent = self.step(dim)
        self.others = others
        self.shape = sent[0].shape
        for other in others:
            other.order.remove(dim)
            more = other.step(dim)
            other.shape = more[0].shape
            sent = [jnp.concatenate(pair, axis=-1) for pair in zip(sent, more)]
        if self.rider is not None:
            wide = sent[0].shape[-1]
            rider = jnp.pad(self.rider, ((0, 0), (0, wide - self.rider.shape[1]))).astype(BF)
            sent = [jnp.concatenate([value.reshape(-1, wide), rider]) for value in sent]
        self.received = [self.grid.move(value, dim, step) for step, value in enumerate(sent, 1)]

    def fold(self):
        for value in self.received:
            if self.rider is not None:
                count = value.shape[0] - self.rider.shape[0]
                self.rider = self.rider + value[count:, : self.rider.shape[1]].astype(F32)
                value = value[:count]
            value = value.reshape(*self.shape[:-1], value.shape[-1])
            at = 0
            for scatter in (self, *self.others):
                wide = scatter.shape[-1]
                scatter.parts.append(value[..., at : at + wide])
                at += wide
        self.received, self.others = [], ()

    def result(self):
        while self.order:
            self.start()
            self.fold()
        return sum(part.astype(F32) for part in self.parts)


def after(values, *steps):
    moved = [piece for step in steps for piece in step.received]
    count = len(values)
    held = lax.optimization_barrier((*values, *moved))
    values, moved = held[:count], list(held[count:])
    for step in steps:
        count = len(step.received)
        step.received, moved = moved[:count], moved[count:]
        step.fold()
    return values


def key_masks(lens, length):
    middle = length // 2
    places = jnp.arange(length, dtype=jnp.int32)
    first, second = lens[:, :1], lens[:, 1:]
    single = places < first
    low = jnp.where(second > 0, single & (places < middle), single)
    high = jnp.where(second > 0, (places >= middle) & (places - middle < second), single)
    mask = jnp.where(jnp.stack([low, high], axis=1), 0.0, NEG)
    return jnp.pad(mask, ((0, 0), (0, 6), (0, 0)))


def body(
    sizes,
    tokens,
    cotangent,
    lengths,
    relevance,
    rel_table,
    w_query,
    w_key,
    w_value,
    w_output,
    w_inner,
    w_outer,
    bias_query,
    bias_value,
    bias_attn,
    bias_inner,
    bias_outer,
    gain_attn,
    shift_attn,
    gain_ffn,
    shift_ffn,
    rel_bias,
    w_score,
):
    query_size, cand_size = sizes
    devices = query_size * cand_size
    grid = Grid(query_size, cand_size)
    both = ("query", "cand")
    own_slot = lax.axis_index("cand")
    micros, length, width = tokens.shape[0], tokens.shape[3], tokens.shape[4]
    heads = rel_bias.shape[1]
    buckets = rel_bias.shape[0] * query_size
    pairs = heads // 2
    group_pairs = pairs // 3
    shard = w_query.shape[0]
    hidden = w_inner.shape[1]
    inner_shard = bias_inner.shape[0]
    spot = jnp.stack([*(grid.at[dim] for dim in ("outer", "inner", "far", "core")), own_slot])
    spot = spot.astype(jnp.int32)

    def own_part(value):
        rows = value.shape[0] // cand_size
        return lax.dynamic_slice_in_dim(value, own_slot * rows, rows, 0)

    def padded(row):
        row = row.reshape(1, -1)
        return jnp.pad(row, ((0, 0), (0, width - row.shape[1])))

    own_lens = lax.dynamic_index_in_dim(lengths[:, 0], own_slot, 1, keepdims=False)
    mask = key_masks(own_lens, length)
    lens_row = lengths.reshape(micros, 2 * cand_size)
    rel_row = relevance.reshape(micros, 2 * cand_size)
    vectors = (
        bias_query, bias_value, bias_attn, bias_outer, gain_attn, shift_attn, gain_ffn, shift_ffn,
        w_score,
    )
    table = jnp.stack(vectors)
    table = jnp.concatenate(
        [
            jnp.pad(table, ((0, 0), (0, width - shard))),
            padded(bias_inner),
            padded(rel_bias),
            jnp.zeros((TABLE_ROWS - len(VECTORS) - 2, width), BF),
        ]
    )
    groups = (group_pairs, pairs - group_pairs)
    w_inner = lax.all_gather(own_part(w_inner), both, axis=0, tiled=True)
    w_outer = lax.all_gather(own_part(w_outer), both, axis=0, tiled=True)
    stepped = shard % 32 == 0 and width // grid.sizes["far"] == TRIO == PAIR * (pairs // 2)
    if stepped:
        half = shard // 2
        blocks = pack(spot, group_pairs, w_query, w_key, w_value, w_output, table)
        head = Gather(grid, blocks[0][None])
        head.start("outer")
        lens_row, rel_row, mask = after((lens_row, rel_row, mask), head)
        (head,) = head.joined()
        block, head.pieces[0] = lax.optimization_barrier((blocks[1], head.pieces[0]))
        rest = Gather(grid, block[None])
        head.start("inner")
        rest.start("outer")
        after((), head, rest)
        head.start("core")
        near_part, far_part = rest.joined((0, half), (half, block.shape[0] - half))
        near_part.start("inner")
        far_part.start("far")
        after((), head)
        shapes = ((width, group_pairs * TRIO), (2 * query_size * TABLE_ROWS, width))
        first_weight, table = place_blocks(
            spot, shapes, (head, ((0, half, 0, 0), (1, TABLE_ROWS, 0, 0)))
        )
        table = table.reshape(query_size, 2, TABLE_ROWS, width)[:, 0]
    else:
        packed = jnp.stack(
            [value.reshape(shard, pairs, PAIR) for value in (w_query, w_key, w_value)], axis=2
        ).reshape(shard, pairs * TRIO)
        gather = partial(lax.all_gather, axis_name="query", axis=0, tiled=True)
        first_weight = gather(packed[:, : group_pairs * TRIO])
        second_weight = gather(packed[:, group_pairs * TRIO :])
        w_output = gather(w_output)
        table = gather(table).reshape(query_size, TABLE_ROWS, width)

    count = len(VECTORS)
    bias_inner = table[:, count, :inner_shard].reshape(1, hidden).astype(F32)
    rel_bias = table[:, count + 1, : rel_bias.size].reshape(buckets, heads)
    table = table[:, :count, :shard].transpose(1, 0, 2).reshape(count, width).astype(F32)
    bias_qkv = jnp.stack(
        [
            table[0].reshape(pairs, PAIR),
            jnp.zeros((pairs, PAIR), F32),
            table[1].reshape(pairs, PAIR),
        ],
        axis=1,
    ).reshape(1, pairs * TRIO)
    table = jnp.pad(table, ((0, TABLE_ROWS - count), (0, 0)))

    one_hot = (rel_table[:, None] == jnp.arange(buckets, dtype=jnp.int32)[None, :]).astype(BF)
    one_hot = jnp.pad(one_hot, ((1, 0), (0, 0)))
    dist = contract(rel_bias, one_hot, 0, 1).reshape(pairs, 2, 2 * length)
    dist = jnp.pad(dist, ((0, 0), (0, 6), (0, 0)))

    inputs = tokens.reshape(micros * length, width)
    if stepped:
        first_weight, bias_qkv, dist, table, bias_inner = after(
            (first_weight, bias_qkv, dist, table, bias_inner), near_part, far_part
        )
        (near_part,), (far_part,) = near_part.joined(), far_part.joined()
        near_part.start("far")
        far_part.start("inner")
    held = attn_fwd(inputs, first_weight, bias_qkv, dist, mask, 0, ())
    if stepped:
        held = after(held, near_part, far_part)
        near_part.start("core")
        far_part.start("core")
        held = after(held, near_part, far_part)
        second_weight, w_output = place_blocks(
            spot,
            ((width, groups[1] * TRIO), (width, width)),
            (near_part, ((0, half, 1, 0),)),
            (far_part, ((0, half, 1, 2), (1, half, 1, 0))),
        )
    qkv, context, probs = attn_fwd(
        inputs, second_weight, bias_qkv, dist, mask, group_pairs, held
    )
    normed_one, inv_one, low, act, slope = ffn_in(
        inputs, context, w_output, table, w_inner, bias_inner
    )
    act, w_outer = lax.optimization_barrier((act, w_outer))
    normed_two, inv_two, hidden_out, scores = ffn_out(act, w_outer, normed_one, table, 2 * micros)

    all_scores = lax.all_gather(
        scores[:, 0, 0].reshape(micros, 1, 2), "cand", axis=1, tiled=True
    ).reshape(micros, 2 * cand_size)
    block_rows = width // devices
    by_far, by_inner = ("far", "inner", "outer"), ("inner", "far", "outer")
    tiles = hidden // width
    grad_two, grad_outer, sums_two, loss, keep, send = outer_bwd(
        spot,
        (hidden // devices, Scatter.spots(grid, by_far, tiles)),
        all_scores,
        lens_row,
        rel_row,
        cotangent.reshape(micros * length, width),
        normed_two,
        inv_two,
        hidden_out,
        table,
        act,
    )
    far_blocks = (block_rows, Scatter.spots(grid, by_far))
    inner_blocks = (block_rows, Scatter.spots(grid, by_inner))
    sum_outer = Scatter(grid, keep, send, by_far)
    grad_in, grad_bias_inner = after(act_bwd(grad_outer, slope, w_outer), sum_outer)
    sum_outer.start()
    grad_one, grad_attn, sums_one, keep, send = after(
        inner_bwd(
            spot, inner_blocks, grad_in, w_inner, low, grad_two, normed_one, inv_one, table, context
        ),
        sum_outer,
    )
    sum_inner = Scatter(grid, keep, send, by_inner)
    sum_outer.start()
    *early, grad_attn = after(
        (
            *attn_bwd(
                spot, far_blocks, qkv, context, grad_attn, probs, w_output, inputs, 0, group_pairs
            ),
            grad_attn,
        ),
        sum_outer,
        sum_inner,
    )
    grad_qkv, dist_grad, bias_grad, keep, send = early
    sum_early = Scatter(grid, keep, send, by_far)
    sum_inner.start()
    sum_outer.start()
    (grad_attn,) = after((grad_attn,), sum_early)
    sum_early.start()
    late = attn_bwd(
        spot, inner_blocks, qkv, context, grad_attn, probs, w_output, inputs, group_pairs,
        pairs - group_pairs,
    )
    others = (grad_qkv, dist_grad, bias_grad, grad_bias_inner, sums_one, sums_two, loss)
    late = after((*late, *others), sum_early, sum_outer, sum_inner)
    late_qkv, late_dist, late_bias, keep, send = late[:5]
    grad_qkv, dist_grad, bias_grad, grad_bias_inner, sums_one, sums_two, loss = late[5:]
    sum_late = Scatter(grid, keep, send, by_inner)
    sum_inner.start()
    sum_early.start()

    dist_grad = jnp.concatenate([dist_grad, late_dist])[:, :2].reshape(heads, 2 * length)
    grad_rel = lax.dot_general(
        dist_grad,
        one_hot.astype(F32),
        (((1,), (0,)), ((), ())),
        precision=lax.Precision.HIGHEST,
    )
    bias_grad = jnp.concatenate([bias_grad, late_bias])[:, 0].reshape(pairs, 3, PAIR)
    small = [
        sums_one[:3],
        sums_two[:4],
        bias_grad.transpose(1, 0, 2).reshape(3, width),
        grad_bias_inner.reshape(-1, width),
        jnp.pad(grad_rel, ((0, 0), (0, width - buckets))),
    ]
    rows = sum(value.shape[0] for value in small)
    fold = keep.shape[1] // width
    small.append(jnp.zeros((-rows % (8 * fold), width), F32))
    small = jnp.concatenate(small)
    rows = small.shape[0] // fold
    rider = jnp.concatenate([small[i * rows : (i + 1) * rows] for i in range(fold)], axis=1)
    grad_qkv, late_qkv, rider = after((grad_qkv, late_qkv, rider), sum_late)
    sum_late.start()
    rider = rider + grid.move(rider.astype(BF), "core", 1).astype(F32)
    other = grid.move(rider.astype(BF), "inner", 1)
    grad_inputs = grad_one + contract(grad_qkv, first_weight, 1, 1)
    grad_inputs = grad_inputs + contract(late_qkv, second_weight, 1, 1)
    grad_inputs, other = after((grad_inputs, other), sum_early, sum_inner)
    sum_inner.start()
    after((), sum_late)
    sum_late.rider = rider + other.astype(F32)
    sum_late.start()
    after((), sum_late)
    sum_late.start(sum_early)
    after((), sum_inner)
    after((), sum_late)
    own_late = sum_late.result()
    own_early = sum_early.result()
    own_outer = sum_outer.result()
    own_inner = sum_inner.result()
    own = jnp.concatenate([own_early, own_late], axis=1).reshape(block_rows, pairs, 3, PAIR)
    own_query, own_key, own_value = [own[:, :, i].reshape(-1, width) for i in range(3)]

    small = jnp.concatenate(
        [sum_late.rider[:, i * width : (i + 1) * width] for i in range(fold)], axis=0
    )
    index = lax.axis_index("query") * cand_size + own_slot
    small_own = lax.dynamic_slice_in_dim(small, index * block_rows, block_rows, 1)
    at = 10 + hidden // width
    flat = small[10:at].reshape(-1)
    own_bias_inner = lax.dynamic_slice_in_dim(flat, index * (hidden // devices), hidden // devices)
    rel_rows = buckets // devices
    own_rel = lax.dynamic_slice_in_dim(small[at : at + heads], index * rel_rows, rel_rows, 1)
    shape = (micros, 1, 1, length, width)
    return (
        hidden_out.reshape(shape),
        loss[:, :1],
        grad_inputs.reshape(shape),
        own_query,
        own_key,
        own_value,
        own_inner[:, hidden:],
        own_inner[:, :hidden],
        own_outer,
        small_own[7],
        small_own[9],
        small_own[2],
        own_bias_inner,
        small_own[5],
        small_own[0],
        small_own[1],
        small_own[3],
        small_own[4],
        own_rel.T,
        small_own[6],
    )


def solution(mesh):
    both = ("query", "cand")
    slots = P(None, "query", "cand", None, None)
    lists = P(None, "query", None, None)
    rows = P("query", None)
    vec_spec = P("query")
    return jax.shard_map(
        partial(body, (mesh.shape["query"], mesh.shape["cand"])),
        mesh=mesh,
        in_specs=(slots, slots, lists, lists, P()) + (rows,) * 6 + (vec_spec,) * 9 + (rows, vec_spec),
        out_specs=(slots, P(None, "query"), slots)
        + (P(both, None),) * 6
        + (P(both),) * 9
        + (P(both, None), P(both)),
        check_vma=False,
    )
```

```python
from functools import partial

import jax
import jax.numpy as jnp
import numpy as np
from jax import lax
from jax.experimental import pallas as pl
from jax.experimental.pallas import tpu as pltpu
from jax.sharding import PartitionSpec as P

HD = 64
PAIR = 2 * HD
TRIO = 3 * PAIR
TILE = 128
BF = jnp.bfloat16
F32 = jnp.float32
NEG = -1000000000.0
EPS = 1e-05

ERFC_P = 0.3
ERFC_C = (
    0.16919777981386785,
    0.17054619772689322,
    0.14956727662616615,
    0.21002273459109255,
    -0.08286335340540726,
    0.5302129644860679,
    -0.49655482906135956,
    0.4777385344298923,
    -0.12786727948795917,
)

VECTORS = (
    "bias_query",
    "bias_value",
    "bias_attn",
    "bias_outer",
    "gain_attn",
    "shift_attn",
    "gain_ffn",
    "shift_ffn",
    "w_score",
)
TABLE_ROWS = 16
ROW = {name: index for index, name in enumerate(VECTORS)}


def cost(micros=0.001):
    return pl.CostEstimate(flops=int(micros * 1.15e9), bytes_accessed=0, transcendentals=0)


def contract(left_mat, right_mat, left_dim, right_dim):
    return lax.dot_general(
        left_mat,
        right_mat,
        (((left_dim,), (right_dim,)), ((), ())),
        preferred_element_type=F32,
    )


def gelu_pair(u):
    size = jnp.abs(u)
    t = 1.0 / (1.0 + (ERFC_P * 0.5**0.5) * size)
    poly = jnp.full_like(u, 0.5 * ERFC_C[-1])
    for coef in ERFC_C[-2::-1]:
        poly = poly * t + 0.5 * coef
    bell = jnp.exp(-0.5 * (u * u))
    tail = poly * t * bell
    cdf = jnp.where(u < 0, tail, 1.0 - tail)
    return u * cdf, cdf + u * ((2.0 * np.pi) ** -0.5 * bell)


def normalise(values):
    centred = values - jnp.mean(values, axis=-1, keepdims=True)
    inv_std = lax.rsqrt(jnp.mean(centred * centred, axis=-1, keepdims=True) + EPS)
    return centred * inv_std, inv_std


def norm_backward(grad_out, normed, inv_std, gain_vec):
    grad_normed = grad_out * gain_vec
    return inv_std * (
        grad_normed
        - jnp.mean(grad_normed, axis=-1, keepdims=True)
        - normed * jnp.mean(grad_normed * normed, axis=-1, keepdims=True)
    )


def row_chunks(rows, size, step):
    size = min(size, rows)

    @pl.loop(0, rows // size)
    def _(index):
        step(pl.ds(pl.multiple_of(index * size, size), size))


def split_rows(core, tile, rows, spots, keep, send):
    for block, spot in enumerate(spots):
        place = slice(spot * rows, (spot + 1) * rows)
        if rows % 8 == 0:
            own = pl.multiple_of((2 * block + core) * rows, 8)
            other = pl.multiple_of((2 * block + 1 - core) * rows, 8)
            keep[place, :] = tile[pl.ds(own, rows), :].astype(keep.dtype)
            send[place, :] = tile[pl.ds(other, rows), :].astype(send.dtype)
        else:
            even = tile[2 * block * rows : (2 * block + 1) * rows, :]
            odd = tile[(2 * block + 1) * rows : (2 * block + 2) * rows, :]
            keep[place, :] = jnp.where(core == 0, even, odd).astype(keep.dtype)
            send[place, :] = jnp.where(core == 0, odd, even).astype(send.dtype)


def attn_fwd_kernel(x_ref, w_ref, b_ref, dist_ref, mask_ref, *refs):
    qkv_ref, ctx_ref, p_ref, table = refs[-4:]
    length = x_ref.shape[0]
    width = 2 * length

    @pl.when(pl.program_id(1) == 0)
    def _():
        for head in range(2):
            row = jnp.broadcast_to(dist_ref[0, head : head + 1, :], (TILE, width))
            table[head] = pltpu.roll(row, 0, 1, stride=1, stride_axis=0)

    qkv = (contract(x_ref[...], w_ref[...], 1, 0) + b_ref[...]).astype(BF)
    qkv_ref[...] = qkv
    q = qkv[:, :PAIR] * jnp.asarray(HD**-0.5, BF)
    k = qkv[:, PAIR : 2 * PAIR]
    v = qkv[:, 2 * PAIR :]
    lane = lax.broadcasted_iota(jnp.int32, (length, PAIR), 1)
    raws = []
    for head in range(2):
        own = (lane < HD) == (head == 0)
        raws.append(contract(jnp.where(own, q, jnp.zeros_like(q)), k, 1, 1))
    outs = []
    for head in range(2):
        for start in range(0, length, TILE):
            half = start // (length // 2)
            logits = (
                raws[head][start : start + TILE]
                + table[head, :, length - start : width - start]
                + mask_ref[0, half : half + 1, :]
            )
            peak = jnp.max(logits, axis=1, keepdims=True)
            grown = jnp.exp(logits - peak)
            total = jnp.sum(grown, axis=1, keepdims=True)
            p_ref[0, head, start : start + TILE, :] = (grown * (1.0 / total)).astype(BF)
        outs.append(contract(p_ref[0, head], v, 1, 0))
    ctx_ref[...] = jnp.where(lane < HD, outs[0], outs[1]).astype(BF)


def attn_fwd(inputs, weight, bias, dist, mask, first, held):
    rows, width = inputs.shape
    micros = mask.shape[0]
    length = rows // micros
    pairs = weight.shape[1] // TRIO
    every = bias.shape[1] // TRIO
    return pl.pallas_call(
        attn_fwd_kernel,
        grid=(pairs, micros),
        in_specs=[
            pl.BlockSpec((length, width), lambda h, m: (m, 0)),
            pl.BlockSpec((width, TRIO), lambda h, m: (0, h)),
            pl.BlockSpec((1, TRIO), lambda h, m: (0, h + first)),
            pl.BlockSpec((1, 8, 2 * length), lambda h, m: (h + first, 0, 0)),
            pl.BlockSpec((1, 8, length), lambda h, m: (m, 0, 0)),
        ]
        + [pl.BlockSpec(memory_space=pl.ANY)] * len(held),
        out_specs=[
            pl.BlockSpec((length, TRIO), lambda h, m: (m, h + first)),
            pl.BlockSpec((length, PAIR), lambda h, m: (m, h + first)),
            pl.BlockSpec((1, 2, length, length), lambda h, m: (m, h + first, 0, 0)),
        ],
        out_shape=[
            jax.ShapeDtypeStruct((rows, every * TRIO), BF),
            jax.ShapeDtypeStruct((rows, every * PAIR), BF),
            jax.ShapeDtypeStruct((micros, 2 * every, length, length), BF),
        ],
        input_output_aliases={5 + index: index for index in range(len(held))},
        scratch_shapes=[pltpu.VMEM((2, TILE, 2 * length), F32)],
        compiler_params=pltpu.CompilerParams(vmem_limit_bytes=62 << 20),
        cost_estimate=cost(),
        name="attn_fwd",
    )(inputs, weight, bias, dist, mask, *held)


def attn_bwd_kernel(
    blocks, place_ref, qkv_ref, o_ref, dr_ref, p_ref, wo_ref, x_ref, *refs
):
    dqkv_ref, gd_ref, db_ref, keep_ref, send_ref, acc, dsb, dw, kept, sent = refs[-10:]
    length = qkv_ref.shape[0]
    width = 2 * length
    first = pl.program_id(1) == 0
    last = pl.program_id(1) == pl.num_programs(1) - 1

    @pl.when(first)
    def _():
        acc[...] = jnp.zeros_like(acc)
        dw[...] = jnp.zeros_like(dw)
        db_ref[...] = jnp.zeros_like(db_ref)

    q = qkv_ref[:, :PAIR]
    k = qkv_ref[:, PAIR : 2 * PAIR]
    v = qkv_ref[:, 2 * PAIR :]
    do = contract(dr_ref[...], wo_ref[...], 1, 1).astype(BF)
    lane = lax.broadcasted_iota(jnp.int32, (length, PAIR), 1)
    prod = do.astype(F32) * o_ref[...].astype(F32)
    dq, dk, dv, inners, dps = [], [], [], [], []
    for head in range(2):
        own = (lane < HD) == (head == 0)
        inners.append(jnp.sum(jnp.where(own, prod, 0.0), axis=1, keepdims=True))
        dps.append(contract(jnp.where(own, do, jnp.zeros_like(do)), v, 1, 1))
        dv.append(contract(p_ref[0, head], do, 0, 0))
    for head in range(2):
        inner, dp = inners[head], dps[head]
        for start in range(0, length, TILE):
            rows = slice(start, start + TILE)
            ds = p_ref[0, head, rows, :].astype(F32) * (dp[rows] - inner[rows])
            acc[head, :, length - start : width - start] += ds
            dsb[head, rows, :] = (ds * HD**-0.5).astype(BF)
        dq.append(contract(dsb[head], k, 1, 0))
        dk.append(contract(dsb[head], q, 0, 0))
    for index, (low, high) in enumerate((dq, dk, dv)):
        cols = slice(index * PAIR, (index + 1) * PAIR)
        grad = jnp.where(lane < HD, low, high).astype(BF)
        dqkv_ref[:, cols] = grad
        db_ref[0, 0:1, cols] += jnp.sum(grad.astype(F32), axis=0, keepdims=True)
    dw[...] += contract(x_ref[...], dqkv_ref[...], 0, 0)

    @pl.when(last)
    def _():
        split_rows(place_ref[3], dw, *blocks, kept, sent)
        keep_ref[...] = kept[...].astype(BF)
        send_ref[...] = sent[...].astype(BF)
        for head in range(2):
            total = acc[head, 0:8, :]
            for start in range(8, TILE, 8):
                total = total + pltpu.roll(acc[head, start : start + 8, :], width - start, 1)
            row = total[0:1, :]
            for step in range(1, 8):
                row = row + pltpu.roll(total[step : step + 1, :], width - step, 1)
            gd_ref[0, head : head + 1, :] = row


def attn_bwd(
    place, blocks, qkv, ctx, d_r, probs, w_output, inputs, first, pairs, held=(), start=0, every=None
):
    rows, width = inputs.shape
    micros, _, length, _ = probs.shape
    at = lambda shape, place: pl.BlockSpec(shape, lambda h, m, c: place(h, m))
    half = width // 2
    every = every or pairs
    return pl.pallas_call(
        partial(attn_bwd_kernel, blocks),
        grid_spec=pltpu.PrefetchScalarGridSpec(
            num_scalar_prefetch=1,
            grid=(pairs, micros),
            in_specs=[
                at((length, TRIO), lambda h, m: (m, h + first)),
                at((length, PAIR), lambda h, m: (m, h + first)),
                at((length, width), lambda h, m: (m, 0)),
                at((1, 2, length, length), lambda h, m: (m, h + first, 0, 0)),
                at((PAIR, width), lambda h, m: (h + first, 0)),
                at((length, width), lambda h, m: (m, 0)),
            ]
            + [pl.BlockSpec(memory_space=pl.ANY)] * len(held),
            out_specs=[
                at((length, TRIO), lambda h, m: (m, h + start)),
                at((1, 8, 2 * length), lambda h, m: (h + start, 0, 0)),
                at((1, 8, TRIO), lambda h, m: (h + start, 0, 0)),
                at((half, TRIO), lambda h, m: (0, h + start)),
                at((half, TRIO), lambda h, m: (0, h + start)),
            ],
            scratch_shapes=[
                pltpu.VMEM((2, TILE, 2 * length), F32),
                pltpu.VMEM((2, length, length), BF),
                pltpu.VMEM((width, TRIO), F32),
                pltpu.VMEM((half, TRIO), F32),
                pltpu.VMEM((half, TRIO), F32),
            ],
        ),
        out_shape=[
            jax.ShapeDtypeStruct((rows, every * TRIO), BF),
            jax.ShapeDtypeStruct((every, 8, 2 * length), F32),
            jax.ShapeDtypeStruct((every, 8, TRIO), F32),
            jax.ShapeDtypeStruct((half, every * TRIO), BF),
            jax.ShapeDtypeStruct((half, every * TRIO), BF),
        ],
        input_output_aliases={7 + index: index for index in range(len(held))},
        compiler_params=pltpu.CompilerParams(vmem_limit_bytes=62 << 20),
        cost_estimate=cost(),
        name="attn_bwd",
    )(place, qkv, ctx, d_r, probs, w_output, inputs, *held)


def vec(ref, name):
    return ref[ROW[name] : ROW[name] + 1, :]


def ffn_in_kernel(
    x_ref, ctx_ref, wo_ref, vec_ref, w_ref, b_ref, n1_ref, i1_ref, low_ref, act_ref, slope_ref
):
    rows = x_ref.shape[0]

    @pl.when(pl.program_id(0) == 0)
    def _():
        size = min(256, rows)
        for start in range(0, rows, size):
            at = slice(start, start + size)
            attn = contract(ctx_ref[at, :], wo_ref[...], 1, 0) + vec(vec_ref, "bias_attn")
            normed, inv_std = normalise(x_ref[at, :].astype(F32) + attn)
            n1_ref[at, :] = normed
            i1_ref[at, :] = inv_std
            first = normed * vec(vec_ref, "gain_attn") + vec(vec_ref, "shift_attn")
            low_ref[at, :] = first.astype(BF)

    def step(at):
        u = contract(low_ref[at, :], w_ref[...], 1, 0) + b_ref[...]
        act, slope = gelu_pair(u)
        act_ref[at, :] = act.astype(BF)
        slope_ref[at, :] = slope.astype(BF)

    row_chunks(rows, 256, step)


def ffn_in(inputs, context, w_output, vectors, w_inner, bias):
    rows, width = inputs.shape
    hidden = w_inner.shape[1]
    size = min(512, hidden)
    whole = pl.BlockSpec((rows, width), lambda n: (0, 0))
    column = pl.BlockSpec((rows, 1), lambda n: (0, 0))
    cols = pl.BlockSpec((rows, size), lambda n: (0, n))
    out = jax.ShapeDtypeStruct((rows, hidden), BF)
    return pl.pallas_call(
        ffn_in_kernel,
        grid=(hidden // size,),
        in_specs=[
            whole,
            whole,
            pl.BlockSpec((width, width), lambda n: (0, 0)),
            pl.BlockSpec((TABLE_ROWS, width), lambda n: (0, 0)),
            pl.BlockSpec((width, size), lambda n: (0, n)),
            pl.BlockSpec((1, size), lambda n: (0, n)),
        ],
        out_specs=[whole, column, whole, cols, cols],
        out_shape=[
            jax.ShapeDtypeStruct((rows, width), F32),
            jax.ShapeDtypeStruct((rows, 1), F32),
            jax.ShapeDtypeStruct((rows, width), BF),
            out,
            out,
        ],
        compiler_params=pltpu.CompilerParams(vmem_limit_bytes=62 << 20),
        cost_estimate=cost(),
        name="ffn_in",
    )(inputs, context, w_output, vectors, w_inner, bias)


def ffn_out_kernel(act_ref, w_ref, n1_ref, vec_ref, n2_ref, i2_ref, hid_ref, score_ref):
    first = n1_ref[...] * vec(vec_ref, "gain_attn") + vec(vec_ref, "shift_attn")
    outer = contract(act_ref[...], w_ref[...], 1, 0) + vec(vec_ref, "bias_outer")
    normed, inv_std = normalise(first + outer)
    n2_ref[...] = normed
    i2_ref[...] = inv_std
    low = (normed * vec(vec_ref, "gain_ffn") + vec(vec_ref, "shift_ffn")).astype(BF)
    hid_ref[...] = low
    row = low[0:8, :].astype(F32)[0:1, :] * vec(vec_ref, "w_score")
    score_ref[0] = jnp.broadcast_to(jnp.sum(row, axis=1, keepdims=True), score_ref.shape[1:])


def ffn_out(act, w_outer, normed, vectors, count):
    rows, hidden = act.shape
    width = w_outer.shape[1]
    size = rows // count
    block = pl.BlockSpec((size, width), lambda r: (r, 0))
    return pl.pallas_call(
        ffn_out_kernel,
        grid=(count,),
        in_specs=[
            pl.BlockSpec((size, hidden), lambda r: (r, 0)),
            pl.BlockSpec((hidden, width), lambda r: (0, 0)),
            block,
            pl.BlockSpec((TABLE_ROWS, width), lambda r: (0, 0)),
        ],
        out_specs=[
            block,
            pl.BlockSpec((size, 1), lambda r: (r, 0)),
            block,
            pl.BlockSpec((1, 8, 128), lambda r: (r, 0, 0)),
        ],
        out_shape=[
            jax.ShapeDtypeStruct((rows, width), F32),
            jax.ShapeDtypeStruct((rows, 1), F32),
            jax.ShapeDtypeStruct((rows, width), BF),
            jax.ShapeDtypeStruct((count, 8, 128), F32),
        ],
        compiler_params=pltpu.CompilerParams(vmem_limit_bytes=62 << 20),
        cost_estimate=cost(),
        name="ffn_out",
    )(act, w_outer, normed, vectors)


def list_loss(scores, lens, relevance):
    present = lens > 0
    masked = jnp.where(present, scores, NEG)
    peak = jnp.max(masked, axis=1, keepdims=True)
    log_total = peak + jnp.log(jnp.sum(jnp.exp(masked - peak), axis=1, keepdims=True))
    log_prob = masked - log_total
    rel = jnp.where(present, relevance, NEG)
    rel_exp = jnp.exp(rel - jnp.max(rel, axis=1, keepdims=True))
    target = rel_exp / jnp.sum(rel_exp, axis=1, keepdims=True)
    loss = -jnp.sum(jnp.where(present, target * log_prob, 0.0), axis=1, keepdims=True)
    return loss, jnp.where(present, jnp.exp(log_prob) - target, 0.0)


def outer_bwd_kernel(
    blocks, place_ref, score_ref, len_ref, rel_ref, cot_ref, n2_ref, i2_ref, hid_ref, vec_ref,
    act_ref, dr_ref, low, sum_ref, loss_ref, keep_ref, send_ref, tile, kept, sent,
):
    rows, width = cot_ref.shape

    @pl.when(pl.program_id(0) == 0)
    def _():
        loss, grad = list_loss(score_ref[...], len_ref[...], rel_ref[...])
        loss_ref[...] = jnp.broadcast_to(loss, loss_ref.shape)
        lane = lax.broadcasted_iota(jnp.int32, grad.shape, 1)
        micros = grad.shape[0]
        sum_ref[...] = jnp.zeros_like(sum_ref)
        firsts = {}
        for half in range(2):
            own = jnp.where(lane == 2 * place_ref[4] + half, grad, 0.0)
            own = jnp.sum(own, axis=1, keepdims=True)
            for micro in range(micros):
                firsts[(2 * micro + half) * (rows // (2 * micros))] = own[micro : micro + 1, :]
        score_row = vec(vec_ref, "w_score")
        gain = vec(vec_ref, "gain_ffn")

        def step(at):
            grad_out = cot_ref[at, :].astype(F32)
            place = lax.broadcasted_iota(jnp.int32, (grad_out.shape[0], 1), 0) + at.start
            shift = jnp.zeros_like(place, F32)
            for first, value in firsts.items():
                shift = jnp.where(place == first, value, shift)
            grad_out = grad_out + shift * score_row
            normed = n2_ref[at, :]
            grad_in = norm_backward(grad_out, normed, i2_ref[at, :], gain)
            dr_ref[at, :] = grad_in
            grad_low = grad_in.astype(BF)
            low[at, :] = grad_low
            sum_ref[0:1, :] += jnp.sum(grad_out * normed, axis=0, keepdims=True)
            sum_ref[1:2, :] += jnp.sum(grad_out, axis=0, keepdims=True)
            sum_ref[2:3, :] += jnp.sum(grad_low.astype(F32), axis=0, keepdims=True)

        row_chunks(rows, 128, step)
        total = jnp.zeros((1, width), F32)
        for first, value in firsts.items():
            total = total + value * hid_ref[first : first + 8, :].astype(F32)[0:1, :]
        sum_ref[3:4, :] = total

    tile[...] = contract(act_ref[...], low[...], 0, 0)
    split_rows(place_ref[3], tile, *blocks, kept, sent)
    keep_ref[...] = kept[...].astype(BF).reshape(keep_ref.shape)
    send_ref[...] = sent[...].astype(BF).reshape(send_ref.shape)


def outer_bwd(
    place, blocks, scores, lens, relevance, cot, normed, inv_std, hid, vectors, act
):
    rows, width = cot.shape
    hidden = act.shape[1]
    size = width
    at = lambda shape, index: pl.BlockSpec(shape, lambda n, c: index(n))
    whole = at((rows, width), lambda n: (0, 0))
    tiny = at(scores.shape, lambda n: (0, 0))
    rows_of, spots = blocks
    tiles = hidden // size
    half = at((len(spots), 1, rows_of, width), lambda n: (0, n, 0, 0))
    return pl.pallas_call(
        partial(outer_bwd_kernel, blocks),
        grid_spec=pltpu.PrefetchScalarGridSpec(
            num_scalar_prefetch=1,
            grid=(hidden // size,),
            in_specs=[
                tiny, tiny, tiny, whole, whole, at((rows, 1), lambda n: (0, 0)), whole,
                at((TABLE_ROWS, width), lambda n: (0, 0)), at((rows, size), lambda n: (0, n)),
            ],
            out_specs=[
                whole, whole, at((8, width), lambda n: (0, 0)),
                at((scores.shape[0], 128), lambda n: (0, 0)), half, half,
            ],
            scratch_shapes=[
                pltpu.VMEM((size, width), F32),
                pltpu.VMEM((size // 2, width), F32),
                pltpu.VMEM((size // 2, width), F32),
            ],
        ),
        out_shape=[
            jax.ShapeDtypeStruct((rows, width), F32),
            jax.ShapeDtypeStruct((rows, width), BF),
            jax.ShapeDtypeStruct((8, width), F32),
            jax.ShapeDtypeStruct((scores.shape[0], 128), F32),
            jax.ShapeDtypeStruct((len(spots), tiles, rows_of, width), BF),
            jax.ShapeDtypeStruct((len(spots), tiles, rows_of, width), BF),
        ],
        compiler_params=pltpu.CompilerParams(vmem_limit_bytes=62 << 20),
        cost_estimate=cost(),
        name="outer_bwd",
    )(place, scores, lens, relevance, cot, normed, inv_std, hid, vectors, act)


def act_bwd_kernel(dr_ref, slope_ref, w2_ref, din_ref, db_ref):
    grad = dr_ref[...]
    wide = w2_ref.shape[0]
    size = min(256, wide)
    for start in range(0, wide, size):
        cols = slice(start, start + size)
        d_act = contract(grad, w2_ref[cols, :], 1, 1)
        d_in = (d_act * slope_ref[:, cols].astype(F32)).astype(BF)
        din_ref[:, cols] = d_in
        db_ref[:, cols] = jnp.sum(d_in.astype(F32), axis=0, keepdims=True)


def act_bwd(grad, slope, w_outer):
    rows, hidden = slope.shape
    width = grad.shape[1]
    size = min(512, hidden)
    cols = pl.BlockSpec((rows, size), lambda n: (0, n))
    return pl.pallas_call(
        act_bwd_kernel,
        grid=(hidden // size,),
        in_specs=[
            pl.BlockSpec((rows, width), lambda n: (0, 0)),
            cols,
            pl.BlockSpec((size, width), lambda n: (n, 0)),
        ],
        out_specs=[cols, pl.BlockSpec((1, size), lambda n: (0, n))],
        out_shape=[
            jax.ShapeDtypeStruct((rows, hidden), BF),
            jax.ShapeDtypeStruct((1, hidden), F32),
        ],
        compiler_params=pltpu.CompilerParams(vmem_limit_bytes=62 << 20),
        cost_estimate=cost(),
        name="act_bwd",
    )(grad, slope, w_outer)


def inner_bwd_kernel(
    blocks, place_ref, din_ref, w1_ref, low_ref, dr_ref, n1_ref, i1_ref, vec_ref, ctx_ref,
    one_ref, grad_ref, sum_ref, keep_ref, send_ref, acc, tile, kept, sent, dr_buf, n1_buf, ctx_buf, sems,
):
    step_id = pl.program_id(0)
    last = pl.num_programs(0) - 1
    needed = [
        pltpu.make_async_copy(source, buffer, sems.at[index])
        for index, (source, buffer) in enumerate(
            ((dr_ref, dr_buf), (n1_ref, n1_buf), (ctx_ref, ctx_buf))
        )
    ]

    @pl.when(step_id == 0)
    def _():
        for copy in needed:
            copy.start()

    rows = low_ref.shape[0]

    @pl.when(step_id < last)
    def _():
        d_in = din_ref[...]
        tile[...] = contract(low_ref[...], d_in, 0, 0)
        part = contract(d_in, w1_ref[...], 1, 1)

        @pl.when(step_id == 0)
        def _():
            acc[...] = part

        @pl.when(step_id > 0)
        def _():
            acc[...] += part

    @pl.when(step_id == last)
    def _():
        for copy in needed:
            copy.wait()
        sum_ref[...] = jnp.zeros_like(sum_ref)
        gain = vec(vec_ref, "gain_attn")

        def step(at):
            grad_out = acc[at, :] + dr_buf[at, :]
            normed = n1_buf[at, :]
            grad_in = norm_backward(grad_out, normed, i1_ref[at, :], gain)
            one_ref[at, :] = grad_in
            grad_low = grad_in.astype(BF)
            grad_ref[at, :] = grad_low
            sum_ref[0:1, :] += jnp.sum(grad_out * normed, axis=0, keepdims=True)
            sum_ref[1:2, :] += jnp.sum(grad_out, axis=0, keepdims=True)
            sum_ref[2:3, :] += jnp.sum(grad_low.astype(F32), axis=0, keepdims=True)

        row_chunks(rows, 128, step)
        tile[...] = contract(ctx_buf[...], grad_ref[...], 0, 0)

    split_rows(place_ref[3], tile, *blocks, kept, sent)
    keep_ref[...] = kept[...].astype(BF)
    send_ref[...] = sent[...].astype(BF)


def inner_bwd(place, blocks, d_in, w_inner, low, d_r, normed, inv_std, vectors, context):
    rows, width = low.shape
    hidden = d_in.shape[1]
    size = width
    tiles = hidden // size
    at = lambda shape, index: pl.BlockSpec(shape, lambda n, c: index(n))
    whole = at((rows, width), lambda n: (0, 0))
    near = lambda n: (0, jnp.minimum(n, tiles - 1))
    half = at((width // 2, size), lambda n: (0, n))
    later = pl.BlockSpec(memory_space=pl.ANY)
    return pl.pallas_call(
        partial(inner_bwd_kernel, blocks),
        grid_spec=pltpu.PrefetchScalarGridSpec(
            num_scalar_prefetch=1,
            grid=(tiles + 1,),
            in_specs=[
                at((rows, size), near), at((width, size), near), whole, later, later,
                at((rows, 1), lambda n: (0, 0)), at((TABLE_ROWS, width), lambda n: (0, 0)), later,
            ],
            out_specs=[whole, whole, at((8, width), lambda n: (0, 0)), half, half],
            scratch_shapes=[
                pltpu.VMEM((rows, width), F32),
                pltpu.VMEM((width, size), F32),
                pltpu.VMEM((width // 2, size), F32),
                pltpu.VMEM((width // 2, size), F32),
                pltpu.VMEM((rows, width), F32),
                pltpu.VMEM((rows, width), F32),
                pltpu.VMEM((rows, width), BF),
                pltpu.SemaphoreType.DMA((3,)),
            ],
        ),
        out_shape=[
            jax.ShapeDtypeStruct((rows, width), F32),
            jax.ShapeDtypeStruct((rows, width), BF),
            jax.ShapeDtypeStruct((8, width), F32),
            jax.ShapeDtypeStruct((width // 2, hidden + width), BF),
            jax.ShapeDtypeStruct((width // 2, hidden + width), BF),
        ],
        compiler_params=pltpu.CompilerParams(vmem_limit_bytes=62 << 20),
        cost_estimate=cost(),
        name="inner_bwd",
    )(place, d_in, w_inner, low, d_r, normed, inv_std, vectors, context)


def shifted(axis_size, group, stride, step):
    pairs = []
    for source in range(axis_size):
        place = source // stride % group
        pairs.append((source, source + ((place + step) % group - place) * stride))
    return pairs


class Grid:
    def __init__(self, query_size, cand_size):
        query, cand = lax.axis_index("query"), lax.axis_index("cand")
        self.sizes = {"outer": query_size // 2, "inner": 2, "far": cand_size // 2, "core": 2}
        self.lengths = {"query": query_size, "cand": cand_size}
        self.axes = {
            "outer": ("query", 2),
            "inner": ("query", 1),
            "far": ("cand", 2),
            "core": ("cand", 1),
        }
        self.at = {
            "outer": query // 2,
            "inner": query % 2,
            "far": cand // 2,
            "core": cand % 2,
        }

    def move(self, value, dim, step):
        axis, stride = self.axes[dim]
        return lax.ppermute(
            value, axis, shifted(self.lengths[axis], self.sizes[dim], stride, step)
        )


def pack_kernel(pairs, place_ref, wq, wk, wv, wo, table, first, middle):
    far, core = place_ref[2], place_ref[3]
    half = wq.shape[0] // 2
    rows = pl.ds(pl.multiple_of(core * half, 16), half)
    for pair in range(pairs):
        for index, weight in enumerate((wq, wk, wv)):
            to = (pair * 3 + index) * PAIR
            first[:half, to : to + PAIR] = weight[rows, pair * PAIR : (pair + 1) * PAIR]
    first[half:, :] = table[...]
    count = wq.shape[1] // PAIR // pairs - 1
    for run in range(count):
        cols = pl.ds(pl.multiple_of(((run + 1) * pairs + far) * PAIR, PAIR), PAIR)
        for index, weight in enumerate((wq, wk, wv)):
            middle[run * half : (run + 1) * half, index * PAIR : (index + 1) * PAIR] = weight[rows, cols]
    wide = wo.shape[1] // 2
    cols = pl.ds(pl.multiple_of(far * wide, PAIR), wide)
    middle[count * half :, :] = wo[rows, cols]


def pack(place, pairs, wq, wk, wv, wo, table):
    shard, width = wq.shape
    half = shard // 2
    count = width // PAIR // pairs
    shapes = [
        (half + TABLE_ROWS, pairs * TRIO),
        (count * half, width // 2),
    ]
    return pl.pallas_call(
        partial(pack_kernel, pairs),
        grid_spec=pltpu.PrefetchScalarGridSpec(
            num_scalar_prefetch=1,
            grid=(1,),
            in_specs=[
                pl.BlockSpec(value.shape, lambda i, c: (0, 0)) for value in (wq, wk, wv, wo, table)
            ],
            out_specs=[pl.BlockSpec(shape, lambda i, c: (0, 0)) for shape in shapes],
        ),
        out_shape=[jax.ShapeDtypeStruct(shape, BF) for shape in shapes],
        compiler_params=pltpu.CompilerParams(vmem_limit_bytes=60 << 20),
        cost_estimate=cost(),
        name="pack",
    )(place, wq, wk, wv, wo, table)


def join_kernel(runs, count, *refs):
    sources, targets = refs[:count], refs[count:]
    at = 0
    for source in sources:
        size = source.shape[0]
        for target, (first, rows) in zip(targets, runs):
            target[at : at + size] = source[:, first : first + rows, :]
        at += size


def join(pieces, runs):
    total = sum(piece.shape[0] for piece in pieces)
    wide = pieces[0].shape[2]
    whole = lambda shape: pl.BlockSpec(shape, lambda i: (0, 0, 0))
    shapes = [(total, rows, wide) for _, rows in runs]
    return pl.pallas_call(
        partial(join_kernel, runs, len(pieces)),
        grid=(1,),
        in_specs=[whole(piece.shape) for piece in pieces],
        out_specs=[whole(shape) for shape in shapes],
        out_shape=[jax.ShapeDtypeStruct(shape, BF) for shape in shapes],
        compiler_params=pltpu.CompilerParams(vmem_limit_bytes=62 << 20),
        cost_estimate=cost(),
        name="join",
    )(*pieces)


class Gather:
    def __init__(self, grid, blocks, places=None):
        self.grid = grid
        self.pieces = [blocks]
        self.places = [places or [{"outer": 0, "inner": 0, "far": 0, "core": 0}]]
        self.received = []

    def joined(self, *runs):
        places = sum(self.places, [])
        runs = runs or ((0, self.pieces[0].shape[1]),)
        return [Gather(self.grid, piece, places) for piece in join(self.pieces, runs)]

    def start(self, dim):
        size = self.grid.sizes[dim]
        self.coming = []
        for piece, places in zip(self.pieces, self.places):
            for step in range(1, size):
                self.received.append(self.grid.move(piece, dim, step))
                self.coming.append(
                    [{**place, dim: (place[dim] + step) % size} for place in places]
                )

    def fold(self):
        self.pieces = self.pieces + self.received
        self.places = self.places + self.coming
        self.received = []


def place_kernel(splits, places, outer, spot_ref, *refs):
    count = 1 + max(run[0] for split in splits for run in split)
    sources, targets, sems = refs[: -1 - count], refs[-1 - count : -1], refs[-1]
    copies = []
    at = 0
    for source, split in zip(sources, splits):
        wide = source.shape[-1]
        for index in range(source.shape[0]):
            place = places[at]
            zed = lax.rem(spot_ref[0] + (outer - place["outer"]), outer)
            other = {
                dim: lax.rem(spot_ref[i] + place[dim], 2)
                for i, dim in enumerate(("inner", "far", "core"), 1)
            }
            block = (zed * 2 + other["inner"]) * 2 + other["core"]
            first = 0
            for target, rows, stride, offset in split:
                cols = slice(None)
                if stride:
                    col = other["far"] * (stride * wide) + offset * wide
                    cols = pl.ds(pl.multiple_of(col, 128), wide)
                copies.append(
                    pltpu.make_async_copy(
                        source.at[index, pl.ds(first, rows), :],
                        targets[target].at[pl.ds(pl.multiple_of(block * rows, 16), rows), cols],
                        sems.at[len(copies)],
                    )
                )
                first += rows
            at += 1
    for copy in copies:
        copy.start()
    for copy in copies:
        copy.wait()


def place_blocks(spot, shapes, *gathers):
    places, pieces, splits, copies = [], [], [], 0
    for gather, split in gathers:
        for piece, found in zip(gather.pieces, gather.places):
            pieces.append(piece)
            splits.append(split)
            places += found
            copies += len(found) * len(split)
    return pl.pallas_call(
        partial(place_kernel, splits, places, gather.grid.sizes["outer"]),
        grid_spec=pltpu.PrefetchScalarGridSpec(
            num_scalar_prefetch=1,
            grid=(1,),
            in_specs=[pl.BlockSpec(memory_space=pl.ANY)] * len(pieces),
            out_specs=[pl.BlockSpec(memory_space=pltpu.VMEM)] * len(shapes),
            scratch_shapes=[pltpu.SemaphoreType.DMA((copies,))],
        ),
        out_shape=[jax.ShapeDtypeStruct(shape, BF) for shape in shapes],
        compiler_params=pltpu.CompilerParams(vmem_limit_bytes=24 << 20),
        cost_estimate=cost(),
        name="place_blocks",
    )(spot, *pieces)


class Scatter:
    def __init__(self, grid, keep, send, order):
        self.grid = grid
        self.dims = list(order)
        self.order = list(order)
        self.sizes = [grid.sizes[dim] for dim in self.dims]
        self.rider, self.others = None, ()
        self.parts = [self.blocks(keep)]
        self.shape = self.blocks(send).shape
        self.received = [grid.move(send, "core", 1)]

    def blocks(self, value):
        return value.reshape(*self.sizes, -1, value.shape[-1])

    @staticmethod
    def spots(grid, order, tiles=1):
        sizes = {dim: grid.sizes[dim] for dim in order}
        if tiles > 1:
            sizes["outer"] //= tiles
        spots = []
        for block in range(int(np.prod(list(sizes.values())))):
            at = {
                "outer": block // (2 * sizes["far"]),
                "inner": block // sizes["far"] % 2,
                "far": block % sizes["far"],
            }
            spot = 0
            for dim in order:
                spot = spot * sizes[dim] + at[dim]
            spots.append(spot)
        return tuple(spots)

    def step(self, dim):
        axis = self.dims.index(dim)
        size, here = self.grid.sizes[dim], self.grid.at[dim]
        sent = []
        for step in range(1, size):
            total = 0.0
            for part in self.parts:
                piece = lax.dynamic_index_in_dim(part, (here + step) % size, axis, keepdims=False)
                total += piece.astype(F32)
            sent.append(total.astype(BF))
        self.parts = [
            lax.dynamic_index_in_dim(part, here, axis, keepdims=False) for part in self.parts
        ]
        self.dims.remove(dim)
        return sent

    def start(self, *others):
        dim = self.order.pop(0)
        sent = self.step(dim)
        self.others = others
        self.shape = sent[0].shape
        for other in others:
            other.order.remove(dim)
            more = other.step(dim)
            other.shape = more[0].shape
            sent = [jnp.concatenate(pair, axis=-1) for pair in zip(sent, more)]
        if self.rider is not None:
            wide = sent[0].shape[-1]
            rider = jnp.pad(self.rider, ((0, 0), (0, wide - self.rider.shape[1]))).astype(BF)
            sent = [jnp.concatenate([value.reshape(-1, wide), rider]) for value in sent]
        self.received = [self.grid.move(value, dim, step) for step, value in enumerate(sent, 1)]

    def fold(self):
        for value in self.received:
            if self.rider is not None:
                count = value.shape[0] - self.rider.shape[0]
                self.rider = self.rider + value[count:, : self.rider.shape[1]].astype(F32)
                value = value[:count]
            value = value.reshape(*self.shape[:-1], value.shape[-1])
            at = 0
            for scatter in (self, *self.others):
                wide = scatter.shape[-1]
                scatter.parts.append(value[..., at : at + wide])
                at += wide
        self.received, self.others = [], ()

    def result(self):
        while self.order:
            self.start()
            self.fold()
        return sum(part.astype(F32) for part in self.parts)


def after(values, *steps):
    moved = [piece for step in steps for piece in step.received]
    count = len(values)
    held = lax.optimization_barrier((*values, *moved))
    values, moved = held[:count], list(held[count:])
    for step in steps:
        count = len(step.received)
        step.received, moved = moved[:count], moved[count:]
        step.fold()
    return values


def key_masks(lens, length):
    middle = length // 2
    places = jnp.arange(length, dtype=jnp.int32)
    first, second = lens[:, :1], lens[:, 1:]
    single = places < first
    low = jnp.where(second > 0, single & (places < middle), single)
    high = jnp.where(second > 0, (places >= middle) & (places - middle < second), single)
    mask = jnp.where(jnp.stack([low, high], axis=1), 0.0, NEG)
    return jnp.pad(mask, ((0, 0), (0, 6), (0, 0)))


def body(
    sizes,
    tokens,
    cotangent,
    lengths,
    relevance,
    rel_table,
    w_query,
    w_key,
    w_value,
    w_output,
    w_inner,
    w_outer,
    bias_query,
    bias_value,
    bias_attn,
    bias_inner,
    bias_outer,
    gain_attn,
    shift_attn,
    gain_ffn,
    shift_ffn,
    rel_bias,
    w_score,
):
    query_size, cand_size = sizes
    devices = query_size * cand_size
    grid = Grid(query_size, cand_size)
    both = ("query", "cand")
    own_slot = lax.axis_index("cand")
    micros, length, width = tokens.shape[0], tokens.shape[3], tokens.shape[4]
    heads = rel_bias.shape[1]
    buckets = rel_bias.shape[0] * query_size
    pairs = heads // 2
    group_pairs = pairs // 3
    shard = w_query.shape[0]
    hidden = w_inner.shape[1]
    inner_shard = bias_inner.shape[0]
    spot = jnp.stack([*(grid.at[dim] for dim in ("outer", "inner", "far", "core")), own_slot])
    spot = spot.astype(jnp.int32)

    def own_part(value):
        rows = value.shape[0] // cand_size
        return lax.dynamic_slice_in_dim(value, own_slot * rows, rows, 0)

    def padded(row):
        row = row.reshape(1, -1)
        return jnp.pad(row, ((0, 0), (0, width - row.shape[1])))

    own_lens = lax.dynamic_index_in_dim(lengths[:, 0], own_slot, 1, keepdims=False)
    mask = key_masks(own_lens, length)
    lens_row = lengths.reshape(micros, 2 * cand_size)
    rel_row = relevance.reshape(micros, 2 * cand_size)
    vectors = (
        bias_query, bias_value, bias_attn, bias_outer, gain_attn, shift_attn, gain_ffn, shift_ffn,
        w_score,
    )
    table = jnp.stack(vectors)
    table = jnp.concatenate(
        [
            jnp.pad(table, ((0, 0), (0, width - shard))),
            padded(bias_inner),
            padded(rel_bias),
            jnp.zeros((TABLE_ROWS - len(VECTORS) - 2, width), BF),
        ]
    )
    groups = (group_pairs, pairs - group_pairs)
    w_inner = lax.all_gather(own_part(w_inner), both, axis=0, tiled=True)
    stepped = shard % 32 == 0 and width // grid.sizes["far"] == TRIO == PAIR * (pairs // 2)
    if stepped:
        half = shard // 2
        blocks = pack(spot, group_pairs, w_query, w_key, w_value, w_output, table)
        head = Gather(grid, blocks[0][None])
        head.start("outer")
        lens_row, rel_row, mask, w_outer = after((lens_row, rel_row, mask, w_outer), head)
        (head,) = head.joined()
        block, head.pieces[0] = lax.optimization_barrier((blocks[1], head.pieces[0]))
        rest = Gather(grid, block[None])
        head.start("inner")
        rest.start("outer")
        after((), head, rest)
        head.start("core")
        near_part, far_part = rest.joined((0, half), (half, block.shape[0] - half))
        near_part.start("inner")
        far_part.start("far")
        after((), head)
        shapes = ((width, group_pairs * TRIO), (2 * query_size * TABLE_ROWS, width))
        first_weight, table = place_blocks(
            spot, shapes, (head, ((0, half, 0, 0), (1, TABLE_ROWS, 0, 0)))
        )
        table = table.reshape(query_size, 2, TABLE_ROWS, width)[:, 0]
    else:
        packed = jnp.stack(
            [value.reshape(shard, pairs, PAIR) for value in (w_query, w_key, w_value)], axis=2
        ).reshape(shard, pairs * TRIO)
        gather = partial(lax.all_gather, axis_name="query", axis=0, tiled=True)
        first_weight = gather(packed[:, : group_pairs * TRIO])
        second_weight = gather(packed[:, group_pairs * TRIO :])
        w_output = gather(w_output)
        table = gather(table).reshape(query_size, TABLE_ROWS, width)

    w_outer = lax.all_gather(own_part(w_outer), both, axis=0, tiled=True)
    count = len(VECTORS)
    bias_inner = table[:, count, :inner_shard].reshape(1, hidden).astype(F32)
    rel_bias = table[:, count + 1, : rel_bias.size].reshape(buckets, heads)
    table = table[:, :count, :shard].transpose(1, 0, 2).reshape(count, width).astype(F32)
    bias_qkv = jnp.stack(
        [
            table[0].reshape(pairs, PAIR),
            jnp.zeros((pairs, PAIR), F32),
            table[1].reshape(pairs, PAIR),
        ],
        axis=1,
    ).reshape(1, pairs * TRIO)
    table = jnp.pad(table, ((0, TABLE_ROWS - count), (0, 0)))

    one_hot = (rel_table[:, None] == jnp.arange(buckets, dtype=jnp.int32)[None, :]).astype(BF)
    one_hot = jnp.pad(one_hot, ((1, 0), (0, 0)))
    dist = contract(rel_bias, one_hot, 0, 1).reshape(pairs, 2, 2 * length)
    dist = jnp.pad(dist, ((0, 0), (0, 6), (0, 0)))

    inputs = tokens.reshape(micros * length, width)
    if stepped:
        first_weight, bias_qkv, dist, table, bias_inner = after(
            (first_weight, bias_qkv, dist, table, bias_inner), near_part, far_part
        )
        (near_part,), (far_part,) = near_part.joined(), far_part.joined()
        near_part.start("far")
        far_part.start("inner")
    held = attn_fwd(inputs, first_weight, bias_qkv, dist, mask, 0, ())
    if stepped:
        held = after(held, near_part, far_part)
        near_part.start("core")
        far_part.start("core")
        held = after(held, near_part, far_part)
        second_weight, w_output = place_blocks(
            spot,
            ((width, groups[1] * TRIO), (width, width)),
            (near_part, ((0, half, 1, 0),)),
            (far_part, ((0, half, 1, 2), (1, half, 1, 0))),
        )
    qkv, context, probs = attn_fwd(
        inputs, second_weight, bias_qkv, dist, mask, group_pairs, held
    )
    normed_one, inv_one, low, act, slope = ffn_in(
        inputs, context, w_output, table, w_inner, bias_inner
    )
    act, w_outer = lax.optimization_barrier((act, w_outer))
    normed_two, inv_two, hidden_out, scores = ffn_out(act, w_outer, normed_one, table, 2 * micros)

    all_scores = lax.all_gather(
        scores[:, 0, 0].reshape(micros, 1, 2), "cand", axis=1, tiled=True
    ).reshape(micros, 2 * cand_size)
    block_rows = width // devices
    by_far, by_inner = ("far", "inner", "outer"), ("inner", "far", "outer")
    tiles = hidden // width
    grad_two, grad_outer, sums_two, loss, keep, send = outer_bwd(
        spot,
        (hidden // devices, Scatter.spots(grid, by_far, tiles)),
        all_scores,
        lens_row,
        rel_row,
        cotangent.reshape(micros * length, width),
        normed_two,
        inv_two,
        hidden_out,
        table,
        act,
    )
    far_blocks = (block_rows, Scatter.spots(grid, by_far))
    inner_blocks = (block_rows, Scatter.spots(grid, by_inner))
    sum_outer = Scatter(grid, keep, send, by_far)
    grad_in, grad_bias_inner = after(act_bwd(grad_outer, slope, w_outer), sum_outer)
    sum_outer.start()
    grad_one, grad_attn, sums_one, keep, send = after(
        inner_bwd(
            spot, inner_blocks, grad_in, w_inner, low, grad_two, normed_one, inv_one, table, context
        ),
        sum_outer,
    )
    sum_inner = Scatter(grid, keep, send, by_inner)
    sum_outer.start()
    *early, grad_attn = after(
        (
            *attn_bwd(
                spot, far_blocks, qkv, context, grad_attn, probs, w_output, inputs, 0, group_pairs
            ),
            grad_attn,
        ),
        sum_outer,
        sum_inner,
    )
    grad_qkv, dist_grad, bias_grad, keep, send = early
    sum_early = Scatter(grid, keep, send, by_far)
    sum_inner.start()
    sum_outer.start()
    (grad_attn,) = after((grad_attn,), sum_early)
    sum_early.start()
    late = attn_bwd(
        spot, inner_blocks, qkv, context, grad_attn, probs, w_output, inputs, group_pairs,
        pairs - group_pairs,
    )
    others = (grad_qkv, dist_grad, bias_grad, grad_bias_inner, sums_one, sums_two, loss)
    late = after((*late, *others), sum_early, sum_outer, sum_inner)
    late_qkv, late_dist, late_bias, keep, send = late[:5]
    grad_qkv, dist_grad, bias_grad, grad_bias_inner, sums_one, sums_two, loss = late[5:]
    sum_late = Scatter(grid, keep, send, by_inner)
    sum_inner.start()
    sum_early.start()

    waiting = (grad_qkv, late_qkv, dist_grad, late_dist, bias_grad, late_bias)
    waiting = after((*waiting, grad_bias_inner, sums_one, sums_two), sum_late)
    grad_qkv, late_qkv, dist_grad, late_dist, bias_grad, late_bias = waiting[:6]
    grad_bias_inner, sums_one, sums_two = waiting[6:]
    fold = keep.shape[1] // width
    sum_late.start()
    dist_grad = jnp.concatenate([dist_grad, late_dist])[:, :2].reshape(heads, 2 * length)
    grad_rel = lax.dot_general(
        dist_grad,
        one_hot.astype(F32),
        (((1,), (0,)), ((), ())),
        precision=lax.Precision.HIGHEST,
    )
    bias_grad = jnp.concatenate([bias_grad, late_bias])[:, 0].reshape(pairs, 3, PAIR)
    small = [
        sums_one[:3],
        sums_two[:4],
        bias_grad.transpose(1, 0, 2).reshape(3, width),
        grad_bias_inner.reshape(-1, width),
        jnp.pad(grad_rel, ((0, 0), (0, width - buckets))),
    ]
    rows = sum(value.shape[0] for value in small)
    small.append(jnp.zeros((-rows % (8 * fold), width), F32))
    small = jnp.concatenate(small)
    rows = small.shape[0] // fold
    rider = jnp.concatenate([small[i * rows : (i + 1) * rows] for i in range(fold)], axis=1)
    rider = rider + grid.move(rider.astype(BF), "core", 1).astype(F32)
    other = grid.move(rider.astype(BF), "inner", 1)
    grad_inputs = grad_one + contract(grad_qkv, first_weight, 1, 1)
    grad_inputs = grad_inputs + contract(late_qkv, second_weight, 1, 1)
    grad_inputs, other = after((grad_inputs, other), sum_early, sum_inner)
    sum_inner.start()
    after((), sum_late)
    sum_late.rider = rider + other.astype(F32)
    sum_late.start()
    after((), sum_late)
    sum_late.start(sum_early)
    after((), sum_inner)
    after((), sum_late)
    own_late = sum_late.result()
    own_early = sum_early.result()
    own_outer = sum_outer.result()
    own_inner = sum_inner.result()
    own = jnp.concatenate([own_early, own_late], axis=1).reshape(block_rows, pairs, 3, PAIR)
    own_query, own_key, own_value = [own[:, :, i].reshape(-1, width) for i in range(3)]

    small = jnp.concatenate(
        [sum_late.rider[:, i * width : (i + 1) * width] for i in range(fold)], axis=0
    )
    index = lax.axis_index("query") * cand_size + own_slot
    small_own = lax.dynamic_slice_in_dim(small, index * block_rows, block_rows, 1)
    at = 10 + hidden // width
    flat = small[10:at].reshape(-1)
    own_bias_inner = lax.dynamic_slice_in_dim(flat, index * (hidden // devices), hidden // devices)
    rel_rows = buckets // devices
    own_rel = lax.dynamic_slice_in_dim(small[at : at + heads], index * rel_rows, rel_rows, 1)
    shape = (micros, 1, 1, length, width)
    return (
        hidden_out.reshape(shape),
        loss[:, :1],
        grad_inputs.reshape(shape),
        own_query,
        own_key,
        own_value,
        own_inner[:, hidden:],
        own_inner[:, :hidden],
        own_outer,
        small_own[7],
        small_own[9],
        small_own[2],
        own_bias_inner,
        small_own[5],
        small_own[0],
        small_own[1],
        small_own[3],
        small_own[4],
        own_rel.T,
        small_own[6],
    )


def solution(mesh):
    both = ("query", "cand")
    slots = P(None, "query", "cand", None, None)
    lists = P(None, "query", None, None)
    rows = P("query", None)
    vec_spec = P("query")
    return jax.shard_map(
        partial(body, (mesh.shape["query"], mesh.shape["cand"])),
        mesh=mesh,
        in_specs=(slots, slots, lists, lists, P()) + (rows,) * 6 + (vec_spec,) * 9 + (rows, vec_spec),
        out_specs=(slots, P(None, "query"), slots)
        + (P(both, None),) * 6
        + (P(both),) * 9
        + (P(both, None), P(both)),
        check_vma=False,
    )
```

```python
from functools import partial

import jax
import jax.numpy as jnp
import numpy as np
from jax import lax
from jax.experimental import pallas as pl
from jax.experimental.pallas import tpu as pltpu
from jax.sharding import PartitionSpec as P

HD = 64
PAIR = 2 * HD
TRIO = 3 * PAIR
TILE = 128
BF = jnp.bfloat16
F32 = jnp.float32
NEG = -1000000000.0
EPS = 1e-05

ERFC_P = 0.3
ERFC_C = (
    0.16919777981386785,
    0.17054619772689322,
    0.14956727662616615,
    0.21002273459109255,
    -0.08286335340540726,
    0.5302129644860679,
    -0.49655482906135956,
    0.4777385344298923,
    -0.12786727948795917,
)

VECTORS = (
    "bias_query",
    "bias_value",
    "bias_attn",
    "bias_outer",
    "gain_attn",
    "shift_attn",
    "gain_ffn",
    "shift_ffn",
    "w_score",
)
TABLE_ROWS = 16
ROW = {name: index for index, name in enumerate(VECTORS)}


def cost(micros=0.001):
    return pl.CostEstimate(flops=int(micros * 1.15e9), bytes_accessed=0, transcendentals=0)


def contract(left_mat, right_mat, left_dim, right_dim):
    return lax.dot_general(
        left_mat,
        right_mat,
        (((left_dim,), (right_dim,)), ((), ())),
        preferred_element_type=F32,
    )


def gelu_pair(u):
    size = jnp.abs(u)
    t = 1.0 / (1.0 + (ERFC_P * 0.5**0.5) * size)
    poly = jnp.full_like(u, 0.5 * ERFC_C[-1])
    for coef in ERFC_C[-2::-1]:
        poly = poly * t + 0.5 * coef
    bell = jnp.exp(-0.5 * (u * u))
    tail = poly * t * bell
    cdf = jnp.where(u < 0, tail, 1.0 - tail)
    return u * cdf, cdf + u * ((2.0 * np.pi) ** -0.5 * bell)


def normalise(values):
    centred = values - jnp.mean(values, axis=-1, keepdims=True)
    inv_std = lax.rsqrt(jnp.mean(centred * centred, axis=-1, keepdims=True) + EPS)
    return centred * inv_std, inv_std


def norm_backward(grad_out, normed, inv_std, gain_vec):
    grad_normed = grad_out * gain_vec
    return inv_std * (
        grad_normed
        - jnp.mean(grad_normed, axis=-1, keepdims=True)
        - normed * jnp.mean(grad_normed * normed, axis=-1, keepdims=True)
    )


def row_chunks(rows, size, step):
    size = min(size, rows)

    @pl.loop(0, rows // size)
    def _(index):
        step(pl.ds(pl.multiple_of(index * size, size), size))


def split_rows(core, tile, rows, spots, keep, send):
    for block, spot in enumerate(spots):
        place = slice(spot * rows, (spot + 1) * rows)
        if rows % 8 == 0:
            own = pl.multiple_of((2 * block + core) * rows, 8)
            other = pl.multiple_of((2 * block + 1 - core) * rows, 8)
            keep[place, :] = tile[pl.ds(own, rows), :].astype(keep.dtype)
            send[place, :] = tile[pl.ds(other, rows), :].astype(send.dtype)
        else:
            even = tile[2 * block * rows : (2 * block + 1) * rows, :]
            odd = tile[(2 * block + 1) * rows : (2 * block + 2) * rows, :]
            keep[place, :] = jnp.where(core == 0, even, odd).astype(keep.dtype)
            send[place, :] = jnp.where(core == 0, odd, even).astype(send.dtype)


def attn_fwd_kernel(x_ref, w_ref, b_ref, dist_ref, mask_ref, *refs):
    qkv_ref, ctx_ref, p_ref, table = refs[-4:]
    length = x_ref.shape[0]
    width = 2 * length

    @pl.when(pl.program_id(1) == 0)
    def _():
        for head in range(2):
            row = jnp.broadcast_to(dist_ref[0, head : head + 1, :], (TILE, width))
            table[head] = pltpu.roll(row, 0, 1, stride=1, stride_axis=0)

    qkv = (contract(x_ref[...], w_ref[...], 1, 0) + b_ref[...]).astype(BF)
    qkv_ref[...] = qkv
    q = qkv[:, :PAIR] * jnp.asarray(HD**-0.5, BF)
    k = qkv[:, PAIR : 2 * PAIR]
    v = qkv[:, 2 * PAIR :]
    lane = lax.broadcasted_iota(jnp.int32, (length, PAIR), 1)
    raws = []
    for head in range(2):
        own = (lane < HD) == (head == 0)
        raws.append(contract(jnp.where(own, q, jnp.zeros_like(q)), k, 1, 1))
    outs = []
    for head in range(2):
        for start in range(0, length, TILE):
            half = start // (length // 2)
            logits = (
                raws[head][start : start + TILE]
                + table[head, :, length - start : width - start]
                + mask_ref[0, half : half + 1, :]
            )
            peak = jnp.max(logits, axis=1, keepdims=True)
            grown = jnp.exp(logits - peak)
            total = jnp.sum(grown, axis=1, keepdims=True)
            p_ref[0, head, start : start + TILE, :] = (grown * (1.0 / total)).astype(BF)
        outs.append(contract(p_ref[0, head], v, 1, 0))
    ctx_ref[...] = jnp.where(lane < HD, outs[0], outs[1]).astype(BF)


def attn_fwd(inputs, weight, bias, dist, mask, first, held):
    rows, width = inputs.shape
    micros = mask.shape[0]
    length = rows // micros
    pairs = weight.shape[1] // TRIO
    every = bias.shape[1] // TRIO
    return pl.pallas_call(
        attn_fwd_kernel,
        grid=(pairs, micros),
        in_specs=[
            pl.BlockSpec((length, width), lambda h, m: (m, 0)),
            pl.BlockSpec((width, TRIO), lambda h, m: (0, h)),
            pl.BlockSpec((1, TRIO), lambda h, m: (0, h + first)),
            pl.BlockSpec((1, 8, 2 * length), lambda h, m: (h + first, 0, 0)),
            pl.BlockSpec((1, 8, length), lambda h, m: (m, 0, 0)),
        ]
        + [pl.BlockSpec(memory_space=pl.ANY)] * len(held),
        out_specs=[
            pl.BlockSpec((length, TRIO), lambda h, m: (m, h + first)),
            pl.BlockSpec((length, PAIR), lambda h, m: (m, h + first)),
            pl.BlockSpec((1, 2, length, length), lambda h, m: (m, h + first, 0, 0)),
        ],
        out_shape=[
            jax.ShapeDtypeStruct((rows, every * TRIO), BF),
            jax.ShapeDtypeStruct((rows, every * PAIR), BF),
            jax.ShapeDtypeStruct((micros, 2 * every, length, length), BF),
        ],
        input_output_aliases={5 + index: index for index in range(len(held))},
        scratch_shapes=[pltpu.VMEM((2, TILE, 2 * length), F32)],
        compiler_params=pltpu.CompilerParams(vmem_limit_bytes=62 << 20),
        cost_estimate=cost(),
        name="attn_fwd",
    )(inputs, weight, bias, dist, mask, *held)


def attn_bwd_kernel(
    blocks, place_ref, qkv_ref, o_ref, dr_ref, p_ref, wo_ref, x_ref, *refs
):
    dqkv_ref, gd_ref, db_ref, keep_ref, send_ref, acc, dsb, dw, kept, sent = refs[-10:]
    length = qkv_ref.shape[0]
    width = 2 * length
    first = pl.program_id(1) == 0
    last = pl.program_id(1) == pl.num_programs(1) - 1

    @pl.when(first)
    def _():
        acc[...] = jnp.zeros_like(acc)
        dw[...] = jnp.zeros_like(dw)
        db_ref[...] = jnp.zeros_like(db_ref)

    q = qkv_ref[:, :PAIR]
    k = qkv_ref[:, PAIR : 2 * PAIR]
    v = qkv_ref[:, 2 * PAIR :]
    do = contract(dr_ref[...], wo_ref[...], 1, 1).astype(BF)
    lane = lax.broadcasted_iota(jnp.int32, (length, PAIR), 1)
    prod = do.astype(F32) * o_ref[...].astype(F32)
    dq, dk, dv, inners, dps = [], [], [], [], []
    for head in range(2):
        own = (lane < HD) == (head == 0)
        inners.append(jnp.sum(jnp.where(own, prod, 0.0), axis=1, keepdims=True))
        dps.append(contract(jnp.where(own, do, jnp.zeros_like(do)), v, 1, 1))
        dv.append(contract(p_ref[0, head], do, 0, 0))
    for head in range(2):
        inner, dp = inners[head], dps[head]
        for start in range(0, length, TILE):
            rows = slice(start, start + TILE)
            ds = p_ref[0, head, rows, :].astype(F32) * (dp[rows] - inner[rows])
            acc[head, :, length - start : width - start] += ds
            dsb[head, rows, :] = (ds * HD**-0.5).astype(BF)
        dq.append(contract(dsb[head], k, 1, 0))
        dk.append(contract(dsb[head], q, 0, 0))
    for index, (low, high) in enumerate((dq, dk, dv)):
        cols = slice(index * PAIR, (index + 1) * PAIR)
        grad = jnp.where(lane < HD, low, high).astype(BF)
        dqkv_ref[:, cols] = grad
        db_ref[0, 0:1, cols] += jnp.sum(grad.astype(F32), axis=0, keepdims=True)
    dw[...] += contract(x_ref[...], dqkv_ref[...], 0, 0)

    @pl.when(last)
    def _():
        split_rows(place_ref[3], dw, *blocks, kept, sent)
        keep_ref[...] = kept[...].astype(BF)
        send_ref[...] = sent[...].astype(BF)
        for head in range(2):
            total = acc[head, 0:8, :]
            for start in range(8, TILE, 8):
                total = total + pltpu.roll(acc[head, start : start + 8, :], width - start, 1)
            row = total[0:1, :]
            for step in range(1, 8):
                row = row + pltpu.roll(total[step : step + 1, :], width - step, 1)
            gd_ref[0, head : head + 1, :] = row


def attn_bwd(
    place, blocks, qkv, ctx, d_r, probs, w_output, inputs, first, pairs, held=(), start=0, every=None
):
    rows, width = inputs.shape
    micros, _, length, _ = probs.shape
    at = lambda shape, place: pl.BlockSpec(shape, lambda h, m, c: place(h, m))
    half = width // 2
    every = every or pairs
    return pl.pallas_call(
        partial(attn_bwd_kernel, blocks),
        grid_spec=pltpu.PrefetchScalarGridSpec(
            num_scalar_prefetch=1,
            grid=(pairs, micros),
            in_specs=[
                at((length, TRIO), lambda h, m: (m, h + first)),
                at((length, PAIR), lambda h, m: (m, h + first)),
                at((length, width), lambda h, m: (m, 0)),
                at((1, 2, length, length), lambda h, m: (m, h + first, 0, 0)),
                at((PAIR, width), lambda h, m: (h + first, 0)),
                at((length, width), lambda h, m: (m, 0)),
            ]
            + [pl.BlockSpec(memory_space=pl.ANY)] * len(held),
            out_specs=[
                at((length, TRIO), lambda h, m: (m, h + start)),
                at((1, 8, 2 * length), lambda h, m: (h + start, 0, 0)),
                at((1, 8, TRIO), lambda h, m: (h + start, 0, 0)),
                at((half, TRIO), lambda h, m: (0, h + start)),
                at((half, TRIO), lambda h, m: (0, h + start)),
            ],
            scratch_shapes=[
                pltpu.VMEM((2, TILE, 2 * length), F32),
                pltpu.VMEM((2, length, length), BF),
                pltpu.VMEM((width, TRIO), F32),
                pltpu.VMEM((half, TRIO), F32),
                pltpu.VMEM((half, TRIO), F32),
            ],
        ),
        out_shape=[
            jax.ShapeDtypeStruct((rows, every * TRIO), BF),
            jax.ShapeDtypeStruct((every, 8, 2 * length), F32),
            jax.ShapeDtypeStruct((every, 8, TRIO), F32),
            jax.ShapeDtypeStruct((half, every * TRIO), BF),
            jax.ShapeDtypeStruct((half, every * TRIO), BF),
        ],
        input_output_aliases={7 + index: index for index in range(len(held))},
        compiler_params=pltpu.CompilerParams(vmem_limit_bytes=62 << 20),
        cost_estimate=cost(),
        name="attn_bwd",
    )(place, qkv, ctx, d_r, probs, w_output, inputs, *held)


def vec(ref, name):
    return ref[ROW[name] : ROW[name] + 1, :]


def ffn_in_kernel(
    x_ref, ctx_ref, wo_ref, vec_ref, w_ref, b_ref, n1_ref, i1_ref, low_ref, act_ref, slope_ref
):
    rows = x_ref.shape[0]

    @pl.when(pl.program_id(0) == 0)
    def _():
        size = min(256, rows)
        for start in range(0, rows, size):
            at = slice(start, start + size)
            attn = contract(ctx_ref[at, :], wo_ref[...], 1, 0) + vec(vec_ref, "bias_attn")
            normed, inv_std = normalise(x_ref[at, :].astype(F32) + attn)
            n1_ref[at, :] = normed
            i1_ref[at, :] = inv_std
            first = normed * vec(vec_ref, "gain_attn") + vec(vec_ref, "shift_attn")
            low_ref[at, :] = first.astype(BF)

    def step(at):
        u = contract(low_ref[at, :], w_ref[...], 1, 0) + b_ref[...]
        act, slope = gelu_pair(u)
        act_ref[at, :] = act.astype(BF)
        slope_ref[at, :] = slope.astype(BF)

    row_chunks(rows, 256, step)


def ffn_in(inputs, context, w_output, vectors, w_inner, bias):
    rows, width = inputs.shape
    hidden = w_inner.shape[1]
    size = min(512, hidden)
    whole = pl.BlockSpec((rows, width), lambda n: (0, 0))
    column = pl.BlockSpec((rows, 1), lambda n: (0, 0))
    cols = pl.BlockSpec((rows, size), lambda n: (0, n))
    out = jax.ShapeDtypeStruct((rows, hidden), BF)
    return pl.pallas_call(
        ffn_in_kernel,
        grid=(hidden // size,),
        in_specs=[
            whole,
            whole,
            pl.BlockSpec((width, width), lambda n: (0, 0)),
            pl.BlockSpec((TABLE_ROWS, width), lambda n: (0, 0)),
            pl.BlockSpec((width, size), lambda n: (0, n)),
            pl.BlockSpec((1, size), lambda n: (0, n)),
        ],
        out_specs=[whole, column, whole, cols, cols],
        out_shape=[
            jax.ShapeDtypeStruct((rows, width), F32),
            jax.ShapeDtypeStruct((rows, 1), F32),
            jax.ShapeDtypeStruct((rows, width), BF),
            out,
            out,
        ],
        compiler_params=pltpu.CompilerParams(vmem_limit_bytes=62 << 20),
        cost_estimate=cost(),
        name="ffn_in",
    )(inputs, context, w_output, vectors, w_inner, bias)


def ffn_out_kernel(act_ref, w_ref, n1_ref, vec_ref, n2_ref, i2_ref, hid_ref, score_ref):
    first = n1_ref[...] * vec(vec_ref, "gain_attn") + vec(vec_ref, "shift_attn")
    outer = contract(act_ref[...], w_ref[...], 1, 0) + vec(vec_ref, "bias_outer")
    normed, inv_std = normalise(first + outer)
    n2_ref[...] = normed
    i2_ref[...] = inv_std
    low = (normed * vec(vec_ref, "gain_ffn") + vec(vec_ref, "shift_ffn")).astype(BF)
    hid_ref[...] = low
    row = low[0:8, :].astype(F32)[0:1, :] * vec(vec_ref, "w_score")
    score_ref[0] = jnp.broadcast_to(jnp.sum(row, axis=1, keepdims=True), score_ref.shape[1:])


def ffn_out(act, w_outer, normed, vectors, count):
    rows, hidden = act.shape
    width = w_outer.shape[1]
    size = rows // count
    block = pl.BlockSpec((size, width), lambda r: (r, 0))
    return pl.pallas_call(
        ffn_out_kernel,
        grid=(count,),
        in_specs=[
            pl.BlockSpec((size, hidden), lambda r: (r, 0)),
            pl.BlockSpec((hidden, width), lambda r: (0, 0)),
            block,
            pl.BlockSpec((TABLE_ROWS, width), lambda r: (0, 0)),
        ],
        out_specs=[
            block,
            pl.BlockSpec((size, 1), lambda r: (r, 0)),
            block,
            pl.BlockSpec((1, 8, 128), lambda r: (r, 0, 0)),
        ],
        out_shape=[
            jax.ShapeDtypeStruct((rows, width), F32),
            jax.ShapeDtypeStruct((rows, 1), F32),
            jax.ShapeDtypeStruct((rows, width), BF),
            jax.ShapeDtypeStruct((count, 8, 128), F32),
        ],
        compiler_params=pltpu.CompilerParams(vmem_limit_bytes=62 << 20),
        cost_estimate=cost(),
        name="ffn_out",
    )(act, w_outer, normed, vectors)


def list_loss(scores, lens, relevance):
    present = lens > 0
    masked = jnp.where(present, scores, NEG)
    peak = jnp.max(masked, axis=1, keepdims=True)
    log_total = peak + jnp.log(jnp.sum(jnp.exp(masked - peak), axis=1, keepdims=True))
    log_prob = masked - log_total
    rel = jnp.where(present, relevance, NEG)
    rel_exp = jnp.exp(rel - jnp.max(rel, axis=1, keepdims=True))
    target = rel_exp / jnp.sum(rel_exp, axis=1, keepdims=True)
    loss = -jnp.sum(jnp.where(present, target * log_prob, 0.0), axis=1, keepdims=True)
    return loss, jnp.where(present, jnp.exp(log_prob) - target, 0.0)


def outer_bwd_kernel(
    blocks, place_ref, score_ref, len_ref, rel_ref, cot_ref, n2_ref, i2_ref, hid_ref, vec_ref,
    act_ref, dr_ref, low, sum_ref, loss_ref, keep_ref, send_ref, tile, kept, sent,
):
    rows, width = cot_ref.shape

    @pl.when(pl.program_id(0) == 0)
    def _():
        loss, grad = list_loss(score_ref[...], len_ref[...], rel_ref[...])
        loss_ref[...] = jnp.broadcast_to(loss, loss_ref.shape)
        lane = lax.broadcasted_iota(jnp.int32, grad.shape, 1)
        micros = grad.shape[0]
        sum_ref[...] = jnp.zeros_like(sum_ref)
        firsts = {}
        for half in range(2):
            own = jnp.where(lane == 2 * place_ref[4] + half, grad, 0.0)
            own = jnp.sum(own, axis=1, keepdims=True)
            for micro in range(micros):
                firsts[(2 * micro + half) * (rows // (2 * micros))] = own[micro : micro + 1, :]
        score_row = vec(vec_ref, "w_score")
        gain = vec(vec_ref, "gain_ffn")

        def step(at):
            grad_out = cot_ref[at, :].astype(F32)
            place = lax.broadcasted_iota(jnp.int32, (grad_out.shape[0], 1), 0) + at.start
            shift = jnp.zeros_like(place, F32)
            for first, value in firsts.items():
                shift = jnp.where(place == first, value, shift)
            grad_out = grad_out + shift * score_row
            normed = n2_ref[at, :]
            grad_in = norm_backward(grad_out, normed, i2_ref[at, :], gain)
            dr_ref[at, :] = grad_in
            grad_low = grad_in.astype(BF)
            low[at, :] = grad_low
            sum_ref[0:1, :] += jnp.sum(grad_out * normed, axis=0, keepdims=True)
            sum_ref[1:2, :] += jnp.sum(grad_out, axis=0, keepdims=True)
            sum_ref[2:3, :] += jnp.sum(grad_low.astype(F32), axis=0, keepdims=True)

        row_chunks(rows, 256, step)
        total = jnp.zeros((1, width), F32)
        for first, value in firsts.items():
            total = total + value * hid_ref[first : first + 8, :].astype(F32)[0:1, :]
        sum_ref[3:4, :] = total

    tile[...] = contract(act_ref[...], low[...], 0, 0)
    split_rows(place_ref[3], tile, *blocks, kept, sent)
    keep_ref[...] = kept[...].astype(BF).reshape(keep_ref.shape)
    send_ref[...] = sent[...].astype(BF).reshape(send_ref.shape)


def outer_bwd(
    place, blocks, scores, lens, relevance, cot, normed, inv_std, hid, vectors, act
):
    rows, width = cot.shape
    hidden = act.shape[1]
    size = width
    at = lambda shape, index: pl.BlockSpec(shape, lambda n, c: index(n))
    whole = at((rows, width), lambda n: (0, 0))
    tiny = at(scores.shape, lambda n: (0, 0))
    rows_of, spots = blocks
    tiles = hidden // size
    half = at((len(spots), 1, rows_of, width), lambda n: (0, n, 0, 0))
    return pl.pallas_call(
        partial(outer_bwd_kernel, blocks),
        grid_spec=pltpu.PrefetchScalarGridSpec(
            num_scalar_prefetch=1,
            grid=(hidden // size,),
            in_specs=[
                tiny, tiny, tiny, whole, whole, at((rows, 1), lambda n: (0, 0)), whole,
                at((TABLE_ROWS, width), lambda n: (0, 0)), at((rows, size), lambda n: (0, n)),
            ],
            out_specs=[
                whole, whole, at((8, width), lambda n: (0, 0)),
                at((scores.shape[0], 128), lambda n: (0, 0)), half, half,
            ],
            scratch_shapes=[
                pltpu.VMEM((size, width), F32),
                pltpu.VMEM((size // 2, width), F32),
                pltpu.VMEM((size // 2, width), F32),
            ],
        ),
        out_shape=[
            jax.ShapeDtypeStruct((rows, width), F32),
            jax.ShapeDtypeStruct((rows, width), BF),
            jax.ShapeDtypeStruct((8, width), F32),
            jax.ShapeDtypeStruct((scores.shape[0], 128), F32),
            jax.ShapeDtypeStruct((len(spots), tiles, rows_of, width), BF),
            jax.ShapeDtypeStruct((len(spots), tiles, rows_of, width), BF),
        ],
        compiler_params=pltpu.CompilerParams(vmem_limit_bytes=62 << 20),
        cost_estimate=cost(),
        name="outer_bwd",
    )(place, scores, lens, relevance, cot, normed, inv_std, hid, vectors, act)


def act_bwd_kernel(dr_ref, slope_ref, w2_ref, din_ref, db_ref):
    grad = dr_ref[...]
    wide = w2_ref.shape[0]
    size = min(512, wide)
    for start in range(0, wide, size):
        cols = slice(start, start + size)
        d_act = contract(grad, w2_ref[cols, :], 1, 1)
        d_in = (d_act * slope_ref[:, cols].astype(F32)).astype(BF)
        din_ref[:, cols] = d_in
        db_ref[:, cols] = jnp.sum(d_in.astype(F32), axis=0, keepdims=True)


def act_bwd(grad, slope, w_outer):
    rows, hidden = slope.shape
    width = grad.shape[1]
    size = min(1024, hidden)
    cols = pl.BlockSpec((rows, size), lambda n: (0, n))
    return pl.pallas_call(
        act_bwd_kernel,
        grid=(hidden // size,),
        in_specs=[
            pl.BlockSpec((rows, width), lambda n: (0, 0)),
            cols,
            pl.BlockSpec((size, width), lambda n: (n, 0)),
        ],
        out_specs=[cols, pl.BlockSpec((1, size), lambda n: (0, n))],
        out_shape=[
            jax.ShapeDtypeStruct((rows, hidden), BF),
            jax.ShapeDtypeStruct((1, hidden), F32),
        ],
        compiler_params=pltpu.CompilerParams(vmem_limit_bytes=62 << 20),
        cost_estimate=cost(),
        name="act_bwd",
    )(grad, slope, w_outer)


def inner_bwd_kernel(
    blocks, place_ref, din_ref, w1_ref, low_ref, dr_ref, n1_ref, i1_ref, vec_ref, ctx_ref,
    one_ref, grad_ref, sum_ref, keep_ref, send_ref, acc, tile, kept, sent, dr_buf, n1_buf, ctx_buf, sems,
):
    step_id = pl.program_id(0)
    last = pl.num_programs(0) - 1
    needed = [
        pltpu.make_async_copy(source, buffer, sems.at[index])
        for index, (source, buffer) in enumerate(
            ((dr_ref, dr_buf), (n1_ref, n1_buf), (ctx_ref, ctx_buf))
        )
    ]

    @pl.when(step_id == 0)
    def _():
        for copy in needed:
            copy.start()

    rows = low_ref.shape[0]

    @pl.when(step_id < last)
    def _():
        d_in = din_ref[...]
        tile[...] = contract(low_ref[...], d_in, 0, 0)
        part = contract(d_in, w1_ref[...], 1, 1)

        @pl.when(step_id == 0)
        def _():
            acc[...] = part

        @pl.when(step_id > 0)
        def _():
            acc[...] += part

    @pl.when(step_id == last)
    def _():
        for copy in needed:
            copy.wait()
        sum_ref[...] = jnp.zeros_like(sum_ref)
        gain = vec(vec_ref, "gain_attn")

        def step(at):
            grad_out = acc[at, :] + dr_buf[at, :]
            normed = n1_buf[at, :]
            grad_in = norm_backward(grad_out, normed, i1_ref[at, :], gain)
            one_ref[at, :] = grad_in
            grad_low = grad_in.astype(BF)
            grad_ref[at, :] = grad_low
            sum_ref[0:1, :] += jnp.sum(grad_out * normed, axis=0, keepdims=True)
            sum_ref[1:2, :] += jnp.sum(grad_out, axis=0, keepdims=True)
            sum_ref[2:3, :] += jnp.sum(grad_low.astype(F32), axis=0, keepdims=True)

        row_chunks(rows, 256, step)
        tile[...] = contract(ctx_buf[...], grad_ref[...], 0, 0)

    split_rows(place_ref[3], tile, *blocks, kept, sent)
    keep_ref[...] = kept[...].astype(BF)
    send_ref[...] = sent[...].astype(BF)


def inner_bwd(place, blocks, d_in, w_inner, low, d_r, normed, inv_std, vectors, context):
    rows, width = low.shape
    hidden = d_in.shape[1]
    size = width
    tiles = hidden // size
    at = lambda shape, index: pl.BlockSpec(shape, lambda n, c: index(n))
    whole = at((rows, width), lambda n: (0, 0))
    near = lambda n: (0, jnp.minimum(n, tiles - 1))
    half = at((width // 2, size), lambda n: (0, n))
    later = pl.BlockSpec(memory_space=pl.ANY)
    return pl.pallas_call(
        partial(inner_bwd_kernel, blocks),
        grid_spec=pltpu.PrefetchScalarGridSpec(
            num_scalar_prefetch=1,
            grid=(tiles + 1,),
            in_specs=[
                at((rows, size), near), at((width, size), near), whole, later, later,
                at((rows, 1), lambda n: (0, 0)), at((TABLE_ROWS, width), lambda n: (0, 0)), later,
            ],
            out_specs=[whole, whole, at((8, width), lambda n: (0, 0)), half, half],
            scratch_shapes=[
                pltpu.VMEM((rows, width), F32),
                pltpu.VMEM((width, size), F32),
                pltpu.VMEM((width // 2, size), F32),
                pltpu.VMEM((width // 2, size), F32),
                pltpu.VMEM((rows, width), F32),
                pltpu.VMEM((rows, width), F32),
                pltpu.VMEM((rows, width), BF),
                pltpu.SemaphoreType.DMA((3,)),
            ],
        ),
        out_shape=[
            jax.ShapeDtypeStruct((rows, width), F32),
            jax.ShapeDtypeStruct((rows, width), BF),
            jax.ShapeDtypeStruct((8, width), F32),
            jax.ShapeDtypeStruct((width // 2, hidden + width), BF),
            jax.ShapeDtypeStruct((width // 2, hidden + width), BF),
        ],
        compiler_params=pltpu.CompilerParams(vmem_limit_bytes=62 << 20),
        cost_estimate=cost(),
        name="inner_bwd",
    )(place, d_in, w_inner, low, d_r, normed, inv_std, vectors, context)


def shifted(axis_size, group, stride, step):
    pairs = []
    for source in range(axis_size):
        place = source // stride % group
        pairs.append((source, source + ((place + step) % group - place) * stride))
    return pairs


class Grid:
    def __init__(self, query_size, cand_size):
        query, cand = lax.axis_index("query"), lax.axis_index("cand")
        self.sizes = {"outer": query_size // 2, "inner": 2, "far": cand_size // 2, "core": 2}
        self.lengths = {"query": query_size, "cand": cand_size}
        self.axes = {
            "outer": ("query", 2),
            "inner": ("query", 1),
            "far": ("cand", 2),
            "core": ("cand", 1),
        }
        self.at = {
            "outer": query // 2,
            "inner": query % 2,
            "far": cand // 2,
            "core": cand % 2,
        }

    def move(self, value, dim, step):
        axis, stride = self.axes[dim]
        return lax.ppermute(
            value, axis, shifted(self.lengths[axis], self.sizes[dim], stride, step)
        )


def pack_kernel(pairs, place_ref, wq, wk, wv, wo, table, first, middle):
    far, core = place_ref[2], place_ref[3]
    half = wq.shape[0] // 2
    rows = pl.ds(pl.multiple_of(core * half, 16), half)
    for pair in range(pairs):
        for index, weight in enumerate((wq, wk, wv)):
            to = (pair * 3 + index) * PAIR
            first[:half, to : to + PAIR] = weight[rows, pair * PAIR : (pair + 1) * PAIR]
    first[half:, :] = table[...]
    count = wq.shape[1] // PAIR // pairs - 1
    for run in range(count):
        cols = pl.ds(pl.multiple_of(((run + 1) * pairs + far) * PAIR, PAIR), PAIR)
        for index, weight in enumerate((wq, wk, wv)):
            middle[run * half : (run + 1) * half, index * PAIR : (index + 1) * PAIR] = weight[rows, cols]
    wide = wo.shape[1] // 2
    cols = pl.ds(pl.multiple_of(far * wide, PAIR), wide)
    middle[count * half :, :] = wo[rows, cols]


def pack(place, pairs, wq, wk, wv, wo, table):
    shard, width = wq.shape
    half = shard // 2
    count = width // PAIR // pairs
    shapes = [
        (half + TABLE_ROWS, pairs * TRIO),
        (count * half, width // 2),
    ]
    return pl.pallas_call(
        partial(pack_kernel, pairs),
        grid_spec=pltpu.PrefetchScalarGridSpec(
            num_scalar_prefetch=1,
            grid=(1,),
            in_specs=[
                pl.BlockSpec(value.shape, lambda i, c: (0, 0)) for value in (wq, wk, wv, wo, table)
            ],
            out_specs=[pl.BlockSpec(shape, lambda i, c: (0, 0)) for shape in shapes],
        ),
        out_shape=[jax.ShapeDtypeStruct(shape, BF) for shape in shapes],
        compiler_params=pltpu.CompilerParams(vmem_limit_bytes=60 << 20),
        cost_estimate=cost(),
        name="pack",
    )(place, wq, wk, wv, wo, table)


def join_kernel(runs, count, *refs):
    sources, targets = refs[:count], refs[count:]
    at = 0
    for source in sources:
        size = source.shape[0]
        for target, (first, rows) in zip(targets, runs):
            target[at : at + size] = source[:, first : first + rows, :]
        at += size


def join(pieces, runs):
    total = sum(piece.shape[0] for piece in pieces)
    wide = pieces[0].shape[2]
    whole = lambda shape: pl.BlockSpec(shape, lambda i: (0, 0, 0))
    shapes = [(total, rows, wide) for _, rows in runs]
    return pl.pallas_call(
        partial(join_kernel, runs, len(pieces)),
        grid=(1,),
        in_specs=[whole(piece.shape) for piece in pieces],
        out_specs=[whole(shape) for shape in shapes],
        out_shape=[jax.ShapeDtypeStruct(shape, BF) for shape in shapes],
        compiler_params=pltpu.CompilerParams(vmem_limit_bytes=62 << 20),
        cost_estimate=cost(),
        name="join",
    )(*pieces)


class Gather:
    def __init__(self, grid, blocks, places=None):
        self.grid = grid
        self.pieces = [blocks]
        self.places = [places or [{"outer": 0, "inner": 0, "far": 0, "core": 0}]]
        self.received = []

    def joined(self, *runs):
        places = sum(self.places, [])
        runs = runs or ((0, self.pieces[0].shape[1]),)
        return [Gather(self.grid, piece, places) for piece in join(self.pieces, runs)]

    def start(self, dim):
        size = self.grid.sizes[dim]
        self.coming = []
        for piece, places in zip(self.pieces, self.places):
            for step in range(1, size):
                self.received.append(self.grid.move(piece, dim, step))
                self.coming.append(
                    [{**place, dim: (place[dim] + step) % size} for place in places]
                )

    def fold(self):
        self.pieces = self.pieces + self.received
        self.places = self.places + self.coming
        self.received = []


def place_kernel(splits, places, outer, spot_ref, *refs):
    count = 1 + max(run[0] for split in splits for run in split)
    sources, targets, sems = refs[: -1 - count], refs[-1 - count : -1], refs[-1]
    copies = []
    at = 0
    for source, split in zip(sources, splits):
        wide = source.shape[-1]
        for index in range(source.shape[0]):
            place = places[at]
            zed = lax.rem(spot_ref[0] + (outer - place["outer"]), outer)
            other = {
                dim: lax.rem(spot_ref[i] + place[dim], 2)
                for i, dim in enumerate(("inner", "far", "core"), 1)
            }
            block = (zed * 2 + other["inner"]) * 2 + other["core"]
            first = 0
            for target, rows, stride, offset in split:
                cols = slice(None)
                if stride:
                    col = other["far"] * (stride * wide) + offset * wide
                    cols = pl.ds(pl.multiple_of(col, 128), wide)
                copies.append(
                    pltpu.make_async_copy(
                        source.at[index, pl.ds(first, rows), :],
                        targets[target].at[pl.ds(pl.multiple_of(block * rows, 16), rows), cols],
                        sems.at[len(copies)],
                    )
                )
                first += rows
            at += 1
    for copy in copies:
        copy.start()
    for copy in copies:
        copy.wait()


def place_blocks(spot, shapes, *gathers):
    places, pieces, splits, copies = [], [], [], 0
    for gather, split in gathers:
        for piece, found in zip(gather.pieces, gather.places):
            pieces.append(piece)
            splits.append(split)
            places += found
            copies += len(found) * len(split)
    return pl.pallas_call(
        partial(place_kernel, splits, places, gather.grid.sizes["outer"]),
        grid_spec=pltpu.PrefetchScalarGridSpec(
            num_scalar_prefetch=1,
            grid=(1,),
            in_specs=[pl.BlockSpec(memory_space=pl.ANY)] * len(pieces),
            out_specs=[pl.BlockSpec(memory_space=pltpu.VMEM)] * len(shapes),
            scratch_shapes=[pltpu.SemaphoreType.DMA((copies,))],
        ),
        out_shape=[jax.ShapeDtypeStruct(shape, BF) for shape in shapes],
        compiler_params=pltpu.CompilerParams(vmem_limit_bytes=24 << 20),
        cost_estimate=cost(),
        name="place_blocks",
    )(spot, *pieces)


class Scatter:
    def __init__(self, grid, keep, send, order):
        self.grid = grid
        self.dims = list(order)
        self.order = list(order)
        self.sizes = [grid.sizes[dim] for dim in self.dims]
        self.rider, self.others = None, ()
        self.parts = [self.blocks(keep)]
        self.shape = self.blocks(send).shape
        self.received = [grid.move(send, "core", 1)]

    def blocks(self, value):
        return value.reshape(*self.sizes, -1, value.shape[-1])

    @staticmethod
    def spots(grid, order, tiles=1):
        sizes = {dim: grid.sizes[dim] for dim in order}
        if tiles > 1:
            sizes["outer"] //= tiles
        spots = []
        for block in range(int(np.prod(list(sizes.values())))):
            at = {
                "outer": block // (2 * sizes["far"]),
                "inner": block // sizes["far"] % 2,
                "far": block % sizes["far"],
            }
            spot = 0
            for dim in order:
                spot = spot * sizes[dim] + at[dim]
            spots.append(spot)
        return tuple(spots)

    def step(self, dim):
        axis = self.dims.index(dim)
        size, here = self.grid.sizes[dim], self.grid.at[dim]
        sent = []
        for step in range(1, size):
            total = 0.0
            for part in self.parts:
                piece = lax.dynamic_index_in_dim(part, (here + step) % size, axis, keepdims=False)
                total += piece.astype(F32)
            sent.append(total.astype(BF))
        self.parts = [
            lax.dynamic_index_in_dim(part, here, axis, keepdims=False) for part in self.parts
        ]
        self.dims.remove(dim)
        return sent

    def start(self, *others):
        dim = self.order.pop(0)
        sent = self.step(dim)
        self.others = others
        self.shape = sent[0].shape
        for other in others:
            other.order.remove(dim)
            more = other.step(dim)
            other.shape = more[0].shape
            sent = [jnp.concatenate(pair, axis=-1) for pair in zip(sent, more)]
        if self.rider is not None:
            wide = sent[0].shape[-1]
            rider = jnp.pad(self.rider, ((0, 0), (0, wide - self.rider.shape[1]))).astype(BF)
            sent = [jnp.concatenate([value.reshape(-1, wide), rider]) for value in sent]
        self.received = [self.grid.move(value, dim, step) for step, value in enumerate(sent, 1)]

    def fold(self):
        for value in self.received:
            if self.rider is not None:
                count = value.shape[0] - self.rider.shape[0]
                self.rider = self.rider + value[count:, : self.rider.shape[1]].astype(F32)
                value = value[:count]
            value = value.reshape(*self.shape[:-1], value.shape[-1])
            at = 0
            for scatter in (self, *self.others):
                wide = scatter.shape[-1]
                scatter.parts.append(value[..., at : at + wide])
                at += wide
        self.received, self.others = [], ()

    def result(self):
        while self.order:
            self.start()
            self.fold()
        return sum(part.astype(F32) for part in self.parts)


def after(values, *steps):
    moved = [piece for step in steps for piece in step.received]
    count = len(values)
    held = lax.optimization_barrier((*values, *moved))
    values, moved = held[:count], list(held[count:])
    for step in steps:
        count = len(step.received)
        step.received, moved = moved[:count], moved[count:]
        step.fold()
    return values


def key_masks(lens, length):
    middle = length // 2
    places = jnp.arange(length, dtype=jnp.int32)
    first, second = lens[:, :1], lens[:, 1:]
    single = places < first
    low = jnp.where(second > 0, single & (places < middle), single)
    high = jnp.where(second > 0, (places >= middle) & (places - middle < second), single)
    mask = jnp.where(jnp.stack([low, high], axis=1), 0.0, NEG)
    return jnp.pad(mask, ((0, 0), (0, 6), (0, 0)))


def body(
    sizes,
    tokens,
    cotangent,
    lengths,
    relevance,
    rel_table,
    w_query,
    w_key,
    w_value,
    w_output,
    w_inner,
    w_outer,
    bias_query,
    bias_value,
    bias_attn,
    bias_inner,
    bias_outer,
    gain_attn,
    shift_attn,
    gain_ffn,
    shift_ffn,
    rel_bias,
    w_score,
):
    query_size, cand_size = sizes
    devices = query_size * cand_size
    grid = Grid(query_size, cand_size)
    both = ("query", "cand")
    own_slot = lax.axis_index("cand")
    micros, length, width = tokens.shape[0], tokens.shape[3], tokens.shape[4]
    heads = rel_bias.shape[1]
    buckets = rel_bias.shape[0] * query_size
    pairs = heads // 2
    group_pairs = pairs // 3
    shard = w_query.shape[0]
    hidden = w_inner.shape[1]
    inner_shard = bias_inner.shape[0]
    spot = jnp.stack([*(grid.at[dim] for dim in ("outer", "inner", "far", "core")), own_slot])
    spot = spot.astype(jnp.int32)

    def own_part(value):
        rows = value.shape[0] // cand_size
        return lax.dynamic_slice_in_dim(value, own_slot * rows, rows, 0)

    def padded(row):
        row = row.reshape(1, -1)
        return jnp.pad(row, ((0, 0), (0, width - row.shape[1])))

    own_lens = lax.dynamic_index_in_dim(lengths[:, 0], own_slot, 1, keepdims=False)
    mask = key_masks(own_lens, length)
    lens_row = lengths.reshape(micros, 2 * cand_size)
    rel_row = relevance.reshape(micros, 2 * cand_size)
    vectors = (
        bias_query, bias_value, bias_attn, bias_outer, gain_attn, shift_attn, gain_ffn, shift_ffn,
        w_score,
    )
    table = jnp.stack(vectors)
    table = jnp.concatenate(
        [
            jnp.pad(table, ((0, 0), (0, width - shard))),
            padded(bias_inner),
            padded(rel_bias),
            jnp.zeros((TABLE_ROWS - len(VECTORS) - 2, width), BF),
        ]
    )
    groups = (group_pairs, pairs - group_pairs)
    w_inner = lax.all_gather(own_part(w_inner), both, axis=0, tiled=True)
    stepped = shard % 32 == 0 and width // grid.sizes["far"] == TRIO == PAIR * (pairs // 2)
    if stepped:
        half = shard // 2
        blocks = pack(spot, group_pairs, w_query, w_key, w_value, w_output, table)
        head = Gather(grid, blocks[0][None])
        head.start("outer")
        lens_row, rel_row, mask, w_outer = after((lens_row, rel_row, mask, w_outer), head)
        (head,) = head.joined()
        block, head.pieces[0] = lax.optimization_barrier((blocks[1], head.pieces[0]))
        rest = Gather(grid, block[None])
        head.start("inner")
        rest.start("outer")
        after((), head, rest)
        head.start("core")
        near_part, far_part = rest.joined((0, half), (half, block.shape[0] - half))
        near_part.start("inner")
        far_part.start("far")
        after((), head)
        shapes = ((width, group_pairs * TRIO), (2 * query_size * TABLE_ROWS, width))
        first_weight, table = place_blocks(
            spot, shapes, (head, ((0, half, 0, 0), (1, TABLE_ROWS, 0, 0)))
        )
        table = table.reshape(query_size, 2, TABLE_ROWS, width)[:, 0]
    else:
        packed = jnp.stack(
            [value.reshape(shard, pairs, PAIR) for value in (w_query, w_key, w_value)], axis=2
        ).reshape(shard, pairs * TRIO)
        gather = partial(lax.all_gather, axis_name="query", axis=0, tiled=True)
        first_weight = gather(packed[:, : group_pairs * TRIO])
        second_weight = gather(packed[:, group_pairs * TRIO :])
        w_output = gather(w_output)
        table = gather(table).reshape(query_size, TABLE_ROWS, width)

    w_outer = lax.all_gather(own_part(w_outer), both, axis=0, tiled=True)
    count = len(VECTORS)
    bias_inner = table[:, count, :inner_shard].reshape(1, hidden).astype(F32)
    rel_bias = table[:, count + 1, : rel_bias.size].reshape(buckets, heads)
    table = table[:, :count, :shard].transpose(1, 0, 2).reshape(count, width).astype(F32)
    bias_qkv = jnp.stack(
        [
            table[0].reshape(pairs, PAIR),
            jnp.zeros((pairs, PAIR), F32),
            table[1].reshape(pairs, PAIR),
        ],
        axis=1,
    ).reshape(1, pairs * TRIO)
    table = jnp.pad(table, ((0, TABLE_ROWS - count), (0, 0)))

    one_hot = (rel_table[:, None] == jnp.arange(buckets, dtype=jnp.int32)[None, :]).astype(BF)
    one_hot = jnp.pad(one_hot, ((1, 0), (0, 0)))
    dist = contract(rel_bias, one_hot, 0, 1).reshape(pairs, 2, 2 * length)
    dist = jnp.pad(dist, ((0, 0), (0, 6), (0, 0)))

    inputs = tokens.reshape(micros * length, width)
    if stepped:
        first_weight, bias_qkv, dist, table, bias_inner = after(
            (first_weight, bias_qkv, dist, table, bias_inner), near_part, far_part
        )
        (near_part,), (far_part,) = near_part.joined(), far_part.joined()
        near_part.start("far")
        far_part.start("inner")
    held = attn_fwd(inputs, first_weight, bias_qkv, dist, mask, 0, ())
    if stepped:
        held = after(held, near_part, far_part)
        near_part.start("core")
        far_part.start("core")
        held = after(held, near_part, far_part)
        second_weight, w_output = place_blocks(
            spot,
            ((width, groups[1] * TRIO), (width, width)),
            (near_part, ((0, half, 1, 0),)),
            (far_part, ((0, half, 1, 2), (1, half, 1, 0))),
        )
    qkv, context, probs = attn_fwd(
        inputs, second_weight, bias_qkv, dist, mask, group_pairs, held
    )
    normed_one, inv_one, low, act, slope = ffn_in(
        inputs, context, w_output, table, w_inner, bias_inner
    )
    act, w_outer = lax.optimization_barrier((act, w_outer))
    normed_two, inv_two, hidden_out, scores = ffn_out(act, w_outer, normed_one, table, 2 * micros)

    all_scores = lax.all_gather(
        scores[:, 0, 0].reshape(micros, 1, 2), "cand", axis=1, tiled=True
    ).reshape(micros, 2 * cand_size)
    block_rows = width // devices
    by_far, by_inner = ("far", "inner", "outer"), ("inner", "far", "outer")
    tiles = hidden // width
    grad_two, grad_outer, sums_two, loss, keep, send = outer_bwd(
        spot,
        (hidden // devices, Scatter.spots(grid, by_far, tiles)),
        all_scores,
        lens_row,
        rel_row,
        cotangent.reshape(micros * length, width),
        normed_two,
        inv_two,
        hidden_out,
        table,
        act,
    )
    far_blocks = (block_rows, Scatter.spots(grid, by_far))
    inner_blocks = (block_rows, Scatter.spots(grid, by_inner))
    sum_outer = Scatter(grid, keep, send, by_far)
    grad_in, grad_bias_inner = after(act_bwd(grad_outer, slope, w_outer), sum_outer)
    sum_outer.start()
    grad_one, grad_attn, sums_one, keep, send = after(
        inner_bwd(
            spot, inner_blocks, grad_in, w_inner, low, grad_two, normed_one, inv_one, table, context
        ),
        sum_outer,
    )
    sum_inner = Scatter(grid, keep, send, by_inner)
    sum_outer.start()
    *early, grad_attn = after(
        (
            *attn_bwd(
                spot, far_blocks, qkv, context, grad_attn, probs, w_output, inputs, 0, group_pairs
            ),
            grad_attn,
        ),
        sum_outer,
        sum_inner,
    )
    grad_qkv, dist_grad, bias_grad, keep, send = early
    sum_early = Scatter(grid, keep, send, by_far)
    sum_inner.start()
    sum_outer.start()
    (grad_attn,) = after((grad_attn,), sum_early)
    sum_early.start()
    late = attn_bwd(
        spot, inner_blocks, qkv, context, grad_attn, probs, w_output, inputs, group_pairs,
        pairs - group_pairs,
    )
    others = (grad_qkv, dist_grad, bias_grad, grad_bias_inner, sums_one, sums_two, loss)
    late = after((*late, *others), sum_early, sum_outer, sum_inner)
    late_qkv, late_dist, late_bias, keep, send = late[:5]
    grad_qkv, dist_grad, bias_grad, grad_bias_inner, sums_one, sums_two, loss = late[5:]
    sum_late = Scatter(grid, keep, send, by_inner)
    sum_inner.start()
    sum_early.start()

    waiting = (grad_qkv, late_qkv, dist_grad, late_dist, bias_grad, late_bias)
    waiting = after((*waiting, grad_bias_inner, sums_one, sums_two), sum_late)
    grad_qkv, late_qkv, dist_grad, late_dist, bias_grad, late_bias = waiting[:6]
    grad_bias_inner, sums_one, sums_two = waiting[6:]
    fold = keep.shape[1] // width
    sum_late.start()
    dist_grad = jnp.concatenate([dist_grad, late_dist])[:, :2].reshape(heads, 2 * length)
    grad_rel = lax.dot_general(
        dist_grad,
        one_hot.astype(F32),
        (((1,), (0,)), ((), ())),
        precision=lax.Precision.HIGHEST,
    )
    bias_grad = jnp.concatenate([bias_grad, late_bias])[:, 0].reshape(pairs, 3, PAIR)
    small = [
        sums_one[:3],
        sums_two[:4],
        bias_grad.transpose(1, 0, 2).reshape(3, width),
        grad_bias_inner.reshape(-1, width),
        jnp.pad(grad_rel, ((0, 0), (0, width - buckets))),
    ]
    rows = sum(value.shape[0] for value in small)
    small.append(jnp.zeros((-rows % (8 * fold), width), F32))
    small = jnp.concatenate(small)
    rows = small.shape[0] // fold
    rider = jnp.concatenate([small[i * rows : (i + 1) * rows] for i in range(fold)], axis=1)
    rider = rider + grid.move(rider.astype(BF), "core", 1).astype(F32)
    other = grid.move(rider.astype(BF), "inner", 1)
    grad_inputs = grad_one + contract(grad_qkv, first_weight, 1, 1)
    grad_inputs = grad_inputs + contract(late_qkv, second_weight, 1, 1)
    grad_inputs, other = after((grad_inputs, other), sum_early, sum_inner)
    sum_inner.start()
    after((), sum_late)
    sum_late.rider = rider + other.astype(F32)
    sum_late.start()
    after((), sum_late)
    sum_late.start(sum_early)
    after((), sum_inner)
    after((), sum_late)
    own_late = sum_late.result()
    own_early = sum_early.result()
    own_outer = sum_outer.result()
    own_inner = sum_inner.result()
    own = jnp.concatenate([own_early, own_late], axis=1).reshape(block_rows, pairs, 3, PAIR)
    own_query, own_key, own_value = [own[:, :, i].reshape(-1, width) for i in range(3)]

    small = jnp.concatenate(
        [sum_late.rider[:, i * width : (i + 1) * width] for i in range(fold)], axis=0
    )
    index = lax.axis_index("query") * cand_size + own_slot
    small_own = lax.dynamic_slice_in_dim(small, index * block_rows, block_rows, 1)
    at = 10 + hidden // width
    flat = small[10:at].reshape(-1)
    own_bias_inner = lax.dynamic_slice_in_dim(flat, index * (hidden // devices), hidden // devices)
    rel_rows = buckets // devices
    own_rel = lax.dynamic_slice_in_dim(small[at : at + heads], index * rel_rows, rel_rows, 1)
    shape = (micros, 1, 1, length, width)
    return (
        hidden_out.reshape(shape),
        loss[:, :1],
        grad_inputs.reshape(shape),
        own_query,
        own_key,
        own_value,
        own_inner[:, hidden:],
        own_inner[:, :hidden],
        own_outer,
        small_own[7],
        small_own[9],
        small_own[2],
        own_bias_inner,
        small_own[5],
        small_own[0],
        small_own[1],
        small_own[3],
        small_own[4],
        own_rel.T,
        small_own[6],
    )


def solution(mesh):
    both = ("query", "cand")
    slots = P(None, "query", "cand", None, None)
    lists = P(None, "query", None, None)
    rows = P("query", None)
    vec_spec = P("query")
    return jax.shard_map(
        partial(body, (mesh.shape["query"], mesh.shape["cand"])),
        mesh=mesh,
        in_specs=(slots, slots, lists, lists, P()) + (rows,) * 6 + (vec_spec,) * 9 + (rows, vec_spec),
        out_specs=(slots, P(None, "query"), slots)
        + (P(both, None),) * 6
        + (P(both),) * 9
        + (P(both, None), P(both)),
        check_vma=False,
    )
```
